32 devices in a mesh: dom: 32 (over z, y, x, core).
Axes of the slice: x: 2, y: 2, z: 4, core: 2. Of those that a mesh axis runs over, the one named last changes fastest.
Arguments:
- start_state: float32 [504, 8192], P(None, 'dom'), may hold values from -6 to 6
- material: float32 [3, 8192], P(None, 'dom'), may hold values from 0.35 to 1.4
- geometry: float32 [3, 8192], P(None, 'dom'), may hold values from 0.6 to 1.6
- clusters: int32 [8192], P('dom'), may hold values from 0 to 1, as said below
- neighbours: int32 [4, 8192], P(None, 'dom'), may hold values from -1 to 8191, as said below
- orientation: int32 [4, 8192], P(None, 'dom'), may hold values from 0 to 11
- stiffness: float32 [3, 56, 56], replicated, may hold values from -0.75 to 0.75
- face_trace: float32 [4, 21, 56], replicated, may hold values from -0.75 to 0.75
- face_lift: float32 [4, 56, 21], replicated, may hold values from -1.25 to 1.25
- face_turns: float32 [3, 21, 21], replicated, may hold values from -1.25 to 1.25
- cotangent: float32 [504, 8192], P(None, 'dom'), may hold values from -0.27 to 0.27
Outputs:
- final_state: float32 [504, 8192], P(None, 'dom')
- material_grad: float32 [3, 8192], P(None, 'dom')
The draws below stay inside these ranges and needn't reach their ends.
Inputs may be any that keep to these rules, and one draw needn't show every extreme that they name: `clusters`: 1 marks a fine element; a device's block of 256 elements holds at most 128 fine ones, and some block holds exactly 128. `neighbours`: element n sits on device n // 256. A neighbour on another device is 1 to 4 devices away counted around the device cycle, or exactly half the cycle away. For every device and every such distance (up or down), at most 16 of the device's faces name elements there; on every device exactly 16 faces name elements half the cycle away.
All inputs are finite; a program needn't handle non-finite values.
Results may differ from the reference program's by a relative error of at most 0.0001.
Values sent between devices are 32-bit elements; how exact they have to be, the bound alone decides.
A program may use at most 192 MiB of HBM per device.

```python
import math
import jax
import jax.numpy as jnp
from jax import lax

VARS = 9
BASIS = 56
FACE_BASIS = 21
TERMS = 6
REACH = 4
E_DEV = 256
CAP = 16
FINE_DEV = 128
ELEMS = 8192


def block_ranks(key, blocks, length):
    keys = jax.random.split(key, blocks)
    order = jax.vmap(lambda subkey: jax.random.permutation(subkey, length))(keys)
    row_ids = jnp.arange(blocks)[:, None]
    return jnp.zeros((blocks, length), jnp.int32).at[row_ids, order].set(jnp.arange(length, dtype=jnp.int32)[None, :])


def draw_clusters(key, part):
    device_count = ELEMS // E_DEV
    key_start, key_order, key_pick = jax.random.split(jax.random.fold_in(key, 23), 3)
    band_start = jax.random.randint(key_start, (), 0, device_count)
    band_width = max(1, device_count // 8)
    in_band = (jnp.arange(device_count) - band_start) % device_count < band_width
    element_rank = block_ranks(key_order, device_count, E_DEV)
    sparse_pick = jax.random.randint(key_pick, (device_count, E_DEV), 0, 8) == 0
    fine_mask = (element_rank < FINE_DEV) & (in_band[:, None] | sparse_pick)
    return fine_mask.astype(jnp.int32).reshape(ELEMS)


def draw_neighbours(key, part):
    device_count = ELEMS // E_DEV
    face_count = 4 * E_DEV
    near_count = 2 * REACH
    lane_count = near_count + 1
    key_counts, key_full, key_order, key_far, key_edge = jax.random.split(jax.random.fold_in(key, 11), 5)
    counts = jax.random.randint(key_counts, (device_count, lane_count), CAP // 2, CAP + 1)
    full_lane = jax.random.randint(key_full, (device_count,), 0, near_count)
    lane_ids = jnp.arange(lane_count)[None, :]
    counts = jnp.where(lane_ids == full_lane[:, None], CAP, counts)
    counts = jnp.where(lane_ids == near_count, CAP, counts)
    face_rank = block_ranks(key_order, device_count, face_count)
    lane_pick = face_rank // CAP
    lane_slot = face_rank % CAP
    lane_clip = jnp.minimum(lane_pick, lane_count - 1)
    remote = (face_rank < lane_count * CAP) & (lane_slot < jnp.take_along_axis(counts, lane_clip, axis=1))
    offset = jnp.where(lane_clip < REACH, lane_clip + 1, jnp.where(lane_clip < near_count, -(lane_clip - REACH + 1), device_count // 2))
    device_ids = jnp.arange(device_count)[:, None]
    target = (device_ids + offset) % device_count
    far_pick = jax.random.randint(key_far, (device_count, face_count), 0, E_DEV)
    boundary = jax.random.randint(key_edge, (device_count, face_count), 0, 16) == 0
    remote_id = target * E_DEV + far_pick
    local_id = device_ids * E_DEV + far_pick
    neighbour_ids = jnp.where(remote, remote_id, jnp.where(boundary, -1, local_id))
    return neighbour_ids.reshape(device_count, 4, E_DEV).transpose(1, 0, 2).reshape(4, ELEMS).astype(jnp.int32)


def place_ends(values, own_key, smallest, high):
    longest = values.shape.index(max(values.shape))
    spots = []
    for shift in (0, 1):
        where = [jax.random.randint(jax.random.fold_in(own_key, axis), (), 0, length) for axis, length in enumerate(values.shape)]
        where[longest] = (where[longest] + shift) % values.shape[longest]
        spots.append(tuple(where))
    return values.at[spots[0]].set(smallest).at[spots[1]].set(high)


def levels(stream_key, dims, cuts, low, top_value):
    level = 1.0
    for position, shards_of in cuts:
        steps = jax.random.uniform(jax.random.fold_in(jax.random.fold_in(stream_key, 6), position), (shards_of,), jnp.float32, low / len(cuts), top_value / len(cuts))
        level = level * jnp.repeat(jnp.exp(steps), dims[position] // shards_of).reshape((-1,) + (1,) * (len(dims) - 1 - position))
    return level


def scatter_about(rng, shape, width, reach, cuts=(), kind=jnp.bfloat16):
    values = width * jax.random.normal(rng, shape, jnp.float32)
    if cuts:
        values = values * levels(rng, shape, cuts, -0.22, 0.18)
    return jnp.clip(values, -reach, reach).astype(kind)


def setup_inputs(seed: int = 0) -> dict:
    arg_keys = jax.random.split(jax.random.key(seed), 12)
    start_state = scatter_about(arg_keys[0], (VARS * BASIS, ELEMS), 1.0, 6.0, ((1, 32),), jnp.float32)
    material = jnp.clip(jnp.exp(math.log(1.4) - 1.3862944 * jax.random.uniform(arg_keys[1], (3, ELEMS), jnp.float32) ** levels(arg_keys[1], (3, ELEMS), ((1, 32),), -0.2, 0.2)), 0.35, 1.4)
    geometry = jnp.clip(jnp.exp(math.log(1.6) - 0.98082923 * jax.random.uniform(arg_keys[2], (3, ELEMS), jnp.float32) ** levels(arg_keys[2], (3, ELEMS), ((1, 32),), -0.2, 0.2)), 0.6, 1.6)
    clusters = draw_clusters(jax.random.fold_in(arg_keys[11], 71), 0)
    neighbours = draw_neighbours(jax.random.fold_in(arg_keys[11], 71), 0)
    orientation = place_ends(jax.random.randint(arg_keys[5], (4, ELEMS), 0, 12), jax.random.fold_in(arg_keys[5], 1), 0, 11).astype(jnp.int32)
    stiffness = scatter_about(arg_keys[6], (3, BASIS, BASIS), BASIS ** -0.5, 0.75, (), jnp.float32)
    face_trace = scatter_about(arg_keys[7], (4, FACE_BASIS, BASIS), BASIS ** -0.5, 0.75, (), jnp.float32)
    face_lift = scatter_about(arg_keys[8], (4, BASIS, FACE_BASIS), FACE_BASIS ** -0.5, 1.25, (), jnp.float32)
    face_turns = scatter_about(arg_keys[9], (3, FACE_BASIS, FACE_BASIS), FACE_BASIS ** -0.5, 1.25, (), jnp.float32)
    cotangent = scatter_about(arg_keys[10], (VARS * BASIS, ELEMS), 0.045, 0.27, ((1, 32),), jnp.float32)
    return {"start_state": start_state, "material": material, "geometry": geometry, "clusters": clusters, "neighbours": neighbours, "orientation": orientation, "stiffness": stiffness, "face_trace": face_trace, "face_lift": face_lift, "face_turns": face_turns, "cotangent": cotangent}


highest = lax.Precision.HIGHEST
dt_step = 0.5
root_third = 0.5773502691896258
face_normals = ((0.0, 0.0, -1.0), (0.0, -1.0, 0.0), (-1.0, 0.0, 0.0), (root_third, root_third, root_third))

def taylor_weights(start_time, length):
    weights = []
    factorial = 1.0
    for degree in range(TERMS):
        factorial = factorial * (degree + 1)
        weights.append(((start_time + length) ** (degree + 1) - start_time ** (degree + 1)) / factorial)
    return weights

def star_apply(along_x, along_y, along_z, lame_value, shear_value, inverse_density):
    longitudinal = lame_value + 2.0 * shear_value
    outputs = [-(longitudinal * along_x[6] + lame_value * along_y[7] + lame_value * along_z[8]), -(lame_value * along_x[6] + longitudinal * along_y[7] + lame_value * along_z[8]), -(lame_value * along_x[6] + lame_value * along_y[7] + longitudinal * along_z[8]), -shear_value * (along_x[7] + along_y[6]), -shear_value * (along_y[8] + along_z[7]), -shear_value * (along_x[8] + along_z[6]), -inverse_density * (along_x[0] + along_y[3] + along_z[5]), -inverse_density * (along_x[3] + along_y[1] + along_z[4]), -inverse_density * (along_x[5] + along_y[4] + along_z[2])]
    return jnp.stack(outputs)

def basis_apply(matrix, values):
    return jnp.einsum('bc,vce->vbe', matrix, values, precision=highest)

def basis_transposed(matrix, values):
    return jnp.einsum('cb,vce->vbe', matrix, values, precision=highest)

def time_derivative(values, mat_values, geometry, stiffness):
    pieces = [geometry[axis_no] * basis_apply(stiffness[axis_no], values) for axis_no in range(3)]
    return -star_apply(pieces[0], pieces[1], pieces[2], mat_values[0], mat_values[1], mat_values[2])

def predict(values, mat_values, geometry, stiffness, weight_sets):
    totals = [weights[0] * values for weights in weight_sets]
    current = values
    for degree in range(1, TERMS):
        current = time_derivative(current, mat_values, geometry, stiffness)
        totals = [partial_sum + weights[degree] * current for partial_sum, weights in zip(totals, weight_sets)]
    return totals

def face_traces(window, face_trace):
    traced = jnp.einsum('gjb,vbe->vjge', face_trace, window, precision=highest)
    return traced.reshape(traced.shape[0], traced.shape[1], -1)

def orient_apply(raw_faces, far_turns, face_turns):
    result = jnp.zeros_like(raw_faces)
    for turn_no in range(3):
        turned = jnp.einsum('ji,vie->vje', face_turns[turn_no], raw_faces, precision=highest)
        result = result + jnp.where(far_turns == turn_no, turned, 0.0)
    return result

def update(window, inner, outer, mat_values, geometry, stiffness, face_lift):
    elements = window.shape[2]
    pieces = [geometry[axis_no] * basis_transposed(stiffness[axis_no], window) for axis_no in range(3)]
    change = star_apply(pieces[0], pieces[1], pieces[2], mat_values[0], mat_values[1], mat_values[2])
    wave_speed = jnp.sqrt((mat_values[0] + 2.0 * mat_values[1]) * mat_values[2])
    for face_no in range(4):
        own_side = inner[:, :, face_no * elements:(face_no + 1) * elements]
        far_side = outer[:, :, face_no * elements:(face_no + 1) * elements]
        average = 0.5 * (own_side + far_side)
        normal = face_normals[face_no]
        face_flux = star_apply(normal[0] * geometry[0] * average, normal[1] * geometry[1] * average, normal[2] * geometry[2] * average, mat_values[0], mat_values[1], mat_values[2])
        face_flux = face_flux + 0.5 * wave_speed * (own_side - far_side)
        change = change - jnp.einsum('bj,vje->vbe', face_lift[face_no], face_flux, precision=highest)
    return change

def outer_traces(inner, neighbours, orientation, face_turns, elements):
    flat_neighbour = neighbours.reshape(-1)
    face_codes = orientation.reshape(-1)
    index = face_codes // 3 * elements + jnp.maximum(flat_neighbour, 0)
    raw_faces = jnp.take(inner, index, axis=2)
    raw_faces = jnp.where(flat_neighbour >= 0, raw_faces, 0.0)
    return orient_apply(raw_faces, face_codes % 3, face_turns)

def reference(start_state, material, geometry, clusters, neighbours, orientation, stiffness, face_trace, face_lift, face_turns, cotangent):
    elements = start_state.shape[1]
    values = start_state.reshape(VARS, BASIS, elements)
    fine_mask = clusters == 1
    weights_first = taylor_weights(0.0, 0.5 * dt_step)
    weights_later = taylor_weights(0.5 * dt_step, 0.5 * dt_step)

    def forward(mat_values):
        window_first, window_coarse = predict(values, mat_values, geometry, stiffness, [weights_first, weights_later])
        inner_first = face_traces(window_first, face_trace)
        outer_first = outer_traces(inner_first, neighbours, orientation, face_turns, elements)
        change_first = update(window_first, inner_first, outer_first, mat_values, geometry, stiffness, face_lift)
        middle = values + change_first
        window_fine = predict(middle, mat_values, geometry, stiffness, [weights_first])[0]
        window_second = jnp.where(fine_mask, window_fine, window_coarse)
        inner_second = face_traces(window_second, face_trace)
        outer_second = outer_traces(inner_second, neighbours, orientation, face_turns, elements)
        change_second = update(window_second, inner_second, outer_second, mat_values, geometry, stiffness, face_lift)
        return values + change_first + change_second
    final_values, pullback = jax.vjp(forward, material)
    material_grad = pullback(cotangent.reshape(VARS, BASIS, elements))[0]
    return (final_values.reshape(VARS * BASIS, elements), material_grad)
```

```python
import functools

import jax
import jax.numpy as jnp
from jax import lax
from jax.experimental import pallas as pl
from jax.experimental.pallas import tpu as pltpu
from jax.sharding import PartitionSpec as P

VARS = 9
TERMS = 6
REACH = 4
CAP = 16
FINE_DEV = 128
LANES = 2 * REACH + 1
SLOTS = LANES * CAP
STEPS = TERMS - 1
f32, bf16, i32 = jnp.float32, jnp.bfloat16, jnp.int32

dt_step = 0.5
root_third = 0.5773502691896258
H = 0.5 * dt_step

A0 = H
STEP_SCALE = [H * H / 2.0] + [H / (k + 2.0) for k in range(1, STEPS)]
C_OVER_A = [2.0 ** (k + 1) - 1.0 for k in range(TERMS)]

NEED = [(0, 1), (1, 1), (2, 1), (0, 2), (1, 2), (2, 2), (0, 3), (0, 3), (0, 3)]
PAIRS = [((6, 7), 0, 3), ((8, 3), 0, 3), ((0, 1), 0, 2), ((4, 2), 1, 2), ((5,), 2, 2)]
READS = [
    {3: 7, 5: 8, 6: 0, 7: 3, 8: 5},
    {3: 6, 4: 8, 6: 3, 7: 1, 8: 4},
    {4: 7, 5: 6, 6: 5, 7: 4, 8: 2},
]


def up_to(n, m):
    return -(-n // m) * m


def halves(x):
    high = x.astype(bf16)
    return high, (x - high.astype(f32)).astype(bf16)


def padded(x, rows):
    if x.shape[0] == rows:
        return x
    return jnp.concatenate([x, jnp.zeros((rows - x.shape[0], x.shape[1]), f32)], axis=0)


def right3(x, rows):
    high, low = halves(padded(x, rows))
    return jnp.concatenate([high, high, low], axis=0)


def left3(a):
    high = a.astype(bf16).astype(f32)
    return jnp.concatenate([high, a - high, high], axis=1).astype(bf16)


def stack2(x, rows):
    return jnp.concatenate(halves(padded(x, rows)), axis=0)


def mm(a, b):
    return jnp.dot(a, b, preferred_element_type=f32)


def mm_t(a, b):
    return lax.dot_general(a, b, (((1,), (1,)), ((), ())), preferred_element_type=f32)


def add(*terms):
    total = None
    for t in terms:
        if t is not None:
            total = t if total is None else total + t
    return total


def blocks(ref, size, base=0):
    return [ref[base + v * size : base + (v + 1) * size, :] for v in range(VARS)]


def put(ref, values, base=0):
    size = values[0].shape[0]
    for v in range(VARS):
        ref[base + v * size : base + (v + 1) * size, :] = values[v]


def row(ref, n):
    return ref[n : n + 1, :]


class Mat:
    def __init__(self, con, base, geo):
        self.lam, self.mu2 = row(con, base), row(con, base + 1)
        self.mg = [row(con, base + 2 + a) for a in range(3)]
        self.rg = [row(con, base + 5 + a) for a in range(3)]
        self.g = [row(geo, a) for a in range(3)]


def forward_mix(p, m):
    t = [m.g[a] * p(6 + a, a) for a in range(3)]
    spread = m.lam * (t[0] + t[1] + t[2])
    return [
        spread + m.mu2 * t[0],
        spread + m.mu2 * t[1],
        spread + m.mu2 * t[2],
        m.mg[0] * p(7, 0) + m.mg[1] * p(6, 1),
        m.mg[1] * p(8, 1) + m.mg[2] * p(7, 2),
        m.mg[0] * p(8, 0) + m.mg[2] * p(6, 2),
        m.rg[0] * p(0, 0) + m.rg[1] * p(3, 1) + m.rg[2] * p(5, 2),
        m.rg[0] * p(3, 0) + m.rg[1] * p(1, 1) + m.rg[2] * p(4, 2),
        m.rg[0] * p(5, 0) + m.rg[1] * p(4, 1) + m.rg[2] * p(2, 2),
    ]


def normal_mix(r, m):
    u = m.lam * (r[0] + r[1] + r[2])
    return [u + m.mu2 * r[a] for a in range(3)] + list(r[3:])


def backward_mix(p, m):
    return [
        m.rg[0] * p(6, 0),
        m.rg[1] * p(7, 1),
        m.rg[2] * p(8, 2),
        m.rg[0] * p(7, 0) + m.rg[1] * p(6, 1),
        m.rg[1] * p(8, 1) + m.rg[2] * p(7, 2),
        m.rg[0] * p(8, 0) + m.rg[2] * p(6, 2),
        m.g[0] * p(0, 0) + m.mg[1] * p(3, 1) + m.mg[2] * p(5, 2),
        m.g[1] * p(1, 1) + m.mg[0] * p(3, 0) + m.mg[2] * p(4, 2),
        m.g[2] * p(2, 2) + m.mg[1] * p(4, 1) + m.mg[0] * p(5, 0),
    ]


def products(mat, values):
    size, width = values[0].shape
    pitch = mat.shape[0] // 4
    out = {}
    if width == FINE_DEV:
        groups = PAIRS
    else:
        groups = [((v,), s, c) for v, (s, c) in enumerate(NEED)]
    for names, start, count in groups:
        x = [values[v] for v in names]
        x = x[0] if len(x) == 1 else jnp.concatenate(x, axis=1)
        y = mm(mat[start * pitch : (start + count) * pitch, :], right3(x, pitch))
        for n, v in enumerate(names):
            for i in range(count):
                out[v, (start + i) % 3] = y[
                    i * pitch : i * pitch + size, n * width : (n + 1) * width
                ]
    return lambda v, axis: out[v, axis]


def apply_step(mat, values, m):
    return forward_mix(products(mat, values), m)


def apply_back(mat, values, m):
    return backward_mix(products(mat, normal_mix(values, m)), m)


def fold8(x):
    total = x[0:8]
    for n in range(8, x.shape[0], 8):
        total = total + x[n : n + 8]
    return total


def group_sums(r, x):
    mixed = (r[0] + r[1] + r[2]) * (x[0] + x[1] + x[2])
    groups = [add(*[r[v] * x[v] for v in range(g, g + 3)]) for g in (0, 3, 6)]
    return [fold8(g) for g in [mixed] + groups]


def plus(total, more):
    return more if total is None else [a + b for a, b in zip(total, more)]


def narrow(x, hot_c, rows):
    y = mm_t(stack2(x, rows), hot_c)
    return y[: x.shape[0]] + y[rows : rows + x.shape[0]]


def widen(x, hot_c2, rows):
    high, low = halves(padded(x, rows))
    return mm(jnp.concatenate([high, low], axis=1), hot_c2)[: x.shape[0]]


def trace_faces(tr, window, own, own_hl, fb, elems):
    size = window.shape[0] // VARS
    rows = own_hl.shape[0] // 2
    for v in range(VARS):
        t = mm(tr[...], right3(window[v * size : (v + 1) * size, :], tr.shape[1] // 3))
        for g in range(4):
            own[v * fb : (v + 1) * fb, g * elems : (g + 1) * elems] = t[g * fb : (g + 1) * fb]
    for g in range(4):
        cols = slice(g * elems, (g + 1) * elems)
        high, low = halves(padded(own[:, cols], rows))
        own_hl[:rows, cols] = high
        own_hl[rows:, cols] = low


def turn_blocks(mat, x, which):
    fb = x[0].shape[0]
    first, second = which == 0, which == 1
    out = []
    for n in range(0, len(x), 2):
        pair = x[n] if n + 1 == len(x) else jnp.concatenate(x[n : n + 2], axis=0)
        y = mm(mat[...], right3(pair, 2 * fb))
        for i in range(min(2, len(x) - n)):
            part = [y[o * 2 * fb + i * fb : o * 2 * fb + (i + 1) * fb] for o in range(3)]
            out.append(jnp.where(first, part[0], jnp.where(second, part[1], part[2])))
    return out


def split_rows(x, fb):
    return [x[v * fb : (v + 1) * fb] for v in range(VARS)]


def local_outer(own_hl, hot, turn, tn, out, fb, elems):
    rows = own_hl.shape[0] // 2
    for f in range(4):
        cols = slice(f * elems, (f + 1) * elems)
        y = mm(own_hl[...], hot[:, cols])
        raw = y[: VARS * fb] + y[rows : rows + VARS * fb]
        turned = turn_blocks(tn, split_rows(raw, fb), turn[f : f + 1, :])
        out[:, cols] = jnp.concatenate(turned, axis=0)


def serve(hot_in, own_hl, tx):
    rows = own_hl.shape[0] // 2
    tx[:, :rows] = mm_t(hot_in[...], own_hl[:rows, :]) + mm_t(hot_in[...], own_hl[rows:, :])
    tx[:, rows:] = jnp.zeros((tx.shape[0], tx.shape[1] - rows), f32)


def flipped(rx):
    x = rx[...]
    return padded(x, up_to(x.shape[0], 128)).T[:, : x.shape[0]]


def face_rows(f, x, fc):
    if f == 3:
        return forward_mix(lambda v, axis: x[v], fc)
    axis = 2 - f
    kl, kp, _, km, kr = fc
    t = x[6 + axis]
    rows = [kl * t] * 3 + [None] * 6
    rows[axis] = kp * t
    for v, source in READS[axis].items():
        rows[v] = (km if v < 6 else kr) * x[source]
    return rows


def face_rows_back(f, r, fc):
    if f == 3:
        s = normal_mix(r, fc)
        return backward_mix(lambda v, axis: s[v], fc)
    axis = 2 - f
    kl, _, k2, km, kr = fc
    out = [None] * VARS
    out[6 + axis] = kl * (r[0] + r[1] + r[2]) + k2 * r[axis]
    for v, source in READS[axis].items():
        out[source] = (km if v < 6 else kr) * r[v]
    return out


def face_consts(f, fcon, con):
    if f == 3:
        m = Mat.__new__(Mat)
        m.lam, m.mu2 = row(fcon, 15), row(fcon, 16)
        m.mg = [row(fcon, 17 + a) for a in range(3)]
        m.rg = [row(fcon, 20 + a) for a in range(3)]
        m.g = [row(fcon, 23 + a) for a in range(3)]
        return m
    return [row(fcon, 5 * f + n) for n in range(5)]


def far_side(rx, slot_turn, tn, hot_slot, out_loc, fb):
    rows = up_to(VARS * fb, 16)
    turned = turn_blocks(tn, split_rows(flipped(rx), fb), slot_turn[0:1, :])
    high_low = stack2(jnp.concatenate(turned, axis=0), rows)

    def far(f, elems):
        cols = slice(f * elems, (f + 1) * elems)
        y = mm(high_low, hot_slot[:, cols])
        return out_loc[:, cols] + (y[: VARS * fb] + y[rows : rows + VARS * fb])

    return far


def surface(lf, own, far, fcon, con, fb, elems, jump_ref, flux_ref):
    half_speed = row(fcon, 26)
    fluxes = [[] for _ in range(VARS)]
    for f in range(4):
        cols = slice(f * elems, (f + 1) * elems)
        a, b = split_rows(own[:, cols], fb), split_rows(far(f, elems), fb)
        rows = face_rows(f, [x + y for x, y in zip(a, b)], face_consts(f, fcon, con))
        for v in range(VARS):
            jump = a[v] - b[v]
            flux = add(half_speed * jump, rows[v])
            jump_ref[v * fb : (v + 1) * fb, cols] = jump
            flux_ref[v * fb : (v + 1) * fb, cols] = flux
            fluxes[v].append(flux)
    return [mm(lf[...], right3(jnp.concatenate(x, axis=0), 4 * fb)) for x in fluxes]


def face_sums(lifted, jump_ref, flux_ref, half_speed, fb, elems):
    total, speed = None, None
    for f in range(4):
        cols = slice(f * elems, (f + 1) * elems)
        r, d, x = [split_rows(ref[:, cols], fb) for ref in (lifted, jump_ref, flux_ref)]
        of_jump, of_flux = group_sums(r, d), group_sums(r, x)
        total = plus(total, [a - half_speed * b for a, b in zip(of_flux, of_jump)])
        more = of_jump[1] + of_jump[2] + of_jump[3]
        speed = more if speed is None else speed + more
    return total, speed


def faces_cot(seed, lt, tnt, turn, extra, fcon, con, lifted, own_cot, x_hl, fb, elems):
    half_speed = row(fcon, 26)
    rows = x_hl.shape[0] // 2
    for v in range(VARS):
        y = mm(lt[...], right3(seed[v], lt.shape[1] // 3))
        for f in range(4):
            lifted[v * fb : (v + 1) * fb, f * elems : (f + 1) * elems] = y[f * fb : (f + 1) * fb]
    for f in range(4):
        cols = slice(f * elems, (f + 1) * elems)
        r = split_rows(lifted[:, cols], fb)
        back = face_rows_back(f, r, face_consts(f, fcon, con))
        x = []
        for v in range(VARS):
            side = half_speed * r[v]
            own_cot[v * fb : (v + 1) * fb, cols] = add(side, back[v])
            x.append(-side if back[v] is None else back[v] - side)
        turned = turn_blocks(tnt, x, turn[f : f + 1, :])
        if extra is not None:
            turned.append(extra[:, cols])
        high, low = halves(padded(jnp.concatenate(turned, axis=0), rows))
        x_hl[:rows, cols] = high
        x_hl[rows:, cols] = low


def send_cot(hot_slot, x_hl, tx):
    serve(hot_slot, x_hl, tx)


def faces_back(own_cot, x_hl, hot, rx, hot_in, trt, fb, elems):
    rows = x_hl.shape[0] // 2
    arrived = stack2(flipped(rx)[:rows], rows)
    for g in range(4):
        cols = slice(g * elems, (g + 1) * elems)
        y = mm_t(x_hl[...], hot[cols, :]) + mm(arrived, hot_in[:, cols])
        own_cot[:, cols] = own_cot[:, cols] + (y[: VARS * fb] + y[rows : rows + VARS * fb])
    out = []
    for v in range(VARS):
        x = [own_cot[v * fb : (v + 1) * fb, g * elems : (g + 1) * elems] for g in range(4)]
        out.append(mm(trt[...], right3(jnp.concatenate(x, axis=0), 4 * fb)))
    return out


def peers_of(devices):
    me = lax.axis_index("dom")
    shifts = [n + 1 for n in range(REACH)] + [-(n + 1) for n in range(REACH)] + [devices // 2]
    return [
        [lax.rem(me + sign * s + 2 * devices, devices) for s in shifts] for sign in (1, -1)
    ]


def send_all(peers, src, dst, send_sems, recv_sems, base=0):
    copies = []
    for n in reversed(range(LANES)):
        rows = pl.ds(n * CAP, CAP)
        copy = pltpu.make_async_remote_copy(
            src_ref=src.at[rows],
            dst_ref=dst.at[rows],
            send_sem=send_sems.at[base + n],
            recv_sem=recv_sems.at[base + n],
            device_id=(peers[n],),
            device_id_type=pl.DeviceIdType.MESH,
        )
        copy.start()
        copies.append(copy)
    return copies


def one_hot(mask):
    return jnp.where(mask, 1.0, 0.0).astype(bf16)


def face_places(
    devices, neighbours, orientation, fine, hot, hot_slot, hot_c, turn, slot_turn, extra
):
    elems = neighbours.shape[1]
    me = lax.axis_index("dom")
    at = lax.broadcasted_iota(i32, (16, elems), 0)
    square = (elems, elems)
    at_n, at_e = lax.broadcasted_iota(i32, square, 0), lax.broadcasted_iota(i32, square, 1)
    at_s = lax.broadcasted_iota(i32, (SLOTS, elems), 0)
    at_8 = lax.broadcasted_iota(i32, (8, elems), 0)
    earlier = one_hot(at_n <= at_e)
    lanes, marks = [], []
    for f in range(4):
        cols = slice(f * elems, (f + 1) * elems)
        name, code = neighbours[f : f + 1, :], orientation[f : f + 1, :]
        far_face = sum(jnp.where(code >= 3 * g, 1, 0) for g in (1, 2, 3))
        turn[f : f + 1, :] = code - 3 * far_face
        present = name >= 0
        safe = jnp.maximum(name, 0)
        owner = jnp.floor((safe.astype(f32) + 0.5) * (1.0 / elems)).astype(i32)
        index = safe - owner * elems
        away = owner - me
        away = jnp.where(away < 0, away + devices, away)
        local = present & (away == 0)
        for g in range(4):
            key = jnp.where(local & (far_face == g), index, -1)
            hot[g * elems : (g + 1) * elems, cols] = one_hot(at_n == key)
        lane = jnp.where(
            away <= REACH,
            away - 1,
            jnp.where(away >= devices - REACH, REACH + devices - away - 1, 2 * REACH),
        )
        lane = jnp.where(present & (away != 0), lane, LANES)
        lanes.append(lane)
        marks.append(jnp.where(at == lane, 1.0, 0.0))
        index_f, face_f = index.astype(f32), far_face.astype(f32)
        extra[:, cols] = jnp.where(
            at_8 == 0, index_f, jnp.where(at_8 == 1, face_f, jnp.where(at_8 == 2, 1.0, 0.0))
        )
    is_fine = fine[...] == 1
    marks.append(jnp.where((at == 0) & is_fine, 1.0, 0.0))
    run = mm(jnp.concatenate(marks, axis=0).astype(bf16), earlier)
    carry = jnp.zeros((16, 1), f32)
    for f in range(4):
        cols = slice(f * elems, (f + 1) * elems)
        mine = run[16 * f : 16 * f + 16]
        rank = jnp.sum((mine + carry - 1.0) * marks[f], axis=0, keepdims=True).astype(i32)
        carry = carry + mine[:, elems - 1 :]
        slot = jnp.where(lanes[f] < LANES, lanes[f] * CAP + rank, -1)
        hot_slot[:, cols] = one_hot(at_s == slot)
    rank = jnp.where(is_fine, run[64:65].astype(i32) - 1, -1)
    picked = one_hot(lax.broadcasted_iota(i32, (FINE_DEV, elems), 0) == rank)
    hot_c[:FINE_DEV, :] = picked
    hot_c[FINE_DEV:, :] = picked
    turns = jnp.concatenate([turn[f : f + 1, :].astype(f32) for f in range(4)], axis=1)
    turns = jnp.broadcast_to(turns, (16, 4 * elems)).astype(bf16)
    slot_turn[...] = mm_t(turns, hot_slot[...])


def constants(mat_ref, geo_ref, con, fcon):
    lam, mu, rinv = [row(mat_ref, n) for n in range(3)]
    geo = [row(geo_ref, n) for n in range(3)]
    rows = [lam, 2.0 * mu] + [mu * g for g in geo] + [rinv * g for g in geo]
    base = jnp.concatenate(rows, axis=0)
    for n, scale in enumerate([-1.0] + STEP_SCALE):
        con[8 * n : 8 * n + 8, :] = scale * base
    rows = []
    for f in range(3):
        h = 0.5 * geo[2 - f]
        rows += [lam * h, (lam + 2.0 * mu) * h, 2.0 * mu * h, mu * h, rinv * h]
    h = [(-0.5 * root_third) * g for g in geo]
    rows += [lam, 2.0 * mu] + [mu * x for x in h] + [rinv * x for x in h] + h
    rows += [0.5 * jnp.sqrt((lam + 2.0 * mu) * rinv)]
    for n, x in enumerate(rows):
        fcon[n : n + 1, :] = x


def pitched(pad, matrices):
    pad[...] = jnp.zeros(pad.shape, f32)
    for n, x in enumerate(matrices):
        pad[n, : x.shape[0], : x.shape[1]] = x
    return [pad[n] for n in range(len(matrices))]


def turn_matrix(pad, matrices):
    zero = jnp.zeros(pad.shape[1:], f32)
    out = []
    for x in pitched(pad, matrices):
        out += [jnp.concatenate([x, zero], axis=1), jnp.concatenate([zero, x], axis=1)]
    return left3(jnp.concatenate(out, axis=0))


def step_kernel(
    devices,
    state, cot, mat_ref, geo_ref, fine, neighbours, orientation, stiffness, face_trace,
    face_lift, face_turns,
    final, grad,
    w1, wc, w2, coarse, seed1, middle, vol1, vol2, cur,
    q1, q2, hist,
    own, lifted1, lifted2, out_loc, own_cot1, own_cot2, jump, flux,
    tx0, tx1, tx2, tx3, rx0, rx1, rx2, rx3,
    con, fcon, con_f, geo_f, extra, slot_turn,
    k_pad, t_pad, l_pad, n_pad,
    ks, kt, tr, lt, trt, lf, tn, tnt, hot, hot_slot, hot_in, hot_c, own_hl, x_hl1, x_hl2,
    turn, send_sems, recv_sems,
):
    up, down = peers_of(devices)
    barrier = pltpu.get_barrier_semaphore()
    for peer in up:
        pl.semaphore_signal(
            barrier, inc=1, device_id=(peer,), device_id_type=pl.DeviceIdType.MESH
        )
    elems = state.shape[1]
    count = state.shape[0]
    size = count // VARS
    fb = t_pad.shape[1]
    wide = up_to(count, 16)

    constants(mat_ref, geo_ref, con, fcon)
    stiff = pitched(k_pad, [stiffness[d] for d in range(3)])
    ks[...] = left3(jnp.concatenate(stiff + stiff[:1], axis=0))
    stiff = [x.T for x in stiff]
    kt[...] = left3(jnp.concatenate(stiff + stiff[:1], axis=0))
    trace = jnp.concatenate(pitched(t_pad, [face_trace[:, g, :] for g in range(4)]), axis=0)
    tr[...] = left3(trace)
    trt[...] = left3(trace.T)[:size]
    lift = jnp.concatenate(pitched(l_pad, [-face_lift[:, f, :] for f in range(4)]), axis=0)
    lt[...] = left3(lift)
    lf[...] = left3(lift.T)[:size]
    turns = [face_turns[o] for o in range(3)]
    tn[...] = turn_matrix(n_pad, turns)
    tnt[...] = turn_matrix(n_pad, [x.T for x in turns])
    face_places(
        devices, neighbours, orientation, fine, hot, hot_slot, hot_c, turn, slot_turn, extra
    )
    base, half_speed = Mat(con, 0, geo_ref), row(fcon, 26)

    seed2 = blocks(cot, size)
    faces_cot(seed2, lt, tnt, turn, extra, fcon, con, lifted2, own_cot2, x_hl2, fb, elems)
    serve(hot_slot, x_hl2, tx0)
    pl.semaphore_wait(barrier, LANES)
    sent0 = send_all(up, tx0, rx0, send_sems, recv_sems, 0)

    is_fine = fine[...] == 1
    narrow_con = mm_t(
        jnp.concatenate(
            halves(con[0:16, :]) + halves(padded(geo_ref[...], 16)), axis=0
        ),
        hot_c[:FINE_DEV, :],
    )
    geo_f[...] = narrow_con[32:40] + narrow_con[48:56]
    for n, scale in enumerate(STEP_SCALE):
        con_f[8 * n : 8 * n + 8, :] = -scale * (narrow_con[0:8] + narrow_con[16:24])

    for k in range(STEPS):
        old = blocks(state, size) if k == 0 else blocks(q1, size, (k - 1) * count)
        put(q1, apply_step(ks, old, Mat(con, 8 * (k + 1), geo_ref)), k * count)
    for v in range(VARS):
        rows = slice(v * size, (v + 1) * size)
        terms = [A0 * state[rows, :]]
        terms += [q1[k * count + v * size : k * count + (v + 1) * size, :] for k in range(STEPS)]
        w1[rows, :] = add(*terms)
        later = add(*[c * t if c != 1.0 else t for c, t in zip(C_OVER_A, terms)])
        wc[rows, :] = jnp.where(is_fine, 0.0, later)
    trace_faces(tr, w1, own, own_hl, fb, elems)
    local_outer(own_hl, hot, turn, tn, out_loc, fb, elems)
    put(vol1, apply_step(kt, blocks(w1, size), base))
    for copy in sent0:
        copy.wait()

    key = rx0[:, VARS * fb : VARS * fb + 3]
    key = jnp.where(key[:, 2:3] > 0.5, key[:, 1:2] * float(elems) + key[:, 0:1], -1.0)
    at = lax.broadcasted_iota(i32, (SLOTS, 4 * elems), 1)
    hot_in[...] = one_hot(at == key.astype(i32))
    serve(hot_in, own_hl, tx1)
    sent1 = send_all(down, tx1, rx1, send_sems, recv_sems, LANES)

    back = faces_back(own_cot2, x_hl2, hot, rx0, hot_in, trt, fb, elems)
    direct = apply_back(ks, seed2, base)
    back = [a + b for a, b in zip(back, direct)]
    put(coarse, [jnp.where(is_fine, 0.0, x) for x in back])
    part = narrow(jnp.concatenate(back, axis=0), hot_c[:FINE_DEV, :], wide)
    part = split_rows(part, size)
    put(hist, part, (STEPS - 1) * count)
    for k in range(STEPS - 1, 0, -1):
        r = apply_back(kt, blocks(hist, size, k * count), Mat(con_f, 8 * k, geo_f))
        put(hist, [a + b for a, b in zip(r, blocks(hist, size, (STEPS - 1) * count))], (k - 1) * count)
    r = apply_back(kt, blocks(hist, size, 0), Mat(con_f, 0, geo_f))
    r = [a + A0 * b for a, b in zip(r, blocks(hist, size, (STEPS - 1) * count))]
    r = widen(jnp.concatenate(r, axis=0), hot_c[...], wide)
    seed1[...] = r + cot[...]
    faces_cot(
        blocks(seed1, size), lt, tnt, turn, None, fcon, con, lifted1, own_cot1, x_hl1, fb, elems
    )
    serve(hot_slot, x_hl1, tx3)
    sent3 = send_all(up, tx3, rx3, send_sems, recv_sems, 2 * LANES)
    for copy in sent1:
        copy.wait()

    far = far_side(rx1, slot_turn, tn, hot_slot, out_loc, fb)
    change = surface(lf, own, far, fcon, con, fb, elems, jump, flux)
    put(middle, [
        s + m + c for s, m, c in zip(blocks(state, size), blocks(vol1, size), change)
    ])
    start = split_rows(narrow(middle[...], hot_c[:FINE_DEV, :], wide), size)
    for k in range(STEPS):
        old = start if k == 0 else blocks(q2, size, (k - 1) * count)
        put(q2, apply_step(ks, old, Mat(con_f, 8 * k, geo_f)), k * count)
    window = [
        add(A0 * start[v], *[
            q2[k * count + v * size : k * count + (v + 1) * size, :] for k in range(STEPS)
        ])
        for v in range(VARS)
    ]
    w2[...] = widen(jnp.concatenate(window, axis=0), hot_c[...], wide) + wc[...]
    sums, speed = face_sums(lifted1, jump, flux, half_speed, fb, elems)
    trace_faces(tr, w2, own, own_hl, fb, elems)
    serve(hot_in, own_hl, tx2)
    sent2 = send_all(down, tx2, rx2, send_sems, recv_sems, 3 * LANES)

    local_outer(own_hl, hot, turn, tn, out_loc, fb, elems)
    put(vol2, apply_step(kt, blocks(w2, size), base))
    sums = plus(sums, group_sums(blocks(seed1, size), blocks(vol1, size)))
    sums = plus(sums, group_sums(seed2, blocks(vol2, size)))
    fine_sums = None
    for k in range(STEPS):
        fine_sums = plus(
            fine_sums, group_sums(blocks(hist, size, k * count), blocks(q2, size, k * count))
        )
    fine_sums = [jnp.sum(x, axis=0, keepdims=True) for x in fine_sums]
    fine_sums = widen(jnp.concatenate(fine_sums + fine_sums, axis=0), hot_c[...], 16)
    direct = apply_back(ks, blocks(seed1, size), base)
    for copy in sent3:
        copy.wait()
    back = faces_back(own_cot1, x_hl1, hot, rx3, hot_in, trt, fb, elems)
    put(seed1, [a + b for a, b in zip(back, direct)])
    for k in range(STEPS, 0, -1):
        r = [a + C_OVER_A[k] * b for a, b in zip(blocks(seed1, size), blocks(coarse, size))]
        if k < STEPS:
            old = blocks(cur, size)
            r = [a + b for a, b in zip(r, apply_back(kt, old, Mat(con, 8 * (k + 1), geo_ref)))]
        put(cur, r)
        sums = plus(sums, group_sums(blocks(cur, size), blocks(q1, size, (k - 1) * count)))
    for copy in sent2:
        copy.wait()

    far = far_side(rx2, slot_turn, tn, hot_slot, out_loc, fb)
    change = surface(lf, own, far, fcon, con, fb, elems, jump, flux)
    put(final, [
        s + m + c for s, m, c in zip(blocks(middle, size), blocks(vol2, size), change)
    ])
    more, more_speed = face_sums(lifted2, jump, flux, half_speed, fb, elems)
    sums = [jnp.sum(a + b, axis=0, keepdims=True) for a, b in zip(sums, more)]
    sums = [a + fine_sums[n : n + 1] for n, a in enumerate(sums)]
    g_speed = 0.5 * jnp.sum(speed + more_speed, axis=0, keepdims=True)
    lam, mu, rinv = [row(mat_ref, n) for n in range(3)]
    wave = jnp.sqrt((lam + 2.0 * mu) * rinv)
    g_lam = sums[0] / (3.0 * lam + 2.0 * mu)
    g_mu = (sums[1] - lam * g_lam + sums[2]) / mu
    g_speed = g_speed / wave
    grad[...] = jnp.concatenate(
        [
            g_lam + 0.5 * g_speed * rinv,
            g_mu + g_speed * rinv,
            sums[3] / rinv + 0.5 * g_speed * (lam + 2.0 * mu),
        ],
        axis=0,
    )


def body(
    start_state, material, geometry, clusters, neighbours, orientation,
    stiffness, face_trace, face_lift, face_turns, cotangent,
):
    rows, elems = start_state.shape
    basis = rows // VARS
    devices = lax.axis_size("dom")
    fb = up_to(face_trace.shape[1], 8)
    pitch = up_to(basis, 16)
    frows = up_to(VARS * fb + 8, 16)
    full, faces, slots = (rows, elems), (VARS * fb, 4 * elems), (SLOTS, up_to(frows, 128))
    args = (
        start_state, cotangent, material, geometry, clusters.reshape(1, elems), neighbours,
        orientation, stiffness, face_trace.transpose(1, 0, 2), face_lift.transpose(2, 0, 1),
        face_turns,
    )
    scratch = [full] * 9
    scratch += [(STEPS * rows, elems)] + [(STEPS * rows, FINE_DEV)] * 2
    scratch += [faces] * 8 + [slots] * 8
    scratch += [(8 * TERMS, elems), (32, elems), (8 * STEPS, FINE_DEV), (8, FINE_DEV)]
    scratch += [(8, 4 * elems), (16, SLOTS)]
    scratch += [(3, pitch, pitch), (4, fb, pitch), (4, fb, pitch), (3, fb, fb)]
    packed = [(4 * pitch, 3 * pitch)] * 2 + [(4 * fb, 3 * pitch)] * 2
    packed += [(basis, 12 * fb)] * 2 + [(6 * fb, 6 * fb)] * 2
    packed += [(4 * elems, 4 * elems)] + [(SLOTS, 4 * elems)] * 2 + [(2 * FINE_DEV, elems)]
    packed += [(2 * frows, 4 * elems)] * 3
    return pl.pallas_call(
        functools.partial(step_kernel, devices),
        out_shape=[
            jax.ShapeDtypeStruct((rows, elems), f32),
            jax.ShapeDtypeStruct((3, elems), f32),
        ],
        in_specs=[pl.BlockSpec(memory_space=pltpu.VMEM)] * len(args),
        out_specs=[pl.BlockSpec(memory_space=pltpu.VMEM)] * 2,
        scratch_shapes=[pltpu.VMEM(s, f32) for s in scratch]
        + [pltpu.VMEM(s, bf16) for s in packed]
        + [pltpu.VMEM((4, elems), i32)]
        + [pltpu.SemaphoreType.DMA((4 * LANES,))] * 2,
        compiler_params=pltpu.CompilerParams(
            vmem_limit_bytes=60000 * 1024, collective_id=0, has_side_effects=True
        ),
        name="ader_step",
    )(*args)


def solution(mesh):
    return jax.shard_map(
        body,
        mesh=mesh,
        in_specs=(
            P(None, "dom"),
            P(None, "dom"),
            P(None, "dom"),
            P("dom"),
            P(None, "dom"),
            P(None, "dom"),
            P(),
            P(),
            P(),
            P(),
            P(None, "dom"),
        ),
        out_specs=(P(None, "dom"), P(None, "dom")),
        check_vma=False,
    )
```

```python
import functools

import jax
import jax.numpy as jnp
from jax import lax
from jax.experimental import pallas as pl
from jax.experimental.pallas import tpu as pltpu
from jax.sharding import PartitionSpec as P

VARS = 9
TERMS = 6
REACH = 4
CAP = 16
FINE_DEV = 128
LANES = 2 * REACH + 1
SLOTS = LANES * CAP
STEPS = TERMS - 1
f32, bf16, i32 = jnp.float32, jnp.bfloat16, jnp.int32

dt_step = 0.5
root_third = 0.5773502691896258
H = 0.5 * dt_step

A0 = H
STEP_SCALE = [H * H / 2.0] + [H / (k + 2.0) for k in range(1, STEPS)]
C_OVER_A = [2.0 ** (k + 1) - 1.0 for k in range(TERMS)]

NEED = [(0, 1), (1, 1), (2, 1), (0, 2), (1, 2), (2, 2), (0, 3), (0, 3), (0, 3)]
PAIRS = [((6, 7), 0, 3), ((8, 3), 0, 3), ((0, 1), 0, 2), ((4, 2), 1, 2), ((5,), 2, 2)]
READS = [
    {3: 7, 5: 8, 6: 0, 7: 3, 8: 5},
    {3: 6, 4: 8, 6: 3, 7: 1, 8: 4},
    {4: 7, 5: 6, 6: 5, 7: 4, 8: 2},
]


def up_to(n, m):
    return -(-n // m) * m


def halves(x):
    high = x.astype(bf16)
    return high, (x - high.astype(f32)).astype(bf16)


def padded(x, rows):
    if x.shape[0] == rows:
        return x
    return jnp.concatenate([x, jnp.zeros((rows - x.shape[0], x.shape[1]), f32)], axis=0)


def right3(x, rows):
    high, low = halves(padded(x, rows))
    return jnp.concatenate([high, high, low], axis=0)


def left3(a):
    high = a.astype(bf16).astype(f32)
    return jnp.concatenate([high, a - high, high], axis=1).astype(bf16)


def stack2(x, rows):
    return jnp.concatenate(halves(padded(x, rows)), axis=0)


def mm(a, b):
    return jnp.dot(a, b, preferred_element_type=f32)


def mm_t(a, b):
    return lax.dot_general(a, b, (((1,), (1,)), ((), ())), preferred_element_type=f32)


def add(*terms):
    total = None
    for t in terms:
        if t is not None:
            total = t if total is None else total + t
    return total


def blocks(ref, size, base=0):
    return [ref[base + v * size : base + (v + 1) * size, :] for v in range(VARS)]


def put(ref, values, base=0):
    size = values[0].shape[0]
    for v in range(VARS):
        ref[base + v * size : base + (v + 1) * size, :] = values[v]


def row(ref, n):
    return ref[n : n + 1, :]


class Mat:
    def __init__(self, con, base, geo):
        self.lam, self.mu2 = row(con, base), row(con, base + 1)
        self.mg = [row(con, base + 2 + a) for a in range(3)]
        self.rg = [row(con, base + 5 + a) for a in range(3)]
        self.g = [row(geo, a) for a in range(3)]


def forward_mix(p, m):
    t = [m.g[a] * p(6 + a, a) for a in range(3)]
    spread = m.lam * (t[0] + t[1] + t[2])
    return [
        spread + m.mu2 * t[0],
        spread + m.mu2 * t[1],
        spread + m.mu2 * t[2],
        m.mg[0] * p(7, 0) + m.mg[1] * p(6, 1),
        m.mg[1] * p(8, 1) + m.mg[2] * p(7, 2),
        m.mg[0] * p(8, 0) + m.mg[2] * p(6, 2),
        m.rg[0] * p(0, 0) + m.rg[1] * p(3, 1) + m.rg[2] * p(5, 2),
        m.rg[0] * p(3, 0) + m.rg[1] * p(1, 1) + m.rg[2] * p(4, 2),
        m.rg[0] * p(5, 0) + m.rg[1] * p(4, 1) + m.rg[2] * p(2, 2),
    ]


def normal_mix(r, m):
    u = m.lam * (r[0] + r[1] + r[2])
    return [u + m.mu2 * r[a] for a in range(3)] + list(r[3:])


def backward_mix(p, m):
    return [
        m.rg[0] * p(6, 0),
        m.rg[1] * p(7, 1),
        m.rg[2] * p(8, 2),
        m.rg[0] * p(7, 0) + m.rg[1] * p(6, 1),
        m.rg[1] * p(8, 1) + m.rg[2] * p(7, 2),
        m.rg[0] * p(8, 0) + m.rg[2] * p(6, 2),
        m.g[0] * p(0, 0) + m.mg[1] * p(3, 1) + m.mg[2] * p(5, 2),
        m.g[1] * p(1, 1) + m.mg[0] * p(3, 0) + m.mg[2] * p(4, 2),
        m.g[2] * p(2, 2) + m.mg[1] * p(4, 1) + m.mg[0] * p(5, 0),
    ]


def products(mat, values):
    size, width = values[0].shape
    pitch = mat.shape[0] // 4
    out = {}
    if width == FINE_DEV:
        groups = PAIRS
    else:
        groups = [((v,), s, c) for v, (s, c) in enumerate(NEED)]
    for names, start, count in groups:
        x = [values[v] for v in names]
        x = x[0] if len(x) == 1 else jnp.concatenate(x, axis=1)
        y = mm(mat[start * pitch : (start + count) * pitch, :], right3(x, pitch))
        for n, v in enumerate(names):
            for i in range(count):
                out[v, (start + i) % 3] = y[
                    i * pitch : i * pitch + size, n * width : (n + 1) * width
                ]
    return lambda v, axis: out[v, axis]


def apply_step(mat, values, m):
    return forward_mix(products(mat, values), m)


def apply_back(mat, values, m):
    return backward_mix(products(mat, normal_mix(values, m)), m)


def fold8(x):
    total = x[0:8]
    for n in range(8, x.shape[0], 8):
        total = total + x[n : n + 8]
    return total


def group_sums(r, x):
    mixed = (r[0] + r[1] + r[2]) * (x[0] + x[1] + x[2])
    groups = [add(*[r[v] * x[v] for v in range(g, g + 3)]) for g in (0, 3, 6)]
    return [fold8(g) for g in [mixed] + groups]


def plus(total, more):
    return more if total is None else [a + b for a, b in zip(total, more)]


def narrow(x, hot_c, rows):
    y = mm_t(stack2(x, rows), hot_c)
    return y[: x.shape[0]] + y[rows : rows + x.shape[0]]


def widen(x, hot_c2, rows):
    high, low = halves(padded(x, rows))
    return mm(jnp.concatenate([high, low], axis=1), hot_c2)[: x.shape[0]]


def trace_faces(tr, window, own, own_hl, fb, elems):
    size = window.shape[0] // VARS
    rows = own_hl.shape[0] // 2
    for v in range(VARS):
        t = mm(tr[...], right3(window[v * size : (v + 1) * size, :], tr.shape[1] // 3))
        for g in range(4):
            own[v * fb : (v + 1) * fb, g * elems : (g + 1) * elems] = t[g * fb : (g + 1) * fb]
    for g in range(4):
        cols = slice(g * elems, (g + 1) * elems)
        high, low = halves(padded(own[:, cols], rows))
        own_hl[:rows, cols] = high
        own_hl[rows:, cols] = low


def turn_blocks(mat, x, which):
    fb = x[0].shape[0]
    first, second = which == 0, which == 1
    out = []
    for n in range(0, len(x), 2):
        pair = x[n] if n + 1 == len(x) else jnp.concatenate(x[n : n + 2], axis=0)
        y = mm(mat[...], right3(pair, 2 * fb))
        for i in range(min(2, len(x) - n)):
            part = [y[o * 2 * fb + i * fb : o * 2 * fb + (i + 1) * fb] for o in range(3)]
            out.append(jnp.where(first, part[0], jnp.where(second, part[1], part[2])))
    return out


def split_rows(x, fb):
    return [x[v * fb : (v + 1) * fb] for v in range(VARS)]


def local_outer(own_hl, hot, turn, tn, out, fb, elems, f):
    rows = own_hl.shape[0] // 2
    cols = slice(f * elems, (f + 1) * elems)
    y = mm(own_hl[...], hot[:, cols])
    raw = y[: VARS * fb] + y[rows : rows + VARS * fb]
    turned = turn_blocks(tn, split_rows(raw, fb), turn[f : f + 1, :])
    out[:, cols] = jnp.concatenate(turned, axis=0)


def serve(hot_in, own_hl, tx):
    rows = own_hl.shape[0] // 2
    tx[:, :rows] = mm_t(hot_in[...], own_hl[:rows, :]) + mm_t(hot_in[...], own_hl[rows:, :])
    tx[:, rows:] = jnp.zeros((tx.shape[0], tx.shape[1] - rows), f32)


def flipped(rx):
    x = rx[...]
    return padded(x, up_to(x.shape[0], 128)).T[:, : x.shape[0]]


def face_rows(f, x, fc):
    if f == 3:
        return forward_mix(lambda v, axis: x[v], fc)
    axis = 2 - f
    kl, kp, _, km, kr = fc
    t = x[6 + axis]
    rows = [kl * t] * 3 + [None] * 6
    rows[axis] = kp * t
    for v, source in READS[axis].items():
        rows[v] = (km if v < 6 else kr) * x[source]
    return rows


def face_rows_back(f, r, fc):
    if f == 3:
        s = normal_mix(r, fc)
        return backward_mix(lambda v, axis: s[v], fc)
    axis = 2 - f
    kl, _, k2, km, kr = fc
    out = [None] * VARS
    out[6 + axis] = kl * (r[0] + r[1] + r[2]) + k2 * r[axis]
    for v, source in READS[axis].items():
        out[source] = (km if v < 6 else kr) * r[v]
    return out


def face_consts(f, fcon, con):
    if f == 3:
        m = Mat.__new__(Mat)
        m.lam, m.mu2 = row(fcon, 15), row(fcon, 16)
        m.mg = [row(fcon, 17 + a) for a in range(3)]
        m.rg = [row(fcon, 20 + a) for a in range(3)]
        m.g = [row(fcon, 23 + a) for a in range(3)]
        return m
    return [row(fcon, 5 * f + n) for n in range(5)]


def far_side(rx, slot_turn, tn, hot_slot, out_loc, fb):
    rows = up_to(VARS * fb, 16)
    turned = turn_blocks(tn, split_rows(flipped(rx), fb), slot_turn[0:1, :])
    high_low = stack2(jnp.concatenate(turned, axis=0), rows)

    def far(f, elems):
        cols = slice(f * elems, (f + 1) * elems)
        y = mm(high_low, hot_slot[:, cols])
        return out_loc[:, cols] + (y[: VARS * fb] + y[rows : rows + VARS * fb])

    return far


def surface(lf, own, far, fcon, con, fb, elems, jump_ref, flux_ref):
    half_speed = row(fcon, 26)
    fluxes = [[] for _ in range(VARS)]
    for f in range(4):
        cols = slice(f * elems, (f + 1) * elems)
        a, b = split_rows(own[:, cols], fb), split_rows(far(f, elems), fb)
        rows = face_rows(f, [x + y for x, y in zip(a, b)], face_consts(f, fcon, con))
        for v in range(VARS):
            jump = a[v] - b[v]
            flux = add(half_speed * jump, rows[v])
            jump_ref[v * fb : (v + 1) * fb, cols] = jump
            flux_ref[v * fb : (v + 1) * fb, cols] = flux
            fluxes[v].append(flux)
    return [mm(lf[...], right3(jnp.concatenate(x, axis=0), 4 * fb)) for x in fluxes]


def face_sums(lifted, jump_ref, flux_ref, half_speed, fb, elems):
    total, speed = None, None
    for f in range(4):
        cols = slice(f * elems, (f + 1) * elems)
        r, d, x = [split_rows(ref[:, cols], fb) for ref in (lifted, jump_ref, flux_ref)]
        of_jump, of_flux = group_sums(r, d), group_sums(r, x)
        total = plus(total, [a - half_speed * b for a, b in zip(of_flux, of_jump)])
        more = of_jump[1] + of_jump[2] + of_jump[3]
        speed = more if speed is None else speed + more
    return total, speed


def faces_cot(seed, lt, tnt, turn, extra, fcon, con, lifted, own_cot, x_hl, fb, elems):
    half_speed = row(fcon, 26)
    rows = x_hl.shape[0] // 2
    for v in range(VARS):
        y = mm(lt[...], right3(seed[v], lt.shape[1] // 3))
        for f in range(4):
            lifted[v * fb : (v + 1) * fb, f * elems : (f + 1) * elems] = y[f * fb : (f + 1) * fb]
    for f in range(4):
        cols = slice(f * elems, (f + 1) * elems)
        r = split_rows(lifted[:, cols], fb)
        back = face_rows_back(f, r, face_consts(f, fcon, con))
        x = []
        for v in range(VARS):
            side = half_speed * r[v]
            own_cot[v * fb : (v + 1) * fb, cols] = add(side, back[v])
            x.append(-side if back[v] is None else back[v] - side)
        turned = turn_blocks(tnt, x, turn[f : f + 1, :])
        if extra is not None:
            turned.append(extra[:, cols])
        high, low = halves(padded(jnp.concatenate(turned, axis=0), rows))
        x_hl[:rows, cols] = high
        x_hl[rows:, cols] = low


def send_cot(hot_slot, x_hl, tx):
    serve(hot_slot, x_hl, tx)


def scatter_local(own_cot, x_hl, hot, fb, elems, g):
    rows = x_hl.shape[0] // 2
    cols = slice(g * elems, (g + 1) * elems)
    y = mm_t(x_hl[...], hot[cols, :])
    own_cot[:, cols] = own_cot[:, cols] + (y[: VARS * fb] + y[rows : rows + VARS * fb])


def faces_back(own_cot, rx, hot_in, trt, fb, elems):
    rows = up_to(VARS * fb, 16)
    arrived = stack2(flipped(rx)[: VARS * fb], rows)
    for g in range(4):
        cols = slice(g * elems, (g + 1) * elems)
        y = mm(arrived, hot_in[:, cols])
        own_cot[:, cols] = own_cot[:, cols] + (y[: VARS * fb] + y[rows : rows + VARS * fb])
    out = []
    for v in range(VARS):
        x = [own_cot[v * fb : (v + 1) * fb, g * elems : (g + 1) * elems] for g in range(4)]
        out.append(mm(trt[...], right3(jnp.concatenate(x, axis=0), 4 * fb)))
    return out


def weave(steps, pieces):
    done = 0
    for n, step in enumerate(steps):
        step()
        until = (n + 1) * len(pieces) // len(steps)
        for piece in pieces[done:until]:
            piece()
        done = until


def peers_of(devices):
    me = lax.axis_index("dom")
    shifts = [n + 1 for n in range(REACH)] + [-(n + 1) for n in range(REACH)] + [devices // 2]
    return [
        [lax.rem(me + sign * s + 2 * devices, devices) for s in shifts] for sign in (1, -1)
    ]


def send_all(peers, src, dst, send_sems, recv_sems, base=0):
    copies = []
    for n in reversed(range(LANES)):
        rows = pl.ds(n * CAP, CAP)
        copy = pltpu.make_async_remote_copy(
            src_ref=src.at[rows],
            dst_ref=dst.at[rows],
            send_sem=send_sems.at[base + n],
            recv_sem=recv_sems.at[base + n],
            device_id=(peers[n],),
            device_id_type=pl.DeviceIdType.MESH,
        )
        copy.start()
        copies.append(copy)
    return copies


def one_hot(mask):
    return jnp.where(mask, 1.0, 0.0).astype(bf16)


def face_places(
    devices, neighbours, orientation, fine, hot, hot_slot, hot_c, turn, slot_turn, extra
):
    elems = neighbours.shape[1]
    me = lax.axis_index("dom")
    at = lax.broadcasted_iota(i32, (16, elems), 0)
    square = (elems, elems)
    at_n, at_e = lax.broadcasted_iota(i32, square, 0), lax.broadcasted_iota(i32, square, 1)
    at_s = lax.broadcasted_iota(i32, (SLOTS, elems), 0)
    at_8 = lax.broadcasted_iota(i32, (8, elems), 0)
    earlier = one_hot(at_n <= at_e)
    lanes, marks, keys = [], [], []
    for f in range(4):
        cols = slice(f * elems, (f + 1) * elems)
        name, code = neighbours[f : f + 1, :], orientation[f : f + 1, :]
        far_face = sum(jnp.where(code >= 3 * g, 1, 0) for g in (1, 2, 3))
        turn[f : f + 1, :] = code - 3 * far_face
        present = name >= 0
        safe = jnp.maximum(name, 0)
        owner = jnp.floor((safe.astype(f32) + 0.5) * (1.0 / elems)).astype(i32)
        index = safe - owner * elems
        away = owner - me
        away = jnp.where(away < 0, away + devices, away)
        keys.append((cols, present & (away == 0), far_face, index))
        lane = jnp.where(
            away <= REACH,
            away - 1,
            jnp.where(away >= devices - REACH, REACH + devices - away - 1, 2 * REACH),
        )
        lane = jnp.where(present & (away != 0), lane, LANES)
        lanes.append(lane)
        marks.append(jnp.where(at == lane, 1.0, 0.0))
        index_f, face_f = index.astype(f32), far_face.astype(f32)
        extra[:, cols] = jnp.where(
            at_8 == 0, index_f, jnp.where(at_8 == 1, face_f, jnp.where(at_8 == 2, 1.0, 0.0))
        )
    is_fine = fine[...] == 1
    marks.append(jnp.where((at == 0) & is_fine, 1.0, 0.0))
    run = mm(jnp.concatenate(marks, axis=0).astype(bf16), earlier)
    carry = jnp.zeros((16, 1), f32)
    for f in range(4):
        cols = slice(f * elems, (f + 1) * elems)
        mine = run[16 * f : 16 * f + 16]
        rank = jnp.sum((mine + carry - 1.0) * marks[f], axis=0, keepdims=True).astype(i32)
        carry = carry + mine[:, elems - 1 :]
        slot = jnp.where(lanes[f] < LANES, lanes[f] * CAP + rank, -1)
        hot_slot[:, cols] = one_hot(at_s == slot)
    rank = jnp.where(is_fine, run[64:65].astype(i32) - 1, -1)
    picked = one_hot(lax.broadcasted_iota(i32, (FINE_DEV, elems), 0) == rank)
    hot_c[:FINE_DEV, :] = picked
    hot_c[FINE_DEV:, :] = picked
    turns = jnp.concatenate([turn[f : f + 1, :].astype(f32) for f in range(4)], axis=1)
    turns = jnp.broadcast_to(turns, (16, 4 * elems)).astype(bf16)
    slot_turn[...] = mm_t(turns, hot_slot[...])

    def fill(cols, local, far_face, index):
        names = at_n.astype(f32).astype(bf16)
        for g in range(4):
            key = jnp.where(local & (far_face == g), index, -1).astype(f32).astype(bf16)
            hot[g * elems : (g + 1) * elems, cols] = jnp.where(
                names == key, jnp.ones(square, bf16), jnp.zeros(square, bf16)
            )

    return [functools.partial(fill, *key) for key in keys]


def constants(mat_ref, geo_ref, con, fcon):
    lam, mu, rinv = [row(mat_ref, n) for n in range(3)]
    geo = [row(geo_ref, n) for n in range(3)]
    rows = [lam, 2.0 * mu] + [mu * g for g in geo] + [rinv * g for g in geo]
    base = jnp.concatenate(rows, axis=0)
    for n, scale in enumerate([-1.0] + STEP_SCALE):
        con[8 * n : 8 * n + 8, :] = scale * base
    rows = []
    for f in range(3):
        h = 0.5 * geo[2 - f]
        rows += [lam * h, (lam + 2.0 * mu) * h, 2.0 * mu * h, mu * h, rinv * h]
    h = [(-0.5 * root_third) * g for g in geo]
    rows += [lam, 2.0 * mu] + [mu * x for x in h] + [rinv * x for x in h] + h
    rows += [0.5 * jnp.sqrt((lam + 2.0 * mu) * rinv)]
    for n, x in enumerate(rows):
        fcon[n : n + 1, :] = x


def pitched(pad, matrices):
    pad[...] = jnp.zeros(pad.shape, f32)
    for n, x in enumerate(matrices):
        pad[n, : x.shape[0], : x.shape[1]] = x
    return [pad[n] for n in range(len(matrices))]


def turn_matrix(pad, matrices):
    zero = jnp.zeros(pad.shape[1:], f32)
    out = []
    for x in pitched(pad, matrices):
        out += [jnp.concatenate([x, zero], axis=1), jnp.concatenate([zero, x], axis=1)]
    return left3(jnp.concatenate(out, axis=0))


def step_kernel(
    devices,
    state_in, cot_in, mat_in, geo_in, fine_in, neighbours_in, orientation_in, stiffness_in,
    trace_in, lift_in, turns_in,
    final, grad,
    state, cot, mat_ref, geo_ref, stiffness, face_trace, face_lift, face_turns,
    w1, wc, w2, coarse, seed1, middle, vol1, vol2, cur, direct2,
    q1, q2, hist,
    own, lifted1, lifted2, out_loc, own_cot1, own_cot2, jump, flux,
    tx0, tx1, tx2, tx3, rx0, rx1, rx2, rx3,
    con, fcon, con_f, geo_f, extra, slot_turn,
    k_pad, t_pad, l_pad, n_pad,
    ks, kt, tr, lt, trt, lf, tn, tnt, hot, hot_slot, hot_in, hot_c, own_hl, x_hl1, x_hl2,
    fine, neighbours, orientation, turn, load_sems, send_sems, recv_sems,
):
    loads = [
        pltpu.make_async_copy(src, dst, load_sems.at[n])
        for n, (src, dst) in enumerate([
            (neighbours_in, neighbours), (orientation_in, orientation), (mat_in, mat_ref),
            (geo_in, geo_ref), (fine_in, fine), (stiffness_in, stiffness),
            (trace_in, face_trace), (lift_in, face_lift), (turns_in, face_turns),
            (cot_in, cot), (state_in, state),
        ])
    ]
    for load in loads:
        load.start()
    up, down = peers_of(devices)
    barrier = pltpu.get_barrier_semaphore()
    for peer in up:
        pl.semaphore_signal(
            barrier, inc=1, device_id=(peer,), device_id_type=pl.DeviceIdType.MESH
        )
    elems = state.shape[1]
    count = state.shape[0]
    size = count // VARS
    fb = t_pad.shape[1]
    wide = up_to(count, 16)
    part = functools.partial

    for load in loads[:9]:
        load.wait()
    constants(mat_ref, geo_ref, con, fcon)
    trace = jnp.concatenate(pitched(t_pad, [face_trace[:, g, :] for g in range(4)]), axis=0)
    tr[...] = left3(trace)
    trt[...] = left3(trace.T)[:size]
    lift = jnp.concatenate(pitched(l_pad, [-face_lift[:, f, :] for f in range(4)]), axis=0)
    lt[...] = left3(lift)
    lf[...] = left3(lift.T)[:size]
    turns = [face_turns[o] for o in range(3)]
    tn[...] = turn_matrix(n_pad, turns)
    tnt[...] = turn_matrix(n_pad, [x.T for x in turns])
    hot_fills = face_places(
        devices, neighbours, orientation, fine, hot, hot_slot, hot_c, turn, slot_turn, extra
    )
    base, half_speed = Mat(con, 0, geo_ref), row(fcon, 26)

    loads[9].wait()
    seed2 = blocks(cot, size)
    faces_cot(seed2, lt, tnt, turn, extra, fcon, con, lifted2, own_cot2, x_hl2, fb, elems)
    serve(hot_slot, x_hl2, tx0)
    pl.semaphore_wait(barrier, LANES)
    sent0 = send_all(up, tx0, rx0, send_sems, recv_sems, 0)

    stiff = pitched(k_pad, [stiffness[d] for d in range(3)])
    ks[...] = left3(jnp.concatenate(stiff + stiff[:1], axis=0))
    stiff = [x.T for x in stiff]
    kt[...] = left3(jnp.concatenate(stiff + stiff[:1], axis=0))
    is_fine = fine[...] == 1
    loads[10].wait()

    def step1(k):
        old = blocks(state, size) if k == 0 else blocks(q1, size, (k - 1) * count)
        put(q1, apply_step(ks, old, Mat(con, 8 * (k + 1), geo_ref)), k * count)

    def scatter(own_cot, x_hl):
        return [part(scatter_local, own_cot, x_hl, hot, fb, elems, g) for g in range(4)]

    def gather():
        return [
            part(local_outer, own_hl, hot, turn, tn, out_loc, fb, elems, f) for f in range(4)
        ]

    weave([part(step1, k) for k in range(STEPS)], hot_fills + scatter(own_cot2, x_hl2))
    for v in range(VARS):
        rows = slice(v * size, (v + 1) * size)
        terms = [A0 * state[rows, :]]
        terms += [q1[k * count + v * size : k * count + (v + 1) * size, :] for k in range(STEPS)]
        w1[rows, :] = add(*terms)
        later = add(*[c * t if c != 1.0 else t for c, t in zip(C_OVER_A, terms)])
        wc[rows, :] = jnp.where(is_fine, 0.0, later)
    trace_faces(tr, w1, own, own_hl, fb, elems)
    put(direct2, apply_back(ks, seed2, base))
    for copy in sent0:
        copy.wait()

    key = rx0[:, VARS * fb : VARS * fb + 3]
    key = jnp.where(key[:, 2:3] > 0.5, key[:, 1:2] * float(elems) + key[:, 0:1], -1.0)
    at = lax.broadcasted_iota(i32, (SLOTS, 4 * elems), 1)
    hot_in[...] = one_hot(at == key.astype(i32))
    serve(hot_in, own_hl, tx1)
    sent1 = send_all(down, tx1, rx1, send_sems, recv_sems, LANES)

    back = faces_back(own_cot2, rx0, hot_in, trt, fb, elems)
    back = [a + b for a, b in zip(back, blocks(direct2, size))]
    put(coarse, [jnp.where(is_fine, 0.0, x) for x in back])
    seeds = split_rows(narrow(jnp.concatenate(back, axis=0), hot_c[:FINE_DEV, :], wide), size)
    put(hist, seeds, (STEPS - 1) * count)
    narrow_con = mm_t(
        jnp.concatenate(
            halves(con[0:16, :]) + halves(padded(geo_ref[...], 16)), axis=0
        ),
        hot_c[:FINE_DEV, :],
    )
    geo_f[...] = narrow_con[32:40] + narrow_con[48:56]
    for n, scale in enumerate(STEP_SCALE):
        con_f[8 * n : 8 * n + 8, :] = -scale * (narrow_con[0:8] + narrow_con[16:24])

    def back2(k):
        r = apply_back(kt, blocks(hist, size, k * count), Mat(con_f, 8 * k, geo_f))
        scale = A0 if k == 0 else 1.0
        direct = blocks(hist, size, (STEPS - 1) * count)
        r = [a + (b if k else scale * b) for a, b in zip(r, direct)]
        if k:
            put(hist, r, (k - 1) * count)
        else:
            seed1[...] = widen(jnp.concatenate(r, axis=0), hot_c[...], wide) + cot[...]

    def volume(out, window):
        put(out, apply_step(kt, blocks(window, size), base))

    weave([part(back2, k) for k in range(STEPS - 1, -1, -1)], gather() + [part(volume, vol1, w1)])
    faces_cot(
        blocks(seed1, size), lt, tnt, turn, None, fcon, con, lifted1, own_cot1, x_hl1, fb, elems
    )
    serve(hot_slot, x_hl1, tx3)
    sent3 = send_all(up, tx3, rx3, send_sems, recv_sems, 2 * LANES)
    for copy in sent1:
        copy.wait()

    far = far_side(rx1, slot_turn, tn, hot_slot, out_loc, fb)
    change = surface(lf, own, far, fcon, con, fb, elems, jump, flux)
    put(middle, [
        s + m + c for s, m, c in zip(blocks(state, size), blocks(vol1, size), change)
    ])
    start = split_rows(narrow(middle[...], hot_c[:FINE_DEV, :], wide), size)
    first = [A0 * x for x in start]

    def step2(k):
        old = start if k == 0 else blocks(q2, size, (k - 1) * count)
        put(q2, apply_step(ks, old, Mat(con_f, 8 * k, geo_f)), k * count)

    def direct1():
        put(cur, apply_back(ks, blocks(seed1, size), base))

    weave(
        [part(step2, k) for k in range(STEPS)], scatter(own_cot1, x_hl1) + [direct1]
    )
    window = [
        add(first[v], *[
            q2[k * count + v * size : k * count + (v + 1) * size, :] for k in range(STEPS)
        ])
        for v in range(VARS)
    ]
    w2[...] = widen(jnp.concatenate(window, axis=0), hot_c[...], wide) + wc[...]
    sums, speed = face_sums(lifted1, jump, flux, half_speed, fb, elems)
    trace_faces(tr, w2, own, own_hl, fb, elems)
    serve(hot_in, own_hl, tx2)
    sent2 = send_all(down, tx2, rx2, send_sems, recv_sems, 3 * LANES)

    sums = plus(sums, group_sums(blocks(seed1, size), blocks(vol1, size)))
    fine_sums = None
    for k in range(STEPS):
        fine_sums = plus(
            fine_sums, group_sums(blocks(hist, size, k * count), blocks(q2, size, k * count))
        )
    fine_sums = [jnp.sum(x, axis=0, keepdims=True) for x in fine_sums]
    fine_sums = widen(jnp.concatenate(fine_sums + fine_sums, axis=0), hot_c[...], 16)
    for copy in sent3:
        copy.wait()
    back = faces_back(own_cot1, rx3, hot_in, trt, fb, elems)
    put(seed1, [a + b for a, b in zip(back, blocks(cur, size))])
    chain = [sums]

    def back1(k):
        r = [a + C_OVER_A[k] * b for a, b in zip(blocks(seed1, size), blocks(coarse, size))]
        if k < STEPS:
            old = blocks(cur, size)
            r = [a + b for a, b in zip(r, apply_back(kt, old, Mat(con, 8 * (k + 1), geo_ref)))]
        put(cur, r)
        chain[0] = plus(
            chain[0], group_sums(blocks(cur, size), blocks(q1, size, (k - 1) * count))
        )

    weave([part(back1, k) for k in range(STEPS, 0, -1)], gather() + [part(volume, vol2, w2)])
    sums = plus(chain[0], group_sums(seed2, blocks(vol2, size)))
    for copy in sent2:
        copy.wait()

    far = far_side(rx2, slot_turn, tn, hot_slot, out_loc, fb)
    change = surface(lf, own, far, fcon, con, fb, elems, jump, flux)
    put(final, [
        s + m + c for s, m, c in zip(blocks(middle, size), blocks(vol2, size), change)
    ])
    more, more_speed = face_sums(lifted2, jump, flux, half_speed, fb, elems)
    sums = [jnp.sum(a + b, axis=0, keepdims=True) for a, b in zip(sums, more)]
    sums = [a + fine_sums[n : n + 1] for n, a in enumerate(sums)]
    g_speed = 0.5 * jnp.sum(speed + more_speed, axis=0, keepdims=True)
    lam, mu, rinv = [row(mat_ref, n) for n in range(3)]
    wave = jnp.sqrt((lam + 2.0 * mu) * rinv)
    g_lam = sums[0] / (3.0 * lam + 2.0 * mu)
    g_mu = (sums[1] - lam * g_lam + sums[2]) / mu
    g_speed = g_speed / wave
    grad[...] = jnp.concatenate(
        [
            g_lam + 0.5 * g_speed * rinv,
            g_mu + g_speed * rinv,
            sums[3] / rinv + 0.5 * g_speed * (lam + 2.0 * mu),
        ],
        axis=0,
    )


def finish_kernel(final, grad, final_out, grad_out, sems):
    copies = [
        pltpu.make_async_copy(final, final_out, sems.at[0]),
        pltpu.make_async_copy(grad, grad_out, sems.at[1]),
    ]
    for copy in copies:
        copy.start()
    for copy in copies:
        copy.wait()


def body(
    start_state, material, geometry, clusters, neighbours, orientation,
    stiffness, face_trace, face_lift, face_turns, cotangent,
):
    rows, elems = start_state.shape
    basis = rows // VARS
    devices = lax.axis_size("dom")
    fb = up_to(face_trace.shape[1], 8)
    pitch = up_to(basis, 16)
    frows = up_to(VARS * fb + 8, 16)
    full, faces, slots = (rows, elems), (VARS * fb, 4 * elems), (SLOTS, up_to(frows, 128))
    args = (
        start_state, cotangent, material, geometry, clusters.reshape(1, elems), neighbours,
        orientation, stiffness, face_trace.transpose(1, 0, 2), face_lift.transpose(2, 0, 1),
        face_turns,
    )
    scratch = [x.shape for x in args[:4]] + [x.shape for x in args[7:]]
    scratch += [full] * 10
    scratch += [(STEPS * rows, elems)] + [(STEPS * rows, FINE_DEV)] * 2
    scratch += [faces] * 8 + [slots] * 8
    scratch += [(8 * TERMS, elems), (32, elems), (8 * STEPS, FINE_DEV), (8, FINE_DEV)]
    scratch += [(8, 4 * elems), (16, SLOTS)]
    scratch += [(3, pitch, pitch), (4, fb, pitch), (4, fb, pitch), (3, fb, fb)]
    packed = [(4 * pitch, 3 * pitch)] * 2 + [(4 * fb, 3 * pitch)] * 2
    packed += [(basis, 12 * fb)] * 2 + [(6 * fb, 6 * fb)] * 2
    packed += [(4 * elems, 4 * elems)] + [(SLOTS, 4 * elems)] * 2 + [(2 * FINE_DEV, elems)]
    packed += [(2 * frows, 4 * elems)] * 3
    args = [pltpu.with_memory_space_constraint(x, pltpu.HBM) for x in args]
    outs = pl.pallas_call(
        functools.partial(step_kernel, devices),
        out_shape=[
            jax.ShapeDtypeStruct((rows, elems), f32),
            jax.ShapeDtypeStruct((3, elems), f32),
        ],
        in_specs=[pl.BlockSpec(memory_space=pltpu.HBM)] * len(args),
        out_specs=[pl.BlockSpec(memory_space=pltpu.VMEM)] * 2,
        scratch_shapes=[pltpu.VMEM(s, f32) for s in scratch]
        + [pltpu.VMEM(s, bf16) for s in packed]
        + [pltpu.VMEM((1, elems), i32)]
        + [pltpu.VMEM((4, elems), i32)] * 3
        + [pltpu.SemaphoreType.DMA((len(args),))]
        + [pltpu.SemaphoreType.DMA((4 * LANES,))] * 2,
        compiler_params=pltpu.CompilerParams(
            vmem_limit_bytes=48 * 1024 * 1024, collective_id=0, has_side_effects=True
        ),
        name="ader_step",
    )(*args)
    return pl.pallas_call(
        finish_kernel,
        out_shape=[jax.ShapeDtypeStruct(x.shape, f32) for x in outs],
        in_specs=[pl.BlockSpec(memory_space=pltpu.VMEM)] * 2,
        out_specs=[pl.BlockSpec(memory_space=pl.ANY)] * 2,
        scratch_shapes=[pltpu.SemaphoreType.DMA((2,))],
        compiler_params=pltpu.CompilerParams(vmem_limit_bytes=2 * 1024 * 1024),
        name="finish",
    )(*outs)


def solution(mesh):
    return jax.shard_map(
        body,
        mesh=mesh,
        in_specs=(
            P(None, "dom"),
            P(None, "dom"),
            P(None, "dom"),
            P("dom"),
            P(None, "dom"),
            P(None, "dom"),
            P(),
            P(),
            P(),
            P(),
            P(None, "dom"),
        ),
        out_specs=(P(None, "dom"), P(None, "dom")),
        check_vma=False,
    )
```

```python
import functools

import jax
import jax.numpy as jnp
from jax import lax
from jax.experimental import pallas as pl
from jax.experimental.pallas import tpu as pltpu
from jax.sharding import PartitionSpec as P

VARS = 9
TERMS = 6
REACH = 4
CAP = 16
FINE_DEV = 128
LANES = 2 * REACH + 1
SLOTS = LANES * CAP
STEPS = TERMS - 1
f32, bf16, i32 = jnp.float32, jnp.bfloat16, jnp.int32

dt_step = 0.5
root_third = 0.5773502691896258
H = 0.5 * dt_step

A0 = H
STEP_SCALE = [H * H / 2.0] + [H / (k + 2.0) for k in range(1, STEPS)]
C_OVER_A = [2.0 ** (k + 1) - 1.0 for k in range(TERMS)]

NEED = [(0, 1), (1, 1), (2, 1), (0, 2), (1, 2), (2, 2), (0, 3), (0, 3), (0, 3)]
PAIRS = [((6, 7), 0, 3), ((8, 3), 0, 3), ((0, 1), 0, 2), ((4, 2), 1, 2), ((5,), 2, 2)]
READS = [
    {3: 7, 5: 8, 6: 0, 7: 3, 8: 5},
    {3: 6, 4: 8, 6: 3, 7: 1, 8: 4},
    {4: 7, 5: 6, 6: 5, 7: 4, 8: 2},
]


def up_to(n, m):
    return -(-n // m) * m


def halves(x):
    high = x.astype(bf16)
    return high, (x - high.astype(f32)).astype(bf16)


def padded(x, rows):
    if x.shape[0] == rows:
        return x
    return jnp.concatenate([x, jnp.zeros((rows - x.shape[0], x.shape[1]), f32)], axis=0)


def right3(x, rows):
    high, low = halves(padded(x, rows))
    return jnp.concatenate([high, high, low], axis=0)


def left3(a):
    high = a.astype(bf16).astype(f32)
    return jnp.concatenate([high, a - high, high], axis=1).astype(bf16)


def stack2(x, rows):
    return jnp.concatenate(halves(padded(x, rows)), axis=0)


def mm(a, b):
    return jnp.dot(a, b, preferred_element_type=f32)


def mm_t(a, b):
    return lax.dot_general(a, b, (((1,), (1,)), ((), ())), preferred_element_type=f32)


def add(*terms):
    total = None
    for t in terms:
        if t is not None:
            total = t if total is None else total + t
    return total


def blocks(ref, size, base=0):
    return [ref[base + v * size : base + (v + 1) * size, :] for v in range(VARS)]


def put(ref, values, base=0):
    size = values[0].shape[0]
    for v in range(VARS):
        ref[base + v * size : base + (v + 1) * size, :] = values[v]


def row(ref, n):
    return ref[n : n + 1, :]


class Mat:
    def __init__(self, con, base, geo):
        self.lam, self.mu2 = row(con, base), row(con, base + 1)
        self.mg = [row(con, base + 2 + a) for a in range(3)]
        self.rg = [row(con, base + 5 + a) for a in range(3)]
        self.g = [row(geo, a) for a in range(3)]


def forward_mix(p, m):
    t = [m.g[a] * p(6 + a, a) for a in range(3)]
    spread = m.lam * (t[0] + t[1] + t[2])
    return [
        spread + m.mu2 * t[0],
        spread + m.mu2 * t[1],
        spread + m.mu2 * t[2],
        m.mg[0] * p(7, 0) + m.mg[1] * p(6, 1),
        m.mg[1] * p(8, 1) + m.mg[2] * p(7, 2),
        m.mg[0] * p(8, 0) + m.mg[2] * p(6, 2),
        m.rg[0] * p(0, 0) + m.rg[1] * p(3, 1) + m.rg[2] * p(5, 2),
        m.rg[0] * p(3, 0) + m.rg[1] * p(1, 1) + m.rg[2] * p(4, 2),
        m.rg[0] * p(5, 0) + m.rg[1] * p(4, 1) + m.rg[2] * p(2, 2),
    ]


def normal_mix(r, m):
    u = m.lam * (r[0] + r[1] + r[2])
    return [u + m.mu2 * r[a] for a in range(3)] + list(r[3:])


def backward_mix(p, m):
    return [
        m.rg[0] * p(6, 0),
        m.rg[1] * p(7, 1),
        m.rg[2] * p(8, 2),
        m.rg[0] * p(7, 0) + m.rg[1] * p(6, 1),
        m.rg[1] * p(8, 1) + m.rg[2] * p(7, 2),
        m.rg[0] * p(8, 0) + m.rg[2] * p(6, 2),
        m.g[0] * p(0, 0) + m.mg[1] * p(3, 1) + m.mg[2] * p(5, 2),
        m.g[1] * p(1, 1) + m.mg[0] * p(3, 0) + m.mg[2] * p(4, 2),
        m.g[2] * p(2, 2) + m.mg[1] * p(4, 1) + m.mg[0] * p(5, 0),
    ]


def products(mat, values):
    size, width = values[0].shape
    pitch = mat.shape[0] // 4
    out = {}
    if width == FINE_DEV:
        groups = PAIRS
    else:
        groups = [((v,), s, c) for v, (s, c) in enumerate(NEED)]
    for names, start, count in groups:
        x = [values[v] for v in names]
        x = x[0] if len(x) == 1 else jnp.concatenate(x, axis=1)
        y = mm(mat[start * pitch : (start + count) * pitch, :], right3(x, pitch))
        for n, v in enumerate(names):
            for i in range(count):
                out[v, (start + i) % 3] = y[
                    i * pitch : i * pitch + size, n * width : (n + 1) * width
                ]
    return lambda v, axis: out[v, axis]


def apply_step(mat, values, m):
    return forward_mix(products(mat, values), m)


def apply_back(mat, values, m):
    return backward_mix(products(mat, normal_mix(values, m)), m)


def fold8(x):
    total = x[0:8]
    for n in range(8, x.shape[0], 8):
        total = total + x[n : n + 8]
    return total


def group_sums(r, x):
    mixed = (r[0] + r[1] + r[2]) * (x[0] + x[1] + x[2])
    groups = [add(*[r[v] * x[v] for v in range(g, g + 3)]) for g in (0, 3, 6)]
    return [fold8(g) for g in [mixed] + groups]


def plus(total, more):
    return more if total is None else [a + b for a, b in zip(total, more)]


def narrow(x, hot_c, rows):
    y = mm_t(stack2(x, rows), hot_c)
    return y[: x.shape[0]] + y[rows : rows + x.shape[0]]


def widen(x, hot_c2, rows):
    high, low = halves(padded(x, rows))
    return mm(jnp.concatenate([high, low], axis=1), hot_c2)[: x.shape[0]]


def trace_faces(tr, window, own, own_hl, fb, elems):
    size = window.shape[0] // VARS
    rows = own_hl.shape[0] // 2
    for v in range(VARS):
        t = mm(tr[...], right3(window[v * size : (v + 1) * size, :], tr.shape[1] // 3))
        for g in range(4):
            own[v * fb : (v + 1) * fb, g * elems : (g + 1) * elems] = t[g * fb : (g + 1) * fb]
    for g in range(4):
        cols = slice(g * elems, (g + 1) * elems)
        high, low = halves(padded(own[:, cols], rows))
        own_hl[:rows, cols] = high
        own_hl[rows:, cols] = low


def turn_blocks(mat, x, which):
    fb = x[0].shape[0]
    first, second = which == 0, which == 1
    out = []
    for n in range(0, len(x), 2):
        pair = x[n] if n + 1 == len(x) else jnp.concatenate(x[n : n + 2], axis=0)
        y = mm(mat[...], right3(pair, 2 * fb))
        for i in range(min(2, len(x) - n)):
            part = [y[o * 2 * fb + i * fb : o * 2 * fb + (i + 1) * fb] for o in range(3)]
            out.append(jnp.where(first, part[0], jnp.where(second, part[1], part[2])))
    return out


def split_rows(x, fb):
    return [x[v * fb : (v + 1) * fb] for v in range(VARS)]


def local_outer(own_hl, hot, turn, tn, out, fb, elems, f):
    rows = own_hl.shape[0] // 2
    cols = slice(f * elems, (f + 1) * elems)
    high, low = [mm(own_hl[n * rows : (n + 1) * rows, :], hot[:, cols]) for n in range(2)]
    raw = high[: VARS * fb] + low[: VARS * fb]
    turned = turn_blocks(tn, split_rows(raw, fb), turn[f : f + 1, :])
    out[:, cols] = jnp.concatenate(turned, axis=0)


def serve(hot_in, own_hl, tx):
    rows = own_hl.shape[0] // 2
    tx[:, :rows] = mm_t(hot_in[...], own_hl[:rows, :]) + mm_t(hot_in[...], own_hl[rows:, :])
    tx[:, rows:] = jnp.zeros((tx.shape[0], tx.shape[1] - rows), f32)


def flipped(rx):
    x = rx[...]
    return padded(x, up_to(x.shape[0], 128)).T[:, : x.shape[0]]


def face_rows(f, x, fc):
    if f == 3:
        return forward_mix(lambda v, axis: x[v], fc)
    axis = 2 - f
    kl, kp, _, km, kr = fc
    t = x[6 + axis]
    rows = [kl * t] * 3 + [None] * 6
    rows[axis] = kp * t
    for v, source in READS[axis].items():
        rows[v] = (km if v < 6 else kr) * x[source]
    return rows


def face_rows_back(f, r, fc):
    if f == 3:
        s = normal_mix(r, fc)
        return backward_mix(lambda v, axis: s[v], fc)
    axis = 2 - f
    kl, _, k2, km, kr = fc
    out = [None] * VARS
    out[6 + axis] = kl * (r[0] + r[1] + r[2]) + k2 * r[axis]
    for v, source in READS[axis].items():
        out[source] = (km if v < 6 else kr) * r[v]
    return out


def face_consts(f, fcon, con):
    if f == 3:
        m = Mat.__new__(Mat)
        m.lam, m.mu2 = row(fcon, 15), row(fcon, 16)
        m.mg = [row(fcon, 17 + a) for a in range(3)]
        m.rg = [row(fcon, 20 + a) for a in range(3)]
        m.g = [row(fcon, 23 + a) for a in range(3)]
        return m
    return [row(fcon, 5 * f + n) for n in range(5)]


def far_side(rx, slot_turn, tn, hot_slot, out_loc, fb):
    rows = up_to(VARS * fb, 16)
    turned = turn_blocks(tn, split_rows(flipped(rx), fb), slot_turn[0:1, :])
    high_low = stack2(jnp.concatenate(turned, axis=0), rows)

    def far(f, elems):
        cols = slice(f * elems, (f + 1) * elems)
        y = mm(high_low, hot_slot[:, cols])
        return out_loc[:, cols] + (y[: VARS * fb] + y[rows : rows + VARS * fb])

    return far


def surface(lf, own, far, fcon, con, fb, elems, jump_ref, flux_ref):
    half_speed = row(fcon, 26)
    fluxes = [[] for _ in range(VARS)]
    for f in range(4):
        cols = slice(f * elems, (f + 1) * elems)
        a, b = split_rows(own[:, cols], fb), split_rows(far(f, elems), fb)
        rows = face_rows(f, [x + y for x, y in zip(a, b)], face_consts(f, fcon, con))
        for v in range(VARS):
            jump = a[v] - b[v]
            flux = add(half_speed * jump, rows[v])
            jump_ref[v * fb : (v + 1) * fb, cols] = jump
            flux_ref[v * fb : (v + 1) * fb, cols] = flux
            fluxes[v].append(flux)
    return [mm(lf[...], right3(jnp.concatenate(x, axis=0), 4 * fb)) for x in fluxes]


def face_sums(lifted, jump_ref, flux_ref, half_speed, fb, elems):
    total, speed = None, None
    for f in range(4):
        cols = slice(f * elems, (f + 1) * elems)
        r, d, x = [split_rows(ref[:, cols], fb) for ref in (lifted, jump_ref, flux_ref)]
        of_jump, of_flux = group_sums(r, d), group_sums(r, x)
        total = plus(total, [a - half_speed * b for a, b in zip(of_flux, of_jump)])
        more = of_jump[1] + of_jump[2] + of_jump[3]
        speed = more if speed is None else speed + more
    return total, speed


def faces_cot(seed, lt, tnt, turn, extra, fcon, con, lifted, own_cot, x_hl, fb, elems):
    half_speed = row(fcon, 26)
    rows = x_hl.shape[0] // 2
    for v in range(VARS):
        y = mm(lt[...], right3(seed[v], lt.shape[1] // 3))
        for f in range(4):
            lifted[v * fb : (v + 1) * fb, f * elems : (f + 1) * elems] = y[f * fb : (f + 1) * fb]
    for f in range(4):
        cols = slice(f * elems, (f + 1) * elems)
        r = split_rows(lifted[:, cols], fb)
        back = face_rows_back(f, r, face_consts(f, fcon, con))
        x = []
        for v in range(VARS):
            side = half_speed * r[v]
            own_cot[v * fb : (v + 1) * fb, cols] = add(side, back[v])
            x.append(-side if back[v] is None else back[v] - side)
        turned = turn_blocks(tnt, x, turn[f : f + 1, :])
        if extra is not None:
            turned.append(extra[:, cols])
        high, low = halves(padded(jnp.concatenate(turned, axis=0), rows))
        x_hl[:rows, cols] = high
        x_hl[rows:, cols] = low


def send_cot(hot_slot, x_hl, tx):
    serve(hot_slot, x_hl, tx)


def scatter_local(own_cot, x_hl, hot, fb, elems, g):
    rows = x_hl.shape[0] // 2
    cols = slice(g * elems, (g + 1) * elems)
    y = mm_t(x_hl[...], hot[cols, :])
    own_cot[:, cols] = own_cot[:, cols] + (y[: VARS * fb] + y[rows : rows + VARS * fb])


def faces_back(own_cot, rx, hot_in, trt, fb, elems):
    rows = up_to(VARS * fb, 16)
    arrived = stack2(flipped(rx)[: VARS * fb], rows)
    for g in range(4):
        cols = slice(g * elems, (g + 1) * elems)
        y = mm(arrived, hot_in[:, cols])
        own_cot[:, cols] = own_cot[:, cols] + (y[: VARS * fb] + y[rows : rows + VARS * fb])
    out = []
    for v in range(VARS):
        x = [own_cot[v * fb : (v + 1) * fb, g * elems : (g + 1) * elems] for g in range(4)]
        out.append(mm(trt[...], right3(jnp.concatenate(x, axis=0), 4 * fb)))
    return out


def weave(steps, pieces):
    done = 0
    for n, step in enumerate(steps):
        step()
        until = (n + 1) * len(pieces) // len(steps)
        for piece in pieces[done:until]:
            piece()
        done = until


def peers_of(devices):
    me = lax.axis_index("dom")
    shifts = [n + 1 for n in range(REACH)] + [-(n + 1) for n in range(REACH)] + [devices // 2]
    return [
        [lax.rem(me + sign * s + 2 * devices, devices) for s in shifts] for sign in (1, -1)
    ]


def send_all(peers, src, dst, send_sems, recv_sems, base=0):
    copies = []
    for n in reversed(range(LANES)):
        rows = pl.ds(n * CAP, CAP)
        copy = pltpu.make_async_remote_copy(
            src_ref=src.at[rows],
            dst_ref=dst.at[rows],
            send_sem=send_sems.at[base + n],
            recv_sem=recv_sems.at[base + n],
            device_id=(peers[n],),
            device_id_type=pl.DeviceIdType.MESH,
        )
        copy.start()
        copies.append(copy)
    return copies


def one_hot(mask):
    return jnp.where(mask, 1.0, 0.0).astype(bf16)


def face_places(
    devices, neighbours, orientation, fine, hot, hot_slot, hot_c, turn, slot_turn, extra
):
    elems = neighbours.shape[1]
    me = lax.axis_index("dom")
    at = lax.broadcasted_iota(i32, (16, elems), 0)
    square = (elems, elems)
    at_n, at_e = lax.broadcasted_iota(i32, square, 0), lax.broadcasted_iota(i32, square, 1)
    at_s = lax.broadcasted_iota(i32, (SLOTS, elems), 0)
    at_8 = lax.broadcasted_iota(i32, (8, elems), 0)
    earlier = one_hot(at_n <= at_e)
    lanes, marks, keys = [], [], []
    for f in range(4):
        cols = slice(f * elems, (f + 1) * elems)
        name, code = neighbours[f : f + 1, :], orientation[f : f + 1, :]
        far_face = sum(jnp.where(code >= 3 * g, 1, 0) for g in (1, 2, 3))
        turn[f : f + 1, :] = code - 3 * far_face
        present = name >= 0
        safe = jnp.maximum(name, 0)
        owner = jnp.floor((safe.astype(f32) + 0.5) * (1.0 / elems)).astype(i32)
        index = safe - owner * elems
        away = owner - me
        away = jnp.where(away < 0, away + devices, away)
        keys.append((cols, present & (away == 0), far_face, index))
        lane = jnp.where(
            away <= REACH,
            away - 1,
            jnp.where(away >= devices - REACH, REACH + devices - away - 1, 2 * REACH),
        )
        lane = jnp.where(present & (away != 0), lane, LANES)
        lanes.append(lane)
        marks.append(jnp.where(at == lane, 1.0, 0.0))
        index_f, face_f = index.astype(f32), far_face.astype(f32)
        extra[:, cols] = jnp.where(
            at_8 == 0, index_f, jnp.where(at_8 == 1, face_f, jnp.where(at_8 == 2, 1.0, 0.0))
        )
    is_fine = fine[...] == 1
    marks.append(jnp.where((at == 0) & is_fine, 1.0, 0.0))
    run = mm(jnp.concatenate(marks, axis=0).astype(bf16), earlier)
    carry = jnp.zeros((16, 1), f32)
    for f in range(4):
        cols = slice(f * elems, (f + 1) * elems)
        mine = run[16 * f : 16 * f + 16]
        rank = jnp.sum((mine + carry - 1.0) * marks[f], axis=0, keepdims=True).astype(i32)
        carry = carry + mine[:, elems - 1 :]
        slot = jnp.where(lanes[f] < LANES, lanes[f] * CAP + rank, -1)
        hot_slot[:, cols] = one_hot(at_s == slot)
    rank = jnp.where(is_fine, run[64:65].astype(i32) - 1, -1)
    picked = one_hot(lax.broadcasted_iota(i32, (FINE_DEV, elems), 0) == rank)
    hot_c[:FINE_DEV, :] = picked
    hot_c[FINE_DEV:, :] = picked
    turns = jnp.concatenate([turn[f : f + 1, :].astype(f32) for f in range(4)], axis=1)
    turns = jnp.broadcast_to(turns, (16, 4 * elems)).astype(bf16)
    slot_turn[...] = mm_t(turns, hot_slot[...])

    def fill(cols, local, far_face, index):
        names = at_n.astype(f32).astype(bf16)
        for g in range(4):
            key = jnp.where(local & (far_face == g), index, -1).astype(f32).astype(bf16)
            hot[g * elems : (g + 1) * elems, cols] = jnp.where(
                names == key, jnp.ones(square, bf16), jnp.zeros(square, bf16)
            )

    return [functools.partial(fill, *key) for key in keys]


def constants(mat_ref, geo_ref, con, fcon):
    lam, mu, rinv = [row(mat_ref, n) for n in range(3)]
    geo = [row(geo_ref, n) for n in range(3)]
    rows = [lam, 2.0 * mu] + [mu * g for g in geo] + [rinv * g for g in geo]
    base = jnp.concatenate(rows, axis=0)
    for n, scale in enumerate([-1.0] + STEP_SCALE):
        con[8 * n : 8 * n + 8, :] = scale * base
    rows = []
    for f in range(3):
        h = 0.5 * geo[2 - f]
        rows += [lam * h, (lam + 2.0 * mu) * h, 2.0 * mu * h, mu * h, rinv * h]
    h = [(-0.5 * root_third) * g for g in geo]
    rows += [lam, 2.0 * mu] + [mu * x for x in h] + [rinv * x for x in h] + h
    rows += [0.5 * jnp.sqrt((lam + 2.0 * mu) * rinv)]
    for n, x in enumerate(rows):
        fcon[n : n + 1, :] = x


def pitched(pad, matrices):
    pad[...] = jnp.zeros(pad.shape, f32)
    for n, x in enumerate(matrices):
        pad[n, : x.shape[0], : x.shape[1]] = x
    return [pad[n] for n in range(len(matrices))]


def turn_matrix(pad, matrices):
    zero = jnp.zeros(pad.shape[1:], f32)
    out = []
    for x in pitched(pad, matrices):
        out += [jnp.concatenate([x, zero], axis=1), jnp.concatenate([zero, x], axis=1)]
    return left3(jnp.concatenate(out, axis=0))


def step_kernel(
    devices,
    state_in, cot_in, mat_in, geo_in, fine_in, neighbours_in, orientation_in, stiffness_in,
    trace_in, lift_in, turns_in,
    final, grad,
    state, cot, mat_ref, geo_ref, stiffness, face_trace, face_lift, face_turns,
    w1, wc, w2, coarse, seed1, middle, vol1, vol2, cur, direct2,
    q1, q2, hist,
    own, lifted1, lifted2, out_loc, own_cot1, own_cot2, jump, flux,
    tx0, tx1, tx2, tx3, rx0, rx1, rx2, rx3,
    con, fcon, con_f, geo_f, extra, slot_turn,
    k_pad, t_pad, l_pad, n_pad,
    ks, kt, tr, lt, trt, lf, tn, tnt, hot, hot_slot, hot_in, hot_c, own_hl, x_hl1, x_hl2,
    fine, neighbours, orientation, turn, load_sems, send_sems, recv_sems,
):
    loads = [
        pltpu.make_async_copy(src, dst, load_sems.at[n])
        for n, (src, dst) in enumerate([
            (neighbours_in, neighbours), (orientation_in, orientation), (mat_in, mat_ref),
            (geo_in, geo_ref), (fine_in, fine), (stiffness_in, stiffness),
            (trace_in, face_trace), (lift_in, face_lift), (turns_in, face_turns),
            (cot_in, cot), (state_in, state),
        ])
    ]
    for load in loads:
        load.start()
    up, down = peers_of(devices)
    barrier = pltpu.get_barrier_semaphore()
    for peer in up:
        pl.semaphore_signal(
            barrier, inc=1, device_id=(peer,), device_id_type=pl.DeviceIdType.MESH
        )
    elems = state.shape[1]
    count = state.shape[0]
    size = count // VARS
    fb = t_pad.shape[1]
    wide = up_to(count, 16)
    part = functools.partial

    for load in loads[:9]:
        load.wait()
    constants(mat_ref, geo_ref, con, fcon)
    trace = jnp.concatenate(pitched(t_pad, [face_trace[:, g, :] for g in range(4)]), axis=0)
    tr[...] = left3(trace)
    trt[...] = left3(trace.T)[:size]
    lift = jnp.concatenate(pitched(l_pad, [-face_lift[:, f, :] for f in range(4)]), axis=0)
    lt[...] = left3(lift)
    lf[...] = left3(lift.T)[:size]
    turns = [face_turns[o] for o in range(3)]
    tn[...] = turn_matrix(n_pad, turns)
    tnt[...] = turn_matrix(n_pad, [x.T for x in turns])
    hot_fills = face_places(
        devices, neighbours, orientation, fine, hot, hot_slot, hot_c, turn, slot_turn, extra
    )
    base, half_speed = Mat(con, 0, geo_ref), row(fcon, 26)

    loads[9].wait()
    seed2 = blocks(cot, size)
    faces_cot(seed2, lt, tnt, turn, extra, fcon, con, lifted2, own_cot2, x_hl2, fb, elems)
    serve(hot_slot, x_hl2, tx0)

    def scatter(own_cot, x_hl):
        return [part(scatter_local, own_cot, x_hl, hot, fb, elems, g) for g in range(4)]

    for piece in hot_fills + scatter(own_cot2, x_hl2):
        piece()
    pl.semaphore_wait(barrier, LANES)
    sent0 = send_all(up, tx0, rx0, send_sems, recv_sems, 0)

    stiff = pitched(k_pad, [stiffness[d] for d in range(3)])
    ks[...] = left3(jnp.concatenate(stiff + stiff[:1], axis=0))
    stiff = [x.T for x in stiff]
    kt[...] = left3(jnp.concatenate(stiff + stiff[:1], axis=0))
    is_fine = fine[...] == 1
    loads[10].wait()

    def step1(k):
        old = blocks(state, size) if k == 0 else blocks(q1, size, (k - 1) * count)
        put(q1, apply_step(ks, old, Mat(con, 8 * (k + 1), geo_ref)), k * count)

    def gather():
        return [
            part(local_outer, own_hl, hot, turn, tn, out_loc, fb, elems, f) for f in range(4)
        ]

    def volume(out, window):
        put(out, apply_step(kt, blocks(window, size), base))

    for k in range(STEPS):
        step1(k)
    for v in range(VARS):
        rows = slice(v * size, (v + 1) * size)
        terms = [A0 * state[rows, :]]
        terms += [q1[k * count + v * size : k * count + (v + 1) * size, :] for k in range(STEPS)]
        w1[rows, :] = add(*terms)
        later = add(*[c * t if c != 1.0 else t for c, t in zip(C_OVER_A, terms)])
        wc[rows, :] = jnp.where(is_fine, 0.0, later)
    trace_faces(tr, w1, own, own_hl, fb, elems)
    for piece in gather():
        piece()
    volume(vol1, w1)
    put(direct2, apply_back(ks, seed2, base))
    for copy in sent0:
        copy.wait()

    key = rx0[:, VARS * fb : VARS * fb + 3]
    key = jnp.where(key[:, 2:3] > 0.5, key[:, 1:2] * float(elems) + key[:, 0:1], -1.0)
    at = lax.broadcasted_iota(i32, (SLOTS, 4 * elems), 1)
    hot_in[...] = one_hot(at == key.astype(i32))
    serve(hot_in, own_hl, tx1)
    sent1 = send_all(down, tx1, rx1, send_sems, recv_sems, LANES)

    back = faces_back(own_cot2, rx0, hot_in, trt, fb, elems)
    back = [a + b for a, b in zip(back, blocks(direct2, size))]
    put(coarse, [jnp.where(is_fine, 0.0, x) for x in back])
    seeds = split_rows(narrow(jnp.concatenate(back, axis=0), hot_c[:FINE_DEV, :], wide), size)
    put(hist, seeds, (STEPS - 1) * count)
    narrow_con = mm_t(
        jnp.concatenate(
            halves(con[0:16, :]) + halves(padded(geo_ref[...], 16)), axis=0
        ),
        hot_c[:FINE_DEV, :],
    )
    geo_f[...] = narrow_con[32:40] + narrow_con[48:56]
    for n, scale in enumerate(STEP_SCALE):
        con_f[8 * n : 8 * n + 8, :] = -scale * (narrow_con[0:8] + narrow_con[16:24])

    def back2(k):
        r = apply_back(kt, blocks(hist, size, k * count), Mat(con_f, 8 * k, geo_f))
        scale = A0 if k == 0 else 1.0
        direct = blocks(hist, size, (STEPS - 1) * count)
        r = [a + (b if k else scale * b) for a, b in zip(r, direct)]
        if k:
            put(hist, r, (k - 1) * count)
        else:
            seed1[...] = widen(jnp.concatenate(r, axis=0), hot_c[...], wide) + cot[...]

    for k in range(STEPS - 1, -1, -1):
        back2(k)
    faces_cot(
        blocks(seed1, size), lt, tnt, turn, None, fcon, con, lifted1, own_cot1, x_hl1, fb, elems
    )
    serve(hot_slot, x_hl1, tx3)
    sent3 = send_all(up, tx3, rx3, send_sems, recv_sems, 2 * LANES)
    for piece in scatter(own_cot1, x_hl1):
        piece()
    put(cur, apply_back(ks, blocks(seed1, size), base))
    for copy in sent1:
        copy.wait()

    far = far_side(rx1, slot_turn, tn, hot_slot, out_loc, fb)
    change = surface(lf, own, far, fcon, con, fb, elems, jump, flux)
    put(middle, [
        s + m + c for s, m, c in zip(blocks(state, size), blocks(vol1, size), change)
    ])
    start = split_rows(narrow(middle[...], hot_c[:FINE_DEV, :], wide), size)
    first = [A0 * x for x in start]

    def step2(k):
        old = start if k == 0 else blocks(q2, size, (k - 1) * count)
        put(q2, apply_step(ks, old, Mat(con_f, 8 * k, geo_f)), k * count)

    for k in range(STEPS):
        step2(k)
    window = [
        add(first[v], *[
            q2[k * count + v * size : k * count + (v + 1) * size, :] for k in range(STEPS)
        ])
        for v in range(VARS)
    ]
    w2[...] = widen(jnp.concatenate(window, axis=0), hot_c[...], wide) + wc[...]
    trace_faces(tr, w2, own, own_hl, fb, elems)
    serve(hot_in, own_hl, tx2)
    sent2 = send_all(down, tx2, rx2, send_sems, recv_sems, 3 * LANES)

    sums, speed = face_sums(lifted1, jump, flux, half_speed, fb, elems)
    sums = plus(sums, group_sums(blocks(seed1, size), blocks(vol1, size)))
    fine_sums = None
    for k in range(STEPS):
        fine_sums = plus(
            fine_sums, group_sums(blocks(hist, size, k * count), blocks(q2, size, k * count))
        )
    fine_sums = [jnp.sum(x, axis=0, keepdims=True) for x in fine_sums]
    fine_sums = widen(jnp.concatenate(fine_sums + fine_sums, axis=0), hot_c[...], 16)
    for copy in sent3:
        copy.wait()
    back = faces_back(own_cot1, rx3, hot_in, trt, fb, elems)
    put(seed1, [a + b for a, b in zip(back, blocks(cur, size))])
    chain = [sums]

    def back1(k):
        r = [a + C_OVER_A[k] * b for a, b in zip(blocks(seed1, size), blocks(coarse, size))]
        if k < STEPS:
            old = blocks(cur, size)
            r = [a + b for a, b in zip(r, apply_back(kt, old, Mat(con, 8 * (k + 1), geo_ref)))]
        put(cur, r)
        chain[0] = plus(
            chain[0], group_sums(blocks(cur, size), blocks(q1, size, (k - 1) * count))
        )

    weave([part(back1, k) for k in range(STEPS, 0, -1)], gather() + [part(volume, vol2, w2)])
    sums = plus(chain[0], group_sums(seed2, blocks(vol2, size)))
    for copy in sent2:
        copy.wait()

    far = far_side(rx2, slot_turn, tn, hot_slot, out_loc, fb)
    change = surface(lf, own, far, fcon, con, fb, elems, jump, flux)
    put(final, [
        s + m + c for s, m, c in zip(blocks(middle, size), blocks(vol2, size), change)
    ])
    more, more_speed = face_sums(lifted2, jump, flux, half_speed, fb, elems)
    sums = [jnp.sum(a + b, axis=0, keepdims=True) for a, b in zip(sums, more)]
    sums = [a + fine_sums[n : n + 1] for n, a in enumerate(sums)]
    g_speed = 0.5 * jnp.sum(speed + more_speed, axis=0, keepdims=True)
    lam, mu, rinv = [row(mat_ref, n) for n in range(3)]
    wave = jnp.sqrt((lam + 2.0 * mu) * rinv)
    g_lam = sums[0] / (3.0 * lam + 2.0 * mu)
    g_mu = (sums[1] - lam * g_lam + sums[2]) / mu
    g_speed = g_speed / wave
    grad[...] = jnp.concatenate(
        [
            g_lam + 0.5 * g_speed * rinv,
            g_mu + g_speed * rinv,
            sums[3] / rinv + 0.5 * g_speed * (lam + 2.0 * mu),
        ],
        axis=0,
    )


def finish_kernel(final, grad, final_out, grad_out, sems):
    copies = [
        pltpu.make_async_copy(final, final_out, sems.at[0]),
        pltpu.make_async_copy(grad, grad_out, sems.at[1]),
    ]
    for copy in copies:
        copy.start()
    for copy in copies:
        copy.wait()


def body(
    start_state, material, geometry, clusters, neighbours, orientation,
    stiffness, face_trace, face_lift, face_turns, cotangent,
):
    rows, elems = start_state.shape
    basis = rows // VARS
    devices = lax.axis_size("dom")
    fb = up_to(face_trace.shape[1], 8)
    pitch = up_to(basis, 16)
    frows = up_to(VARS * fb + 8, 16)
    full, faces, slots = (rows, elems), (VARS * fb, 4 * elems), (SLOTS, up_to(frows, 128))
    args = (
        start_state, cotangent, material, geometry, clusters.reshape(1, elems), neighbours,
        orientation, stiffness, face_trace.transpose(1, 0, 2), face_lift.transpose(2, 0, 1),
        face_turns,
    )
    scratch = [x.shape for x in args[:4]] + [x.shape for x in args[7:]]
    scratch += [full] * 10
    scratch += [(STEPS * rows, elems)] + [(STEPS * rows, FINE_DEV)] * 2
    scratch += [faces] * 8 + [slots] * 8
    scratch += [(8 * TERMS, elems), (32, elems), (8 * STEPS, FINE_DEV), (8, FINE_DEV)]
    scratch += [(8, 4 * elems), (16, SLOTS)]
    scratch += [(3, pitch, pitch), (4, fb, pitch), (4, fb, pitch), (3, fb, fb)]
    packed = [(4 * pitch, 3 * pitch)] * 2 + [(4 * fb, 3 * pitch)] * 2
    packed += [(basis, 12 * fb)] * 2 + [(6 * fb, 6 * fb)] * 2
    packed += [(4 * elems, 4 * elems)] + [(SLOTS, 4 * elems)] * 2 + [(2 * FINE_DEV, elems)]
    packed += [(2 * frows, 4 * elems)] * 3
    args = [pltpu.with_memory_space_constraint(x, pltpu.HBM) for x in args]
    outs = pl.pallas_call(
        functools.partial(step_kernel, devices),
        out_shape=[
            jax.ShapeDtypeStruct((rows, elems), f32),
            jax.ShapeDtypeStruct((3, elems), f32),
        ],
        in_specs=[pl.BlockSpec(memory_space=pltpu.HBM)] * len(args),
        out_specs=[pl.BlockSpec(memory_space=pltpu.VMEM)] * 2,
        scratch_shapes=[pltpu.VMEM(s, f32) for s in scratch]
        + [pltpu.VMEM(s, bf16) for s in packed]
        + [pltpu.VMEM((1, elems), i32)]
        + [pltpu.VMEM((4, elems), i32)] * 3
        + [pltpu.SemaphoreType.DMA((len(args),))]
        + [pltpu.SemaphoreType.DMA((4 * LANES,))] * 2,
        compiler_params=pltpu.CompilerParams(
            vmem_limit_bytes=48 * 1024 * 1024, collective_id=0, has_side_effects=True
        ),
        name="ader_step",
    )(*args)
    return pl.pallas_call(
        finish_kernel,
        out_shape=[jax.ShapeDtypeStruct(x.shape, f32) for x in outs],
        in_specs=[pl.BlockSpec(memory_space=pltpu.VMEM)] * 2,
        out_specs=[pl.BlockSpec(memory_space=pl.ANY)] * 2,
        scratch_shapes=[pltpu.SemaphoreType.DMA((2,))],
        compiler_params=pltpu.CompilerParams(vmem_limit_bytes=2 * 1024 * 1024),
        name="finish",
    )(*outs)


def solution(mesh):
    return jax.shard_map(
        body,
        mesh=mesh,
        in_specs=(
            P(None, "dom"),
            P(None, "dom"),
            P(None, "dom"),
            P("dom"),
            P(None, "dom"),
            P(None, "dom"),
            P(),
            P(),
            P(),
            P(),
            P(None, "dom"),
        ),
        out_specs=(P(None, "dom"), P(None, "dom")),
        check_vma=False,
    )
```

```python
import functools

import jax
import jax.numpy as jnp
from jax import lax
from jax.experimental import pallas as pl
from jax.experimental.pallas import tpu as pltpu
from jax.sharding import PartitionSpec as P

VARS = 9
TERMS = 6
REACH = 4
CAP = 16
FINE_DEV = 128
LANES = 2 * REACH + 1
SLOTS = LANES * CAP
STEPS = TERMS - 1
f32, bf16, i32 = jnp.float32, jnp.bfloat16, jnp.int32

dt_step = 0.5
root_third = 0.5773502691896258
H = 0.5 * dt_step

A0 = H
STEP_SCALE = [H * H / 2.0] + [H / (k + 2.0) for k in range(1, STEPS)]
C_OVER_A = [2.0 ** (k + 1) - 1.0 for k in range(TERMS)]

NEED = [(0, 1), (1, 1), (2, 1), (0, 2), (1, 2), (2, 2), (0, 3), (0, 3), (0, 3)]
PAIRS = [((6, 7), 0, 3), ((8, 3), 0, 3), ((0, 1), 0, 2), ((4, 2), 1, 2), ((5,), 2, 2)]
READS = [
    {3: 7, 5: 8, 6: 0, 7: 3, 8: 5},
    {3: 6, 4: 8, 6: 3, 7: 1, 8: 4},
    {4: 7, 5: 6, 6: 5, 7: 4, 8: 2},
]


def up_to(n, m):
    return -(-n // m) * m


def halves(x):
    high = x.astype(bf16)
    return high, (x - high.astype(f32)).astype(bf16)


def padded(x, rows):
    if x.shape[0] == rows:
        return x
    return jnp.concatenate([x, jnp.zeros((rows - x.shape[0], x.shape[1]), f32)], axis=0)


def right3(x, rows):
    high, low = halves(padded(x, rows))
    return jnp.concatenate([high, high, low], axis=0)


def left3(a):
    high = a.astype(bf16).astype(f32)
    return jnp.concatenate([high, a - high, high], axis=1).astype(bf16)


def left2(a):
    high = a.astype(bf16).astype(f32)
    upper = jnp.concatenate([high, high], axis=1)
    lower = jnp.concatenate([a - high, jnp.zeros(a.shape, f32)], axis=1)
    return jnp.concatenate([upper, lower], axis=0).astype(bf16)


def apply2(mat, x):
    y = mm(mat[...], stack2(x, x.shape[0]))
    half = y.shape[0] // 2
    return y[:half] + y[half:]


def stack2(x, rows):
    return jnp.concatenate(halves(padded(x, rows)), axis=0)


def mm(a, b):
    return jnp.dot(a, b, preferred_element_type=f32)


def mm_t(a, b):
    return lax.dot_general(a, b, (((1,), (1,)), ((), ())), preferred_element_type=f32)


def add(*terms):
    total = None
    for t in terms:
        if t is not None:
            total = t if total is None else total + t
    return total


def blocks(ref, size, base=0):
    return [ref[base + v * size : base + (v + 1) * size, :] for v in range(VARS)]


def put(ref, values, base=0):
    size = values[0].shape[0]
    for v in range(VARS):
        ref[base + v * size : base + (v + 1) * size, :] = values[v]


def row(ref, n):
    return ref[n : n + 1, :]


class Mat:
    def __init__(self, con, base, geo):
        self.lam, self.mu2 = row(con, base), row(con, base + 1)
        self.mg = [row(con, base + 2 + a) for a in range(3)]
        self.rg = [row(con, base + 5 + a) for a in range(3)]
        self.g = [row(geo, a) for a in range(3)]


def forward_mix(p, m):
    t = [m.g[a] * p(6 + a, a) for a in range(3)]
    spread = m.lam * (t[0] + t[1] + t[2])
    return [
        spread + m.mu2 * t[0],
        spread + m.mu2 * t[1],
        spread + m.mu2 * t[2],
        m.mg[0] * p(7, 0) + m.mg[1] * p(6, 1),
        m.mg[1] * p(8, 1) + m.mg[2] * p(7, 2),
        m.mg[0] * p(8, 0) + m.mg[2] * p(6, 2),
        m.rg[0] * p(0, 0) + m.rg[1] * p(3, 1) + m.rg[2] * p(5, 2),
        m.rg[0] * p(3, 0) + m.rg[1] * p(1, 1) + m.rg[2] * p(4, 2),
        m.rg[0] * p(5, 0) + m.rg[1] * p(4, 1) + m.rg[2] * p(2, 2),
    ]


def normal_mix(r, m):
    u = m.lam * (r[0] + r[1] + r[2])
    return [u + m.mu2 * r[a] for a in range(3)] + list(r[3:])


def backward_mix(p, m):
    return [
        m.rg[0] * p(6, 0),
        m.rg[1] * p(7, 1),
        m.rg[2] * p(8, 2),
        m.rg[0] * p(7, 0) + m.rg[1] * p(6, 1),
        m.rg[1] * p(8, 1) + m.rg[2] * p(7, 2),
        m.rg[0] * p(8, 0) + m.rg[2] * p(6, 2),
        m.g[0] * p(0, 0) + m.mg[1] * p(3, 1) + m.mg[2] * p(5, 2),
        m.g[1] * p(1, 1) + m.mg[0] * p(3, 0) + m.mg[2] * p(4, 2),
        m.g[2] * p(2, 2) + m.mg[1] * p(4, 1) + m.mg[0] * p(5, 0),
    ]


def products(mat, values):
    size, width = values[0].shape
    pitch = mat.shape[2] // 3
    out = {}
    if width == FINE_DEV:
        groups = PAIRS
    else:
        groups = [((v,), s, c) for v, (s, c) in enumerate(NEED)]
    for names, start, count in groups:
        x = [values[v] for v in names]
        x = x[0] if len(x) == 1 else jnp.concatenate(x, axis=1)
        y = mm(mat[start, : count * size, :], right3(x, pitch))
        for n, v in enumerate(names):
            for i in range(count):
                out[v, (start + i) % 3] = y[
                    i * size : (i + 1) * size, n * width : (n + 1) * width
                ]
    return lambda v, axis: out[v, axis]


def apply_step(mat, values, m):
    return forward_mix(products(mat, values), m)


def apply_back(mat, values, m):
    return backward_mix(products(mat, normal_mix(values, m)), m)


def fold8(x):
    total = x[0:8]
    for n in range(8, x.shape[0], 8):
        total = total + x[n : n + 8]
    return total


def group_sums(r, x):
    mixed = (r[0] + r[1] + r[2]) * (x[0] + x[1] + x[2])
    groups = [add(*[r[v] * x[v] for v in range(g, g + 3)]) for g in (0, 3, 6)]
    return [fold8(g) for g in [mixed] + groups]


def plus(total, more):
    return more if total is None else [a + b for a, b in zip(total, more)]


def narrow(x, hot_c, rows):
    y = mm_t(stack2(x, rows), hot_c)
    return y[: x.shape[0]] + y[rows : rows + x.shape[0]]


def widen(x, hot_c2, rows):
    high, low = halves(padded(x, rows))
    return mm(jnp.concatenate([high, low], axis=1), hot_c2)[: x.shape[0]]


def trace_faces(tr, window, own, own_hl, fb, elems):
    size = window.shape[0] // VARS
    rows = own_hl.shape[0] // 2
    for v in range(VARS):
        t = mm(tr[...], right3(window[v * size : (v + 1) * size, :], tr.shape[1] // 3))
        for g in range(4):
            own[v * fb : (v + 1) * fb, g * elems : (g + 1) * elems] = t[g * fb : (g + 1) * fb]
    for g in range(4):
        cols = slice(g * elems, (g + 1) * elems)
        high, low = halves(padded(own[:, cols], rows))
        own_hl[:rows, cols] = high
        own_hl[rows:, cols] = low


def turn_blocks(mat, x, which):
    fb = x[0].shape[0]
    pick = [(w == 0, w == 1) for w in which]
    out = [None] * len(x)
    order = [f * VARS + v for f in range(len(which)) for v in range(VARS - 1)]
    order += [f * VARS + VARS - 1 for f in range(len(which))]
    for n in range(0, len(x), 2):
        names = order[n : n + 2]
        pair = [x[b] for b in names]
        y = mm(mat[...], right3(jnp.concatenate(pair, axis=0), 2 * fb))
        for i, b in enumerate(names):
            first, second = pick[b // VARS]
            part = [y[o * 2 * fb + i * fb : o * 2 * fb + (i + 1) * fb] for o in range(3)]
            out[b] = jnp.where(first, part[0], jnp.where(second, part[1], part[2]))
    return [out[n : n + VARS] for n in range(0, len(x), VARS)]


def split_rows(x, fb):
    return [x[v * fb : (v + 1) * fb] for v in range(VARS)]


def local_outer(own_hl, hot, turn, tn, out, fb, elems, faces):
    rows = own_hl.shape[0] // 2
    raw = []
    for f in faces:
        y = mm(own_hl[...], hot[:, f * elems : (f + 1) * elems])
        raw += split_rows(y[: VARS * fb] + y[rows : rows + VARS * fb], fb)
    turned = turn_blocks(tn, raw, [turn[f : f + 1, :] for f in faces])
    for f, x in zip(faces, turned):
        out[:, f * elems : (f + 1) * elems] = jnp.concatenate(x, axis=0)


def serve(hot_in, own_hl, tx):
    rows = own_hl.shape[0] // 2
    tx[:, :rows] = mm_t(hot_in[...], own_hl[:rows, :]) + mm_t(hot_in[...], own_hl[rows:, :])
    tx[:, rows:] = jnp.zeros((tx.shape[0], tx.shape[1] - rows), f32)


def flipped(rx):
    x = rx[...]
    return padded(x, up_to(x.shape[0], 128)).T[:, : x.shape[0]]


def face_rows(f, x, fc):
    if f == 3:
        return forward_mix(lambda v, axis: x[v], fc)
    axis = 2 - f
    kl, kp, _, km, kr = fc
    t = x[6 + axis]
    rows = [kl * t] * 3 + [None] * 6
    rows[axis] = kp * t
    for v, source in READS[axis].items():
        rows[v] = (km if v < 6 else kr) * x[source]
    return rows


def face_rows_back(f, r, fc):
    if f == 3:
        s = normal_mix(r, fc)
        return backward_mix(lambda v, axis: s[v], fc)
    axis = 2 - f
    kl, _, k2, km, kr = fc
    out = [None] * VARS
    out[6 + axis] = kl * (r[0] + r[1] + r[2]) + k2 * r[axis]
    for v, source in READS[axis].items():
        out[source] = (km if v < 6 else kr) * r[v]
    return out


def face_consts(f, fcon, con):
    if f == 3:
        m = Mat.__new__(Mat)
        m.lam, m.mu2 = row(fcon, 15), row(fcon, 16)
        m.mg = [row(fcon, 17 + a) for a in range(3)]
        m.rg = [row(fcon, 20 + a) for a in range(3)]
        m.g = [row(fcon, 23 + a) for a in range(3)]
        return m
    return [row(fcon, 5 * f + n) for n in range(5)]


def far_side(rx, slot_turn, tn, hot_slot, out_loc, fb):
    rows = up_to(VARS * fb, 16)
    turned = turn_blocks(tn, split_rows(flipped(rx), fb), [slot_turn[0:1, :]])[0]
    high_low = stack2(jnp.concatenate(turned, axis=0), rows)

    def far(f, elems):
        cols = slice(f * elems, (f + 1) * elems)
        y = mm(high_low, hot_slot[:, cols])
        return out_loc[:, cols] + (y[: VARS * fb] + y[rows : rows + VARS * fb])

    return far


def surface(lf, own, far, fcon, con, fb, elems, jump_ref, flux_ref):
    half_speed = row(fcon, 26)
    fluxes = [[] for _ in range(VARS)]
    for f in range(4):
        cols = slice(f * elems, (f + 1) * elems)
        a, b = split_rows(own[:, cols], fb), split_rows(far(f, elems), fb)
        rows = face_rows(f, [x + y for x, y in zip(a, b)], face_consts(f, fcon, con))
        for v in range(VARS):
            jump = a[v] - b[v]
            flux = add(half_speed * jump, rows[v])
            jump_ref[v * fb : (v + 1) * fb, cols] = jump
            flux_ref[v * fb : (v + 1) * fb, cols] = flux
            fluxes[v].append(flux)
    return [apply2(lf, jnp.concatenate(x, axis=0)) for x in fluxes]


def face_sums(lifted, jump_ref, flux_ref, half_speed, fb, elems):
    total, speed = None, None
    for f in range(4):
        cols = slice(f * elems, (f + 1) * elems)
        r, d, x = [split_rows(ref[:, cols], fb) for ref in (lifted, jump_ref, flux_ref)]
        of_jump, of_flux = group_sums(r, d), group_sums(r, x)
        total = plus(total, [a - half_speed * b for a, b in zip(of_flux, of_jump)])
        more = of_jump[1] + of_jump[2] + of_jump[3]
        speed = more if speed is None else speed + more
    return total, speed


def faces_cot(seed, lt, tnt, turn, extra, fcon, con, lifted, own_cot, x_hl, fb, elems):
    half_speed = row(fcon, 26)
    rows = x_hl.shape[0] // 2
    for v in range(VARS):
        y = mm(lt[...], right3(seed[v], lt.shape[1] // 3))
        for f in range(4):
            lifted[v * fb : (v + 1) * fb, f * elems : (f + 1) * elems] = y[f * fb : (f + 1) * fb]
    for faces in ((0, 1), (2, 3)):
        x = []
        for f in faces:
            cols = slice(f * elems, (f + 1) * elems)
            r = split_rows(lifted[:, cols], fb)
            back = face_rows_back(f, r, face_consts(f, fcon, con))
            for v in range(VARS):
                side = half_speed * r[v]
                own_cot[v * fb : (v + 1) * fb, cols] = add(side, back[v])
                x.append(-side if back[v] is None else back[v] - side)
        turned = turn_blocks(tnt, x, [turn[f : f + 1, :] for f in faces])
        for f, y in zip(faces, turned):
            cols = slice(f * elems, (f + 1) * elems)
            if extra is not None:
                y.append(extra[:, cols])
            high, low = halves(padded(jnp.concatenate(y, axis=0), rows))
            x_hl[:rows, cols] = high
            x_hl[rows:, cols] = low


def scatter_local(own_cot, x_hl, hot, fb, elems, g):
    rows = x_hl.shape[0] // 2
    cols = slice(g * elems, (g + 1) * elems)
    y = mm_t(x_hl[...], hot[cols, :])
    own_cot[:, cols] = own_cot[:, cols] + (y[: VARS * fb] + y[rows : rows + VARS * fb])


def faces_back(own_cot, rx, hot_in, trt, fb, elems):
    rows = up_to(VARS * fb, 16)
    arrived = stack2(flipped(rx)[: VARS * fb], rows)
    for g in range(4):
        cols = slice(g * elems, (g + 1) * elems)
        y = mm(arrived, hot_in[:, cols])
        own_cot[:, cols] = own_cot[:, cols] + (y[: VARS * fb] + y[rows : rows + VARS * fb])
    out = []
    for v in range(VARS):
        x = [own_cot[v * fb : (v + 1) * fb, g * elems : (g + 1) * elems] for g in range(4)]
        out.append(apply2(trt, jnp.concatenate(x, axis=0)))
    return out


def weave(steps, pieces):
    done = 0
    for n, step in enumerate(steps):
        step()
        until = (n + 1) * len(pieces) // len(steps)
        for piece in pieces[done:until]:
            piece()
        done = until


def peers_of(devices):
    me = lax.axis_index("dom")
    shifts = [n + 1 for n in range(REACH)] + [-(n + 1) for n in range(REACH)] + [devices // 2]
    return [
        [lax.rem(me + sign * s + 2 * devices, devices) for s in shifts] for sign in (1, -1)
    ]


def send_all(peers, src, dst, send_sems, recv_sems, base=0):
    copies = []
    for n in reversed(range(LANES)):
        rows = pl.ds(n * CAP, CAP)
        copy = pltpu.make_async_remote_copy(
            src_ref=src.at[rows],
            dst_ref=dst.at[rows],
            send_sem=send_sems.at[base + n],
            recv_sem=recv_sems.at[base + n],
            device_id=(peers[n],),
            device_id_type=pl.DeviceIdType.MESH,
        )
        copy.start()
        copies.append(copy)
    return copies


def one_hot(mask):
    return jnp.where(mask, 1.0, 0.0).astype(bf16)


def face_places(
    devices, neighbours, orientation, fine, hot, hot_slot, hot_c, turn, slot_turn, extra
):
    elems = neighbours.shape[1]
    me = lax.axis_index("dom")
    at = lax.broadcasted_iota(i32, (16, elems), 0)
    square = (elems, elems)
    at_n, at_e = lax.broadcasted_iota(i32, square, 0), lax.broadcasted_iota(i32, square, 1)
    at_s = lax.broadcasted_iota(i32, (SLOTS, elems), 0)
    at_8 = lax.broadcasted_iota(i32, (8, elems), 0)
    earlier = one_hot(at_n <= at_e)
    lanes, marks, keys = [], [], []
    for f in range(4):
        cols = slice(f * elems, (f + 1) * elems)
        name, code = neighbours[f : f + 1, :], orientation[f : f + 1, :]
        far_face = sum(jnp.where(code >= 3 * g, 1, 0) for g in (1, 2, 3))
        turn[f : f + 1, :] = code - 3 * far_face
        present = name >= 0
        safe = jnp.maximum(name, 0)
        owner = jnp.floor((safe.astype(f32) + 0.5) * (1.0 / elems)).astype(i32)
        index = safe - owner * elems
        away = owner - me
        away = jnp.where(away < 0, away + devices, away)
        keys.append((cols, present & (away == 0), far_face, index))
        lane = jnp.where(
            away <= REACH,
            away - 1,
            jnp.where(away >= devices - REACH, REACH + devices - away - 1, 2 * REACH),
        )
        lane = jnp.where(present & (away != 0), lane, LANES)
        lanes.append(lane)
        marks.append(jnp.where(at == lane, 1.0, 0.0))
        index_f, face_f = index.astype(f32), far_face.astype(f32)
        extra[:, cols] = jnp.where(
            at_8 == 0, index_f, jnp.where(at_8 == 1, face_f, jnp.where(at_8 == 2, 1.0, 0.0))
        )
    is_fine = fine[...] == 1
    marks.append(jnp.where((at == 0) & is_fine, 1.0, 0.0))
    run = mm(jnp.concatenate(marks, axis=0).astype(bf16), earlier)
    carry = jnp.zeros((16, 1), f32)
    for f in range(4):
        cols = slice(f * elems, (f + 1) * elems)
        mine = run[16 * f : 16 * f + 16]
        rank = jnp.sum((mine + carry - 1.0) * marks[f], axis=0, keepdims=True).astype(i32)
        carry = carry + mine[:, elems - 1 :]
        slot = jnp.where(lanes[f] < LANES, lanes[f] * CAP + rank, -1)
        hot_slot[:, cols] = one_hot(at_s == slot)
    rank = jnp.where(is_fine, run[64:65].astype(i32) - 1, -1)
    picked = one_hot(lax.broadcasted_iota(i32, (FINE_DEV, elems), 0) == rank)
    hot_c[:FINE_DEV, :] = picked
    hot_c[FINE_DEV:, :] = picked
    turns = jnp.concatenate([turn[f : f + 1, :].astype(f32) for f in range(4)], axis=1)
    turns = jnp.broadcast_to(turns, (16, 4 * elems)).astype(bf16)
    slot_turn[...] = mm_t(turns, hot_slot[...])

    def fill(cols, local, far_face, index):
        names = at_n.astype(f32).astype(bf16)
        for g in range(4):
            key = jnp.where(local & (far_face == g), index, -1).astype(f32).astype(bf16)
            hot[g * elems : (g + 1) * elems, cols] = jnp.where(
                names == key, jnp.ones(square, bf16), jnp.zeros(square, bf16)
            )

    return [functools.partial(fill, *key) for key in keys]


def constants(mat_ref, geo_ref, con, fcon):
    lam, mu, rinv = [row(mat_ref, n) for n in range(3)]
    geo = [row(geo_ref, n) for n in range(3)]
    rows = [lam, 2.0 * mu] + [mu * g for g in geo] + [rinv * g for g in geo]
    base = jnp.concatenate(rows, axis=0)
    for n, scale in enumerate([-1.0] + STEP_SCALE):
        con[8 * n : 8 * n + 8, :] = scale * base
    rows = []
    for f in range(3):
        h = 0.5 * geo[2 - f]
        rows += [lam * h, (lam + 2.0 * mu) * h, 2.0 * mu * h, mu * h, rinv * h]
    h = [(-0.5 * root_third) * g for g in geo]
    rows += [lam, 2.0 * mu] + [mu * x for x in h] + [rinv * x for x in h] + h
    rows += [0.5 * jnp.sqrt((lam + 2.0 * mu) * rinv)]
    for n, x in enumerate(rows):
        fcon[n : n + 1, :] = x


def pitched(pad, matrices):
    pad[...] = jnp.zeros(pad.shape, f32)
    for n, x in enumerate(matrices):
        pad[n, : x.shape[0], : x.shape[1]] = x
    return [pad[n] for n in range(len(matrices))]


def turn_matrix(pad, matrices):
    zero = jnp.zeros(pad.shape[1:], f32)
    out = []
    for x in pitched(pad, matrices):
        out += [jnp.concatenate([x, zero], axis=1), jnp.concatenate([zero, x], axis=1)]
    return left3(jnp.concatenate(out, axis=0))


def step_kernel(
    devices,
    state_in, cot_in, mat_in, geo_in, fine_in, neighbours_in, orientation_in, stiffness_in,
    trace_in, lift_in, turns_in,
    final, grad,
    state, cot, mat_ref, geo_ref, stiffness, face_trace, face_lift, face_turns,
    w1, wc, w2, coarse, seed1, middle, vol1, vol2, cur, direct2,
    q1, q2, hist,
    own, lifted1, lifted2, out_loc, own_cot1, own_cot2, jump, flux,
    tx0, tx1, tx2, tx3, rx0, rx1, rx2, rx3,
    con, fcon, con_f, geo_f, extra, slot_turn,
    k_pad, t_pad, l_pad, n_pad,
    ks, kt, tr, lt, trt, lf, tn, tnt, hot, hot_slot, hot_in, hot_c, own_hl, x_hl1, x_hl2,
    fine, neighbours, orientation, turn, load_sems, send_sems, recv_sems,
):
    loads = [
        pltpu.make_async_copy(src, dst, load_sems.at[n])
        for n, (src, dst) in enumerate([
            (neighbours_in, neighbours), (orientation_in, orientation), (mat_in, mat_ref),
            (geo_in, geo_ref), (fine_in, fine), (stiffness_in, stiffness),
            (trace_in, face_trace), (lift_in, face_lift), (turns_in, face_turns),
            (cot_in, cot), (state_in, state),
        ])
    ]
    for load in loads:
        load.start()
    up, down = peers_of(devices)
    barrier = pltpu.get_barrier_semaphore()
    for peer in up:
        pl.semaphore_signal(
            barrier, inc=1, device_id=(peer,), device_id_type=pl.DeviceIdType.MESH
        )
    elems = state.shape[1]
    count = state.shape[0]
    size = count // VARS
    fb = t_pad.shape[1]
    wide = up_to(count, 16)
    part = functools.partial

    for load in loads[:9]:
        load.wait()
    constants(mat_ref, geo_ref, con, fcon)
    trace = jnp.concatenate(pitched(t_pad, [face_trace[:, g, :] for g in range(4)]), axis=0)
    tr[...] = left3(trace)
    trt[...] = left2(trace.T[:size])
    lift = jnp.concatenate(pitched(l_pad, [-face_lift[:, f, :] for f in range(4)]), axis=0)
    lt[...] = left3(lift)
    lf[...] = left2(lift.T[:size])
    turns = [face_turns[o] for o in range(3)]
    tn[...] = turn_matrix(n_pad, turns)
    tnt[...] = turn_matrix(n_pad, [x.T for x in turns])
    hot_fills = face_places(
        devices, neighbours, orientation, fine, hot, hot_slot, hot_c, turn, slot_turn, extra
    )
    base, half_speed = Mat(con, 0, geo_ref), row(fcon, 26)

    loads[9].wait()
    seed2 = blocks(cot, size)
    faces_cot(seed2, lt, tnt, turn, extra, fcon, con, lifted2, own_cot2, x_hl2, fb, elems)
    serve(hot_slot, x_hl2, tx0)

    def scatter(own_cot, x_hl):
        return [part(scatter_local, own_cot, x_hl, hot, fb, elems, g) for g in range(4)]

    for piece in hot_fills + scatter(own_cot2, x_hl2):
        piece()
    pl.semaphore_wait(barrier, LANES)
    sent0 = send_all(up, tx0, rx0, send_sems, recv_sems, 0)

    stiff = pitched(k_pad, [stiffness[d] for d in range(3)])
    for mat, axes in ((ks, stiff), (kt, [x.T for x in stiff])):
        for n in range(3):
            order = [axes[(n + i) % 3][:size] for i in range(3)]
            mat[n] = left3(jnp.concatenate(order, axis=0))
    is_fine = fine[...] == 1
    loads[10].wait()

    def step1(k):
        old = blocks(state, size) if k == 0 else blocks(q1, size, (k - 1) * count)
        put(q1, apply_step(ks, old, Mat(con, 8 * (k + 1), geo_ref)), k * count)

    def gather():
        return [
            part(local_outer, own_hl, hot, turn, tn, out_loc, fb, elems, faces)
            for faces in ((0, 1), (2, 3))
        ]

    def volume(out, window):
        put(out, apply_step(kt, blocks(window, size), base))

    for k in range(STEPS):
        step1(k)
    for v in range(VARS):
        rows = slice(v * size, (v + 1) * size)
        terms = [A0 * state[rows, :]]
        terms += [q1[k * count + v * size : k * count + (v + 1) * size, :] for k in range(STEPS)]
        w1[rows, :] = add(*terms)
        later = add(*[c * t if c != 1.0 else t for c, t in zip(C_OVER_A, terms)])
        wc[rows, :] = jnp.where(is_fine, 0.0, later)
    trace_faces(tr, w1, own, own_hl, fb, elems)
    for piece in gather():
        piece()
    put(direct2, apply_back(ks, seed2, base))
    for copy in sent0:
        copy.wait()

    key = rx0[:, VARS * fb : VARS * fb + 3]
    key = jnp.where(key[:, 2:3] > 0.5, key[:, 1:2] * float(elems) + key[:, 0:1], -1.0)
    at = lax.broadcasted_iota(i32, (SLOTS, 4 * elems), 1)
    hot_in[...] = one_hot(at == key.astype(i32))
    serve(hot_in, own_hl, tx1)
    sent1 = send_all(down, tx1, rx1, send_sems, recv_sems, LANES)

    back = faces_back(own_cot2, rx0, hot_in, trt, fb, elems)
    back = [a + b for a, b in zip(back, blocks(direct2, size))]
    put(coarse, [jnp.where(is_fine, 0.0, x) for x in back])
    seeds = split_rows(narrow(jnp.concatenate(back, axis=0), hot_c[:FINE_DEV, :], wide), size)
    put(hist, seeds, (STEPS - 1) * count)
    narrow_con = mm_t(
        jnp.concatenate(
            halves(con[0:16, :]) + halves(padded(geo_ref[...], 16)), axis=0
        ),
        hot_c[:FINE_DEV, :],
    )
    geo_f[...] = narrow_con[32:40] + narrow_con[48:56]
    for n, scale in enumerate(STEP_SCALE):
        con_f[8 * n : 8 * n + 8, :] = -scale * (narrow_con[0:8] + narrow_con[16:24])

    def back2(k):
        r = apply_back(kt, blocks(hist, size, k * count), Mat(con_f, 8 * k, geo_f))
        scale = A0 if k == 0 else 1.0
        direct = blocks(hist, size, (STEPS - 1) * count)
        r = [a + (b if k else scale * b) for a, b in zip(r, direct)]
        if k:
            put(hist, r, (k - 1) * count)
        else:
            seed1[...] = widen(jnp.concatenate(r, axis=0), hot_c[...], wide) + cot[...]

    for k in range(STEPS - 1, -1, -1):
        back2(k)
    faces_cot(
        blocks(seed1, size), lt, tnt, turn, None, fcon, con, lifted1, own_cot1, x_hl1, fb, elems
    )
    serve(hot_slot, x_hl1, tx3)
    sent3 = send_all(up, tx3, rx3, send_sems, recv_sems, 2 * LANES)
    for piece in scatter(own_cot1, x_hl1):
        piece()
    put(cur, apply_back(ks, blocks(seed1, size), base))
    volume(vol1, w1)
    for copy in sent1:
        copy.wait()

    far = far_side(rx1, slot_turn, tn, hot_slot, out_loc, fb)
    change = surface(lf, own, far, fcon, con, fb, elems, jump, flux)
    put(middle, [
        s + m + c for s, m, c in zip(blocks(state, size), blocks(vol1, size), change)
    ])
    start = split_rows(narrow(middle[...], hot_c[:FINE_DEV, :], wide), size)
    first = [A0 * x for x in start]

    def step2(k):
        old = start if k == 0 else blocks(q2, size, (k - 1) * count)
        put(q2, apply_step(ks, old, Mat(con_f, 8 * k, geo_f)), k * count)

    for k in range(STEPS):
        step2(k)
    window = [
        add(first[v], *[
            q2[k * count + v * size : k * count + (v + 1) * size, :] for k in range(STEPS)
        ])
        for v in range(VARS)
    ]
    w2[...] = widen(jnp.concatenate(window, axis=0), hot_c[...], wide) + wc[...]
    trace_faces(tr, w2, own, own_hl, fb, elems)
    serve(hot_in, own_hl, tx2)
    sent2 = send_all(down, tx2, rx2, send_sems, recv_sems, 3 * LANES)

    sums, speed = face_sums(lifted1, jump, flux, half_speed, fb, elems)
    sums = plus(sums, group_sums(blocks(seed1, size), blocks(vol1, size)))
    fine_sums = None
    for k in range(STEPS):
        fine_sums = plus(
            fine_sums, group_sums(blocks(hist, size, k * count), blocks(q2, size, k * count))
        )
    fine_sums = [jnp.sum(x, axis=0, keepdims=True) for x in fine_sums]
    fine_sums = widen(jnp.concatenate(fine_sums + fine_sums, axis=0), hot_c[...], 16)
    for copy in sent3:
        copy.wait()
    back = faces_back(own_cot1, rx3, hot_in, trt, fb, elems)
    put(seed1, [a + b for a, b in zip(back, blocks(cur, size))])
    chain = [sums]

    def back1(k):
        r = [a + C_OVER_A[k] * b for a, b in zip(blocks(seed1, size), blocks(coarse, size))]
        if k < STEPS:
            old = blocks(cur, size)
            r = [a + b for a, b in zip(r, apply_back(kt, old, Mat(con, 8 * (k + 1), geo_ref)))]
        put(cur, r)
        chain[0] = plus(
            chain[0], group_sums(blocks(cur, size), blocks(q1, size, (k - 1) * count))
        )

    weave([part(back1, k) for k in range(STEPS, 0, -1)], gather() + [part(volume, vol2, w2)])
    sums = plus(chain[0], group_sums(seed2, blocks(vol2, size)))
    for copy in sent2:
        copy.wait()

    far = far_side(rx2, slot_turn, tn, hot_slot, out_loc, fb)
    change = surface(lf, own, far, fcon, con, fb, elems, jump, flux)
    put(final, [
        s + m + c for s, m, c in zip(blocks(middle, size), blocks(vol2, size), change)
    ])
    more, more_speed = face_sums(lifted2, jump, flux, half_speed, fb, elems)
    sums = [jnp.sum(a + b, axis=0, keepdims=True) for a, b in zip(sums, more)]
    sums = [a + fine_sums[n : n + 1] for n, a in enumerate(sums)]
    g_speed = 0.5 * jnp.sum(speed + more_speed, axis=0, keepdims=True)
    lam, mu, rinv = [row(mat_ref, n) for n in range(3)]
    wave = jnp.sqrt((lam + 2.0 * mu) * rinv)
    g_lam = sums[0] / (3.0 * lam + 2.0 * mu)
    g_mu = (sums[1] - lam * g_lam + sums[2]) / mu
    g_speed = g_speed / wave
    grad[...] = jnp.concatenate(
        [
            g_lam + 0.5 * g_speed * rinv,
            g_mu + g_speed * rinv,
            sums[3] / rinv + 0.5 * g_speed * (lam + 2.0 * mu),
        ],
        axis=0,
    )


def finish_kernel(final, grad, final_out, grad_out, sems):
    copies = [
        pltpu.make_async_copy(final, final_out, sems.at[0]),
        pltpu.make_async_copy(grad, grad_out, sems.at[1]),
    ]
    for copy in copies:
        copy.start()
    for copy in copies:
        copy.wait()


def body(
    start_state, material, geometry, clusters, neighbours, orientation,
    stiffness, face_trace, face_lift, face_turns, cotangent,
):
    rows, elems = start_state.shape
    basis = rows // VARS
    devices = lax.axis_size("dom")
    fb = up_to(face_trace.shape[1], 8)
    pitch = up_to(basis, 16)
    frows = up_to(VARS * fb + 8, 16)
    full, faces, slots = (rows, elems), (VARS * fb, 4 * elems), (SLOTS, up_to(frows, 128))
    args = (
        start_state, cotangent, material, geometry, clusters.reshape(1, elems), neighbours,
        orientation, stiffness, face_trace.transpose(1, 0, 2), face_lift.transpose(2, 0, 1),
        face_turns,
    )
    scratch = [x.shape for x in args[:4]] + [x.shape for x in args[7:]]
    scratch += [full] * 10
    scratch += [(STEPS * rows, elems)] + [(STEPS * rows, FINE_DEV)] * 2
    scratch += [faces] * 8 + [slots] * 8
    scratch += [(8 * TERMS, elems), (32, elems), (8 * STEPS, FINE_DEV), (8, FINE_DEV)]
    scratch += [(8, 4 * elems), (16, SLOTS)]
    scratch += [(3, pitch, pitch), (4, fb, pitch), (4, fb, pitch), (3, fb, fb)]
    packed = [(3, 3 * basis, 3 * pitch)] * 2 + [(4 * fb, 3 * pitch)] * 2
    packed += [(2 * basis, 8 * fb)] * 2 + [(6 * fb, 6 * fb)] * 2
    packed += [(4 * elems, 4 * elems)] + [(SLOTS, 4 * elems)] * 2 + [(2 * FINE_DEV, elems)]
    packed += [(2 * frows, 4 * elems)] * 3
    args = [pltpu.with_memory_space_constraint(x, pltpu.HBM) for x in args]
    outs = pl.pallas_call(
        functools.partial(step_kernel, devices),
        out_shape=[
            jax.ShapeDtypeStruct((rows, elems), f32),
            jax.ShapeDtypeStruct((3, elems), f32),
        ],
        in_specs=[pl.BlockSpec(memory_space=pltpu.HBM)] * len(args),
        out_specs=[pl.BlockSpec(memory_space=pltpu.VMEM)] * 2,
        scratch_shapes=[pltpu.VMEM(s, f32) for s in scratch]
        + [pltpu.VMEM(s, bf16) for s in packed]
        + [pltpu.VMEM((1, elems), i32)]
        + [pltpu.VMEM((4, elems), i32)] * 3
        + [pltpu.SemaphoreType.DMA((len(args),))]
        + [pltpu.SemaphoreType.DMA((4 * LANES,))] * 2,
        compiler_params=pltpu.CompilerParams(
            vmem_limit_bytes=48 * 1024 * 1024, collective_id=0, has_side_effects=True
        ),
        name="ader_step",
    )(*args)
    return pl.pallas_call(
        finish_kernel,
        out_shape=[jax.ShapeDtypeStruct(x.shape, f32) for x in outs],
        in_specs=[pl.BlockSpec(memory_space=pltpu.VMEM)] * 2,
        out_specs=[pl.BlockSpec(memory_space=pl.ANY)] * 2,
        scratch_shapes=[pltpu.SemaphoreType.DMA((2,))],
        compiler_params=pltpu.CompilerParams(vmem_limit_bytes=2 * 1024 * 1024),
        name="finish",
    )(*outs)


def solution(mesh):
    return jax.shard_map(
        body,
        mesh=mesh,
        in_specs=(
            P(None, "dom"),
            P(None, "dom"),
            P(None, "dom"),
            P("dom"),
            P(None, "dom"),
            P(None, "dom"),
            P(),
            P(),
            P(),
            P(),
            P(None, "dom"),
        ),
        out_specs=(P(None, "dom"), P(None, "dom")),
        check_vma=False,
    )
```

```python
import functools

import jax
import jax.numpy as jnp
from jax import lax
from jax.experimental import pallas as pl
from jax.experimental.pallas import tpu as pltpu
from jax.sharding import PartitionSpec as P

VARS = 9
TERMS = 6
REACH = 4
CAP = 16
FINE_DEV = 128
LANES = 2 * REACH + 1
SLOTS = LANES * CAP
STEPS = TERMS - 1
f32, bf16, i32 = jnp.float32, jnp.bfloat16, jnp.int32

dt_step = 0.5
root_third = 0.5773502691896258
H = 0.5 * dt_step

A0 = H
STEP_SCALE = [H * H / 2.0] + [H / (k + 2.0) for k in range(1, STEPS)]
C_OVER_A = [2.0 ** (k + 1) - 1.0 for k in range(TERMS)]

NEED = [(0, 1), (1, 1), (2, 1), (0, 2), (1, 2), (2, 2), (0, 3), (0, 3), (0, 3)]
PAIRS = [((6, 7), 0, 3), ((8, 3), 0, 3), ((0, 1), 0, 2), ((4, 2), 1, 2), ((5,), 2, 2)]
READS = [
    {3: 7, 5: 8, 6: 0, 7: 3, 8: 5},
    {3: 6, 4: 8, 6: 3, 7: 1, 8: 4},
    {4: 7, 5: 6, 6: 5, 7: 4, 8: 2},
]


def up_to(n, m):
    return -(-n // m) * m


def halves(x):
    high = x.astype(bf16)
    return high, (x - high.astype(f32)).astype(bf16)


def padded(x, rows):
    if x.shape[0] == rows:
        return x
    return jnp.concatenate([x, jnp.zeros((rows - x.shape[0], x.shape[1]), f32)], axis=0)


def right3(x, rows):
    high, low = halves(padded(x, rows))
    return jnp.concatenate([high, high, low], axis=0)


def left3(a):
    high = a.astype(bf16).astype(f32)
    return jnp.concatenate([high, a - high, high], axis=1).astype(bf16)


def left2(a):
    high = a.astype(bf16).astype(f32)
    upper = jnp.concatenate([high, high], axis=1)
    lower = jnp.concatenate([a - high, jnp.zeros(a.shape, f32)], axis=1)
    return jnp.concatenate([upper, lower], axis=0).astype(bf16)


def apply2(mat, x):
    y = mm(mat[...], stack2(x, x.shape[0]))
    half = y.shape[0] // 2
    return y[:half] + y[half:]


def stack2(x, rows):
    return jnp.concatenate(halves(padded(x, rows)), axis=0)


def mm(a, b):
    return jnp.dot(a, b, preferred_element_type=f32)


def mm_t(a, b):
    return lax.dot_general(a, b, (((1,), (1,)), ((), ())), preferred_element_type=f32)


def add(*terms):
    total = None
    for t in terms:
        if t is not None:
            total = t if total is None else total + t
    return total


def blocks(ref, size, base=0):
    return [ref[base + v * size : base + (v + 1) * size, :] for v in range(VARS)]


def put(ref, values, base=0):
    size = values[0].shape[0]
    for v in range(VARS):
        ref[base + v * size : base + (v + 1) * size, :] = values[v]


def row(ref, n):
    return ref[n : n + 1, :]


class Mat:
    def __init__(self, con, base, geo):
        self.lam, self.mu2 = row(con, base), row(con, base + 1)
        self.mg = [row(con, base + 2 + a) for a in range(3)]
        self.rg = [row(con, base + 5 + a) for a in range(3)]
        self.g = [row(geo, a) for a in range(3)]


def forward_mix(p, m):
    t = [m.g[a] * p(6 + a, a) for a in range(3)]
    spread = m.lam * (t[0] + t[1] + t[2])
    return [
        spread + m.mu2 * t[0],
        spread + m.mu2 * t[1],
        spread + m.mu2 * t[2],
        m.mg[0] * p(7, 0) + m.mg[1] * p(6, 1),
        m.mg[1] * p(8, 1) + m.mg[2] * p(7, 2),
        m.mg[0] * p(8, 0) + m.mg[2] * p(6, 2),
        m.rg[0] * p(0, 0) + m.rg[1] * p(3, 1) + m.rg[2] * p(5, 2),
        m.rg[0] * p(3, 0) + m.rg[1] * p(1, 1) + m.rg[2] * p(4, 2),
        m.rg[0] * p(5, 0) + m.rg[1] * p(4, 1) + m.rg[2] * p(2, 2),
    ]


def normal_mix(r, m):
    u = m.lam * (r[0] + r[1] + r[2])
    return [u + m.mu2 * r[a] for a in range(3)] + list(r[3:])


def backward_mix(p, m):
    return [
        m.rg[0] * p(6, 0),
        m.rg[1] * p(7, 1),
        m.rg[2] * p(8, 2),
        m.rg[0] * p(7, 0) + m.rg[1] * p(6, 1),
        m.rg[1] * p(8, 1) + m.rg[2] * p(7, 2),
        m.rg[0] * p(8, 0) + m.rg[2] * p(6, 2),
        m.g[0] * p(0, 0) + m.mg[1] * p(3, 1) + m.mg[2] * p(5, 2),
        m.g[1] * p(1, 1) + m.mg[0] * p(3, 0) + m.mg[2] * p(4, 2),
        m.g[2] * p(2, 2) + m.mg[1] * p(4, 1) + m.mg[0] * p(5, 0),
    ]


def products(mat, values):
    size, width = values[0].shape
    pitch = mat.shape[2] // 3
    out = {}
    if width == FINE_DEV:
        groups = PAIRS
    else:
        groups = [((v,), s, c) for v, (s, c) in enumerate(NEED)]
    for names, start, count in groups:
        x = [values[v] for v in names]
        x = x[0] if len(x) == 1 else jnp.concatenate(x, axis=1)
        y = mm(mat[start, : count * size, :], right3(x, pitch))
        for n, v in enumerate(names):
            for i in range(count):
                out[v, (start + i) % 3] = y[
                    i * size : (i + 1) * size, n * width : (n + 1) * width
                ]
    return lambda v, axis: out[v, axis]


def apply_step(mat, values, m):
    return forward_mix(products(mat, values), m)


def apply_back(mat, values, m):
    return backward_mix(products(mat, normal_mix(values, m)), m)


def fold8(x):
    total = x[0:8]
    for n in range(8, x.shape[0], 8):
        total = total + x[n : n + 8]
    return total


def group_sums(r, x):
    mixed = (r[0] + r[1] + r[2]) * (x[0] + x[1] + x[2])
    groups = [add(*[r[v] * x[v] for v in range(g, g + 3)]) for g in (0, 3, 6)]
    return [fold8(g) for g in [mixed] + groups]


def plus(total, more):
    return more if total is None else [a + b for a, b in zip(total, more)]


def narrow(x, hot_c, rows):
    y = mm_t(stack2(x, rows), hot_c)
    return y[: x.shape[0]] + y[rows : rows + x.shape[0]]


def widen(x, hot_c2, rows):
    high, low = halves(padded(x, rows))
    return mm(jnp.concatenate([high, low], axis=1), hot_c2)[: x.shape[0]]


def trace_faces(tr, window, own, own_hl, fb, elems):
    size = window.shape[0] // VARS
    rows = own_hl.shape[0] // 2
    for v in range(VARS):
        t = mm(tr[...], right3(window[v * size : (v + 1) * size, :], tr.shape[1] // 3))
        for g in range(4):
            own[v * fb : (v + 1) * fb, g * elems : (g + 1) * elems] = t[g * fb : (g + 1) * fb]
    for g in range(4):
        cols = slice(g * elems, (g + 1) * elems)
        high, low = halves(padded(own[:, cols], rows))
        own_hl[:rows, cols] = high
        own_hl[rows:, cols] = low


def turn_blocks(mat, x, which):
    fb = x[0].shape[0]
    pick = [(w == 0, w == 1) for w in which]
    out = [None] * len(x)
    order = [f * VARS + v for f in range(len(which)) for v in range(VARS - 1)]
    order += [f * VARS + VARS - 1 for f in range(len(which))]
    for n in range(0, len(x), 2):
        names = order[n : n + 2]
        pair = [x[b] for b in names]
        y = mm(mat[...], right3(jnp.concatenate(pair, axis=0), 2 * fb))
        for i, b in enumerate(names):
            first, second = pick[b // VARS]
            part = [y[o * 2 * fb + i * fb : o * 2 * fb + (i + 1) * fb] for o in range(3)]
            out[b] = jnp.where(first, part[0], jnp.where(second, part[1], part[2]))
    return [out[n : n + VARS] for n in range(0, len(x), VARS)]


def split_rows(x, fb):
    return [x[v * fb : (v + 1) * fb] for v in range(VARS)]


def local_outer(own_hl, hot, turn, tn, out, fb, elems, faces):
    rows = own_hl.shape[0] // 2
    raw = []
    for f in faces:
        y = mm(own_hl[...], hot[:, f * elems : (f + 1) * elems])
        raw += split_rows(y[: VARS * fb] + y[rows : rows + VARS * fb], fb)
    turned = turn_blocks(tn, raw, [turn[f : f + 1, :] for f in faces])
    for f, x in zip(faces, turned):
        out[:, f * elems : (f + 1) * elems] = jnp.concatenate(x, axis=0)


def serve(hot_in, own_hl, tx):
    rows = own_hl.shape[0] // 2
    tx[:, :rows] = mm_t(hot_in[...], own_hl[:rows, :]) + mm_t(hot_in[...], own_hl[rows:, :])
    tx[:, rows:] = jnp.zeros((tx.shape[0], tx.shape[1] - rows), f32)


def flipped(rx):
    x = rx[...]
    return padded(x, up_to(x.shape[0], 128)).T[:, : x.shape[0]]


def face_rows(f, x, fc):
    if f == 3:
        return forward_mix(lambda v, axis: x[v], fc)
    axis = 2 - f
    kl, kp, _, km, kr = fc
    t = x[6 + axis]
    rows = [kl * t] * 3 + [None] * 6
    rows[axis] = kp * t
    for v, source in READS[axis].items():
        rows[v] = (km if v < 6 else kr) * x[source]
    return rows


def face_rows_back(f, r, fc):
    if f == 3:
        s = normal_mix(r, fc)
        return backward_mix(lambda v, axis: s[v], fc)
    axis = 2 - f
    kl, _, k2, km, kr = fc
    out = [None] * VARS
    out[6 + axis] = kl * (r[0] + r[1] + r[2]) + k2 * r[axis]
    for v, source in READS[axis].items():
        out[source] = (km if v < 6 else kr) * r[v]
    return out


def face_consts(f, fcon, con):
    if f == 3:
        m = Mat.__new__(Mat)
        m.lam, m.mu2 = row(fcon, 15), row(fcon, 16)
        m.mg = [row(fcon, 17 + a) for a in range(3)]
        m.rg = [row(fcon, 20 + a) for a in range(3)]
        m.g = [row(fcon, 23 + a) for a in range(3)]
        return m
    return [row(fcon, 5 * f + n) for n in range(5)]


def far_side(rx, slot_turn, tn, hot_slot, out_loc, fb):
    rows = up_to(VARS * fb, 16)
    turned = turn_blocks(tn, split_rows(flipped(rx), fb), [slot_turn[0:1, :]])[0]
    high_low = stack2(jnp.concatenate(turned, axis=0), rows)

    def far(f, elems):
        cols = slice(f * elems, (f + 1) * elems)
        y = mm(high_low, hot_slot[:, cols])
        return out_loc[:, cols] + (y[: VARS * fb] + y[rows : rows + VARS * fb])

    return far


def surface(lf, own, far, fcon, con, fb, elems, jump_ref, flux_ref):
    half_speed = row(fcon, 26)
    fluxes = [[] for _ in range(VARS)]
    for f in range(4):
        cols = slice(f * elems, (f + 1) * elems)
        a, b = split_rows(own[:, cols], fb), split_rows(far(f, elems), fb)
        rows = face_rows(f, [x + y for x, y in zip(a, b)], face_consts(f, fcon, con))
        for v in range(VARS):
            jump = a[v] - b[v]
            flux = add(half_speed * jump, rows[v])
            jump_ref[v * fb : (v + 1) * fb, cols] = jump
            flux_ref[v * fb : (v + 1) * fb, cols] = flux
            fluxes[v].append(flux)
    return [apply2(lf, jnp.concatenate(x, axis=0)) for x in fluxes]


def face_sums(lifted, jump_ref, flux_ref, half_speed, fb, elems):
    total, speed = None, None
    for f in range(4):
        cols = slice(f * elems, (f + 1) * elems)
        r, d, x = [split_rows(ref[:, cols], fb) for ref in (lifted, jump_ref, flux_ref)]
        of_jump, of_flux = group_sums(r, d), group_sums(r, x)
        total = plus(total, [a - half_speed * b for a, b in zip(of_flux, of_jump)])
        more = of_jump[1] + of_jump[2] + of_jump[3]
        speed = more if speed is None else speed + more
    return total, speed


def faces_cot(seed, lt, tnt, turn, extra, fcon, con, lifted, own_cot, x_hl, fb, elems):
    half_speed = row(fcon, 26)
    rows = x_hl.shape[0] // 2
    for v in range(VARS):
        y = mm(lt[...], right3(seed[v], lt.shape[1] // 3))
        for f in range(4):
            lifted[v * fb : (v + 1) * fb, f * elems : (f + 1) * elems] = y[f * fb : (f + 1) * fb]
    for faces in ((0, 1), (2, 3)):
        x = []
        for f in faces:
            cols = slice(f * elems, (f + 1) * elems)
            r = split_rows(lifted[:, cols], fb)
            back = face_rows_back(f, r, face_consts(f, fcon, con))
            for v in range(VARS):
                side = half_speed * r[v]
                own_cot[v * fb : (v + 1) * fb, cols] = add(side, back[v])
                x.append(-side if back[v] is None else back[v] - side)
        turned = turn_blocks(tnt, x, [turn[f : f + 1, :] for f in faces])
        for f, y in zip(faces, turned):
            cols = slice(f * elems, (f + 1) * elems)
            if extra is not None:
                y.append(extra[:, cols])
            high, low = halves(padded(jnp.concatenate(y, axis=0), rows))
            x_hl[:rows, cols] = high
            x_hl[rows:, cols] = low


def scatter_local(own_cot, x_hl, hot, fb, elems, g):
    rows = x_hl.shape[0] // 2
    cols = slice(g * elems, (g + 1) * elems)
    y = mm_t(x_hl[...], hot[cols, :])
    own_cot[:, cols] = own_cot[:, cols] + (y[: VARS * fb] + y[rows : rows + VARS * fb])


def faces_back(own_cot, rx, hot_in, trt, fb, elems):
    rows = up_to(VARS * fb, 16)
    arrived = stack2(flipped(rx)[: VARS * fb], rows)
    for g in range(4):
        cols = slice(g * elems, (g + 1) * elems)
        y = mm(arrived, hot_in[:, cols])
        own_cot[:, cols] = own_cot[:, cols] + (y[: VARS * fb] + y[rows : rows + VARS * fb])
    out = []
    for v in range(VARS):
        x = [own_cot[v * fb : (v + 1) * fb, g * elems : (g + 1) * elems] for g in range(4)]
        out.append(apply2(trt, jnp.concatenate(x, axis=0)))
    return out


def weave(steps, pieces):
    done = 0
    for n, step in enumerate(steps):
        step()
        until = (n + 1) * len(pieces) // len(steps)
        for piece in pieces[done:until]:
            piece()
        done = until


def peers_of(devices):
    me = lax.axis_index("dom")
    shifts = [n + 1 for n in range(REACH)] + [-(n + 1) for n in range(REACH)] + [devices // 2]
    return [
        [lax.rem(me + sign * s + 2 * devices, devices) for s in shifts] for sign in (1, -1)
    ]


def send_all(peers, src, dst, send_sems, recv_sems, base=0):
    copies = []
    for n in reversed(range(LANES)):
        rows = pl.ds(n * CAP, CAP)
        copy = pltpu.make_async_remote_copy(
            src_ref=src.at[rows],
            dst_ref=dst.at[rows],
            send_sem=send_sems.at[base + n],
            recv_sem=recv_sems.at[base + n],
            device_id=(peers[n],),
            device_id_type=pl.DeviceIdType.MESH,
        )
        copy.start()
        copies.append(copy)
    return copies


def one_hot(mask):
    return jnp.where(mask, 1.0, 0.0).astype(bf16)


def face_places(
    devices, neighbours, orientation, fine, hot, hot_slot, hot_c, turn, slot_turn, extra
):
    elems = neighbours.shape[1]
    me = lax.axis_index("dom")
    at = lax.broadcasted_iota(i32, (16, elems), 0)
    square = (elems, elems)
    at_n, at_e = lax.broadcasted_iota(i32, square, 0), lax.broadcasted_iota(i32, square, 1)
    at_s = lax.broadcasted_iota(i32, (SLOTS, elems), 0)
    at_8 = lax.broadcasted_iota(i32, (8, elems), 0)
    earlier = one_hot(at_n <= at_e)
    lanes, marks, keys = [], [], []
    for f in range(4):
        cols = slice(f * elems, (f + 1) * elems)
        name, code = neighbours[f : f + 1, :], orientation[f : f + 1, :]
        far_face = sum(jnp.where(code >= 3 * g, 1, 0) for g in (1, 2, 3))
        turn[f : f + 1, :] = code - 3 * far_face
        present = name >= 0
        safe = jnp.maximum(name, 0)
        owner = jnp.floor((safe.astype(f32) + 0.5) * (1.0 / elems)).astype(i32)
        index = safe - owner * elems
        away = owner - me
        away = jnp.where(away < 0, away + devices, away)
        keys.append((cols, present & (away == 0), far_face, index))
        lane = jnp.where(
            away <= REACH,
            away - 1,
            jnp.where(away >= devices - REACH, REACH + devices - away - 1, 2 * REACH),
        )
        lane = jnp.where(present & (away != 0), lane, LANES)
        lanes.append(lane)
        marks.append(jnp.where(at == lane, 1.0, 0.0))
        index_f, face_f = index.astype(f32), far_face.astype(f32)
        extra[:, cols] = jnp.where(
            at_8 == 0, index_f, jnp.where(at_8 == 1, face_f, jnp.where(at_8 == 2, 1.0, 0.0))
        )
    is_fine = fine[...] == 1
    marks.append(jnp.where((at == 0) & is_fine, 1.0, 0.0))
    run = mm(jnp.concatenate(marks, axis=0).astype(bf16), earlier)
    carry = jnp.zeros((16, 1), f32)
    for f in range(4):
        cols = slice(f * elems, (f + 1) * elems)
        mine = run[16 * f : 16 * f + 16]
        rank = jnp.sum((mine + carry - 1.0) * marks[f], axis=0, keepdims=True).astype(i32)
        carry = carry + mine[:, elems - 1 :]
        slot = jnp.where(lanes[f] < LANES, lanes[f] * CAP + rank, -1)
        hot_slot[:, cols] = one_hot(at_s == slot)
    rank = jnp.where(is_fine, run[64:65].astype(i32) - 1, -1)
    picked = one_hot(lax.broadcasted_iota(i32, (FINE_DEV, elems), 0) == rank)
    hot_c[:FINE_DEV, :] = picked
    hot_c[FINE_DEV:, :] = picked
    turns = jnp.concatenate([turn[f : f + 1, :].astype(f32) for f in range(4)], axis=1)
    turns = jnp.broadcast_to(turns, (16, 4 * elems)).astype(bf16)
    slot_turn[...] = mm_t(turns, hot_slot[...])

    def fill(cols, local, far_face, index):
        names = at_n.astype(f32).astype(bf16)
        for g in range(4):
            key = jnp.where(local & (far_face == g), index, -1).astype(f32).astype(bf16)
            hot[g * elems : (g + 1) * elems, cols] = jnp.where(
                names == key, jnp.ones(square, bf16), jnp.zeros(square, bf16)
            )

    return [functools.partial(fill, *key) for key in keys]


def constants(mat_ref, geo_ref, con, fcon):
    lam, mu, rinv = [row(mat_ref, n) for n in range(3)]
    geo = [row(geo_ref, n) for n in range(3)]
    rows = [lam, 2.0 * mu] + [mu * g for g in geo] + [rinv * g for g in geo]
    base = jnp.concatenate(rows, axis=0)
    for n, scale in enumerate([-1.0] + STEP_SCALE):
        con[8 * n : 8 * n + 8, :] = scale * base
    rows = []
    for f in range(3):
        h = 0.5 * geo[2 - f]
        rows += [lam * h, (lam + 2.0 * mu) * h, 2.0 * mu * h, mu * h, rinv * h]
    h = [(-0.5 * root_third) * g for g in geo]
    rows += [lam, 2.0 * mu] + [mu * x for x in h] + [rinv * x for x in h] + h
    rows += [0.5 * jnp.sqrt((lam + 2.0 * mu) * rinv)]
    for n, x in enumerate(rows):
        fcon[n : n + 1, :] = x


def pitched(pad, matrices):
    pad[...] = jnp.zeros(pad.shape, f32)
    for n, x in enumerate(matrices):
        pad[n, : x.shape[0], : x.shape[1]] = x
    return [pad[n] for n in range(len(matrices))]


def turn_matrix(pad, matrices):
    zero = jnp.zeros(pad.shape[1:], f32)
    out = []
    for x in pitched(pad, matrices):
        out += [jnp.concatenate([x, zero], axis=1), jnp.concatenate([zero, x], axis=1)]
    return left3(jnp.concatenate(out, axis=0))


def step_kernel(
    devices,
    state_in, cot_in, mat_in, geo_in, fine_in, neighbours_in, orientation_in, stiffness_in,
    trace_in, lift_in, turns_in,
    final, grad,
    state, cot, mat_ref, geo_ref, stiffness, face_trace, face_lift, face_turns,
    w1, wc, w2, coarse, seed1, middle, vol1, vol2, cur, direct2,
    q1, q2, hist,
    own, lifted1, lifted2, out_loc, own_cot1, own_cot2, jump, flux,
    tx0, tx1, tx2, tx3, rx0, rx1, rx2, rx3,
    con, fcon, con_f, geo_f, extra, slot_turn,
    k_pad, t_pad, l_pad, n_pad,
    ks, kt, tr, lt, trt, lf, tn, tnt, hot, hot_slot, hot_in, hot_c, own_hl, x_hl1, x_hl2,
    fine, neighbours, orientation, turn, load_sems, send_sems, recv_sems,
):
    loads = [
        pltpu.make_async_copy(src, dst, load_sems.at[n])
        for n, (src, dst) in enumerate([
            (neighbours_in, neighbours), (orientation_in, orientation), (mat_in, mat_ref),
            (geo_in, geo_ref), (fine_in, fine), (stiffness_in, stiffness),
            (trace_in, face_trace), (lift_in, face_lift), (turns_in, face_turns),
            (cot_in, cot), (state_in, state),
        ])
    ]
    for load in loads:
        load.start()
    up, down = peers_of(devices)
    barrier = pltpu.get_barrier_semaphore()
    for peer in up:
        pl.semaphore_signal(
            barrier, inc=1, device_id=(peer,), device_id_type=pl.DeviceIdType.MESH
        )
    elems = state.shape[1]
    count = state.shape[0]
    size = count // VARS
    fb = t_pad.shape[1]
    wide = up_to(count, 16)
    part = functools.partial

    for load in loads[:9]:
        load.wait()
    constants(mat_ref, geo_ref, con, fcon)
    trace = jnp.concatenate(pitched(t_pad, [face_trace[:, g, :] for g in range(4)]), axis=0)
    tr[...] = left3(trace)
    trt[...] = left2(trace.T[:size])
    lift = jnp.concatenate(pitched(l_pad, [-face_lift[:, f, :] for f in range(4)]), axis=0)
    lt[...] = left3(lift)
    lf[...] = left2(lift.T[:size])
    turns = [face_turns[o] for o in range(3)]
    tn[...] = turn_matrix(n_pad, turns)
    tnt[...] = turn_matrix(n_pad, [x.T for x in turns])
    hot_fills = face_places(
        devices, neighbours, orientation, fine, hot, hot_slot, hot_c, turn, slot_turn, extra
    )
    base, half_speed = Mat(con, 0, geo_ref), row(fcon, 26)

    loads[9].wait()
    seed2 = blocks(cot, size)
    faces_cot(seed2, lt, tnt, turn, extra, fcon, con, lifted2, own_cot2, x_hl2, fb, elems)
    serve(hot_slot, x_hl2, tx0)

    def scatter(own_cot, x_hl):
        return [part(scatter_local, own_cot, x_hl, hot, fb, elems, g) for g in range(4)]

    pl.semaphore_wait(barrier, LANES)
    sent0 = send_all(up, tx0, rx0, send_sems, recv_sems, 0)

    stiff = pitched(k_pad, [stiffness[d] for d in range(3)])
    for mat, axes in ((ks, stiff), (kt, [x.T for x in stiff])):
        for n in range(3):
            order = [axes[(n + i) % 3][:size] for i in range(3)]
            mat[n] = left3(jnp.concatenate(order, axis=0))
    is_fine = fine[...] == 1
    loads[10].wait()

    def step1(k):
        old = blocks(state, size) if k == 0 else blocks(q1, size, (k - 1) * count)
        put(q1, apply_step(ks, old, Mat(con, 8 * (k + 1), geo_ref)), k * count)

    def gather():
        return [
            part(local_outer, own_hl, hot, turn, tn, out_loc, fb, elems, faces)
            for faces in ((0, 1), (2, 3))
        ]

    def volume(out, window):
        put(out, apply_step(kt, blocks(window, size), base))

    for piece in hot_fills + scatter(own_cot2, x_hl2):
        piece()
    for k in range(STEPS):
        step1(k)
    for v in range(VARS):
        rows = slice(v * size, (v + 1) * size)
        terms = [A0 * state[rows, :]]
        terms += [q1[k * count + v * size : k * count + (v + 1) * size, :] for k in range(STEPS)]
        w1[rows, :] = add(*terms)
        later = add(*[c * t if c != 1.0 else t for c, t in zip(C_OVER_A, terms)])
        wc[rows, :] = jnp.where(is_fine, 0.0, later)
    trace_faces(tr, w1, own, own_hl, fb, elems)
    for piece in gather():
        piece()
    for copy in sent0:
        copy.wait()

    key = rx0[:, VARS * fb : VARS * fb + 3]
    key = jnp.where(key[:, 2:3] > 0.5, key[:, 1:2] * float(elems) + key[:, 0:1], -1.0)
    at = lax.broadcasted_iota(i32, (SLOTS, 4 * elems), 1)
    hot_in[...] = one_hot(at == key.astype(i32))
    serve(hot_in, own_hl, tx1)
    sent1 = send_all(down, tx1, rx1, send_sems, recv_sems, LANES)

    put(direct2, apply_back(ks, seed2, base))
    back = faces_back(own_cot2, rx0, hot_in, trt, fb, elems)
    back = [a + b for a, b in zip(back, blocks(direct2, size))]
    put(coarse, [jnp.where(is_fine, 0.0, x) for x in back])
    seeds = split_rows(narrow(jnp.concatenate(back, axis=0), hot_c[:FINE_DEV, :], wide), size)
    put(hist, seeds, (STEPS - 1) * count)
    narrow_con = mm_t(
        jnp.concatenate(
            halves(con[0:16, :]) + halves(padded(geo_ref[...], 16)), axis=0
        ),
        hot_c[:FINE_DEV, :],
    )
    geo_f[...] = narrow_con[32:40] + narrow_con[48:56]
    for n, scale in enumerate(STEP_SCALE):
        con_f[8 * n : 8 * n + 8, :] = -scale * (narrow_con[0:8] + narrow_con[16:24])

    def back2(k):
        r = apply_back(kt, blocks(hist, size, k * count), Mat(con_f, 8 * k, geo_f))
        scale = A0 if k == 0 else 1.0
        direct = blocks(hist, size, (STEPS - 1) * count)
        r = [a + (b if k else scale * b) for a, b in zip(r, direct)]
        if k:
            put(hist, r, (k - 1) * count)
        else:
            seed1[...] = widen(jnp.concatenate(r, axis=0), hot_c[...], wide) + cot[...]

    for k in range(STEPS - 1, -1, -1):
        back2(k)
    faces_cot(
        blocks(seed1, size), lt, tnt, turn, None, fcon, con, lifted1, own_cot1, x_hl1, fb, elems
    )
    serve(hot_slot, x_hl1, tx3)
    sent3 = send_all(up, tx3, rx3, send_sems, recv_sems, 2 * LANES)
    put(cur, apply_back(ks, blocks(seed1, size), base))
    volume(vol1, w1)
    for copy in sent1:
        copy.wait()

    far = far_side(rx1, slot_turn, tn, hot_slot, out_loc, fb)
    change = surface(lf, own, far, fcon, con, fb, elems, jump, flux)
    put(middle, [
        s + m + c for s, m, c in zip(blocks(state, size), blocks(vol1, size), change)
    ])
    start = split_rows(narrow(middle[...], hot_c[:FINE_DEV, :], wide), size)
    first = [A0 * x for x in start]

    def step2(k):
        old = start if k == 0 else blocks(q2, size, (k - 1) * count)
        put(q2, apply_step(ks, old, Mat(con_f, 8 * k, geo_f)), k * count)

    for k in range(STEPS):
        step2(k)
    window = [
        add(first[v], *[
            q2[k * count + v * size : k * count + (v + 1) * size, :] for k in range(STEPS)
        ])
        for v in range(VARS)
    ]
    w2[...] = widen(jnp.concatenate(window, axis=0), hot_c[...], wide) + wc[...]
    trace_faces(tr, w2, own, own_hl, fb, elems)
    serve(hot_in, own_hl, tx2)
    sent2 = send_all(down, tx2, rx2, send_sems, recv_sems, 3 * LANES)

    sums, speed = face_sums(lifted1, jump, flux, half_speed, fb, elems)
    sums = plus(sums, group_sums(blocks(seed1, size), blocks(vol1, size)))
    for piece in scatter(own_cot1, x_hl1):
        piece()
    fine_sums = None
    for k in range(STEPS):
        fine_sums = plus(
            fine_sums, group_sums(blocks(hist, size, k * count), blocks(q2, size, k * count))
        )
    fine_sums = [jnp.sum(x, axis=0, keepdims=True) for x in fine_sums]
    fine_sums = widen(jnp.concatenate(fine_sums + fine_sums, axis=0), hot_c[...], 16)
    for copy in sent3:
        copy.wait()
    back = faces_back(own_cot1, rx3, hot_in, trt, fb, elems)
    put(seed1, [a + b for a, b in zip(back, blocks(cur, size))])
    chain = [sums]

    def back1(k):
        r = [a + C_OVER_A[k] * b for a, b in zip(blocks(seed1, size), blocks(coarse, size))]
        if k < STEPS:
            old = blocks(cur, size)
            r = [a + b for a, b in zip(r, apply_back(kt, old, Mat(con, 8 * (k + 1), geo_ref)))]
        put(cur, r)
        chain[0] = plus(
            chain[0], group_sums(blocks(cur, size), blocks(q1, size, (k - 1) * count))
        )

    weave([part(back1, k) for k in range(STEPS, 0, -1)], gather() + [part(volume, vol2, w2)])
    sums = plus(chain[0], group_sums(seed2, blocks(vol2, size)))
    for copy in sent2:
        copy.wait()

    far = far_side(rx2, slot_turn, tn, hot_slot, out_loc, fb)
    change = surface(lf, own, far, fcon, con, fb, elems, jump, flux)
    put(final, [
        s + m + c for s, m, c in zip(blocks(middle, size), blocks(vol2, size), change)
    ])
    more, more_speed = face_sums(lifted2, jump, flux, half_speed, fb, elems)
    sums = [jnp.sum(a + b, axis=0, keepdims=True) for a, b in zip(sums, more)]
    sums = [a + fine_sums[n : n + 1] for n, a in enumerate(sums)]
    g_speed = 0.5 * jnp.sum(speed + more_speed, axis=0, keepdims=True)
    lam, mu, rinv = [row(mat_ref, n) for n in range(3)]
    wave = jnp.sqrt((lam + 2.0 * mu) * rinv)
    g_lam = sums[0] / (3.0 * lam + 2.0 * mu)
    g_mu = (sums[1] - lam * g_lam + sums[2]) / mu
    g_speed = g_speed / wave
    grad[...] = jnp.concatenate(
        [
            g_lam + 0.5 * g_speed * rinv,
            g_mu + g_speed * rinv,
            sums[3] / rinv + 0.5 * g_speed * (lam + 2.0 * mu),
        ],
        axis=0,
    )


def finish_kernel(final, grad, final_out, grad_out, sems):
    copies = [
        pltpu.make_async_copy(final, final_out, sems.at[0]),
        pltpu.make_async_copy(grad, grad_out, sems.at[1]),
    ]
    for copy in copies:
        copy.start()
    for copy in copies:
        copy.wait()


def body(
    start_state, material, geometry, clusters, neighbours, orientation,
    stiffness, face_trace, face_lift, face_turns, cotangent,
):
    rows, elems = start_state.shape
    basis = rows // VARS
    devices = lax.axis_size("dom")
    fb = up_to(face_trace.shape[1], 8)
    pitch = up_to(basis, 16)
    frows = up_to(VARS * fb + 8, 16)
    full, faces, slots = (rows, elems), (VARS * fb, 4 * elems), (SLOTS, up_to(frows, 128))
    args = (
        start_state, cotangent, material, geometry, clusters.reshape(1, elems), neighbours,
        orientation, stiffness, face_trace.transpose(1, 0, 2), face_lift.transpose(2, 0, 1),
        face_turns,
    )
    scratch = [x.shape for x in args[:4]] + [x.shape for x in args[7:]]
    scratch += [full] * 10
    scratch += [(STEPS * rows, elems)] + [(STEPS * rows, FINE_DEV)] * 2
    scratch += [faces] * 8 + [slots] * 8
    scratch += [(8 * TERMS, elems), (32, elems), (8 * STEPS, FINE_DEV), (8, FINE_DEV)]
    scratch += [(8, 4 * elems), (16, SLOTS)]
    scratch += [(3, pitch, pitch), (4, fb, pitch), (4, fb, pitch), (3, fb, fb)]
    packed = [(3, 3 * basis, 3 * pitch)] * 2 + [(4 * fb, 3 * pitch)] * 2
    packed += [(2 * basis, 8 * fb)] * 2 + [(6 * fb, 6 * fb)] * 2
    packed += [(4 * elems, 4 * elems)] + [(SLOTS, 4 * elems)] * 2 + [(2 * FINE_DEV, elems)]
    packed += [(2 * frows, 4 * elems)] * 3
    args = [pltpu.with_memory_space_constraint(x, pltpu.HBM) for x in args]
    outs = pl.pallas_call(
        functools.partial(step_kernel, devices),
        out_shape=[
            jax.ShapeDtypeStruct((rows, elems), f32),
            jax.ShapeDtypeStruct((3, elems), f32),
        ],
        in_specs=[pl.BlockSpec(memory_space=pltpu.HBM)] * len(args),
        out_specs=[pl.BlockSpec(memory_space=pltpu.VMEM)] * 2,
        scratch_shapes=[pltpu.VMEM(s, f32) for s in scratch]
        + [pltpu.VMEM(s, bf16) for s in packed]
        + [pltpu.VMEM((1, elems), i32)]
        + [pltpu.VMEM((4, elems), i32)] * 3
        + [pltpu.SemaphoreType.DMA((len(args),))]
        + [pltpu.SemaphoreType.DMA((4 * LANES,))] * 2,
        compiler_params=pltpu.CompilerParams(
            vmem_limit_bytes=48 * 1024 * 1024, collective_id=0, has_side_effects=True
        ),
        name="ader_step",
    )(*args)
    return pl.pallas_call(
        finish_kernel,
        out_shape=[jax.ShapeDtypeStruct(x.shape, f32) for x in outs],
        in_specs=[pl.BlockSpec(memory_space=pltpu.VMEM)] * 2,
        out_specs=[pl.BlockSpec(memory_space=pl.ANY)] * 2,
        scratch_shapes=[pltpu.SemaphoreType.DMA((2,))],
        compiler_params=pltpu.CompilerParams(vmem_limit_bytes=2 * 1024 * 1024),
        name="finish",
    )(*outs)


def solution(mesh):
    return jax.shard_map(
        body,
        mesh=mesh,
        in_specs=(
            P(None, "dom"),
            P(None, "dom"),
            P(None, "dom"),
            P("dom"),
            P(None, "dom"),
            P(None, "dom"),
            P(),
            P(),
            P(),
            P(),
            P(None, "dom"),
        ),
        out_specs=(P(None, "dom"), P(None, "dom")),
        check_vma=False,
    )
```

```python
import functools

import jax
import jax.numpy as jnp
from jax import lax
from jax.experimental import pallas as pl
from jax.experimental.pallas import tpu as pltpu
from jax.sharding import PartitionSpec as P

VARS = 9
TERMS = 6
REACH = 4
CAP = 16
FINE_DEV = 128
LANES = 2 * REACH + 1
SLOTS = LANES * CAP
STEPS = TERMS - 1
f32, bf16, i32 = jnp.float32, jnp.bfloat16, jnp.int32

dt_step = 0.5
root_third = 0.5773502691896258
H = 0.5 * dt_step

A0 = H
STEP_SCALE = [H * H / 2.0] + [H / (k + 2.0) for k in range(1, STEPS)]
C_OVER_A = [2.0 ** (k + 1) - 1.0 for k in range(TERMS)]

NEED = [(0, 1), (1, 1), (2, 1), (0, 2), (1, 2), (2, 2), (0, 3), (0, 3), (0, 3)]
PAIRS = [((6, 7), 0, 3), ((8, 3), 0, 3), ((0, 1), 0, 2), ((4, 2), 1, 2), ((5,), 2, 2)]
READS = [
    {3: 7, 5: 8, 6: 0, 7: 3, 8: 5},
    {3: 6, 4: 8, 6: 3, 7: 1, 8: 4},
    {4: 7, 5: 6, 6: 5, 7: 4, 8: 2},
]


def up_to(n, m):
    return -(-n // m) * m


def halves(x):
    high = x.astype(bf16)
    return high, (x - high.astype(f32)).astype(bf16)


def padded(x, rows):
    if x.shape[0] == rows:
        return x
    return jnp.concatenate([x, jnp.zeros((rows - x.shape[0], x.shape[1]), f32)], axis=0)


def right3(x, rows):
    high, low = halves(padded(x, rows))
    return jnp.concatenate([high, high, low], axis=0)


def left3(a):
    high = a.astype(bf16).astype(f32)
    return jnp.concatenate([high, a - high, high], axis=1).astype(bf16)


def left2(a):
    high = a.astype(bf16).astype(f32)
    upper = jnp.concatenate([high, high], axis=1)
    lower = jnp.concatenate([a - high, jnp.zeros(a.shape, f32)], axis=1)
    return jnp.concatenate([upper, lower], axis=0).astype(bf16)


def apply2(mat, x):
    y = mm(mat[...], stack2(x, x.shape[0]))
    half = y.shape[0] // 2
    return y[:half] + y[half:]


def stack2(x, rows):
    return jnp.concatenate(halves(padded(x, rows)), axis=0)


def mm(a, b):
    return jnp.dot(a, b, preferred_element_type=f32)


def mm_t(a, b):
    return lax.dot_general(a, b, (((1,), (1,)), ((), ())), preferred_element_type=f32)


def add(*terms):
    total = None
    for t in terms:
        if t is not None:
            total = t if total is None else total + t
    return total


def blocks(ref, size, base=0):
    return [ref[base + v * size : base + (v + 1) * size, :] for v in range(VARS)]


def put(ref, values, base=0):
    size = values[0].shape[0]
    for v in range(VARS):
        ref[base + v * size : base + (v + 1) * size, :] = values[v]


def row(ref, n):
    return ref[n : n + 1, :]


class Mat:
    def __init__(self, con, base, geo):
        self.lam, self.mu2 = row(con, base), row(con, base + 1)
        self.mg = [row(con, base + 2 + a) for a in range(3)]
        self.rg = [row(con, base + 5 + a) for a in range(3)]
        self.g = [row(geo, a) for a in range(3)]


def forward_mix(p, m):
    t = [m.g[a] * p(6 + a, a) for a in range(3)]
    spread = m.lam * (t[0] + t[1] + t[2])
    return [
        spread + m.mu2 * t[0],
        spread + m.mu2 * t[1],
        spread + m.mu2 * t[2],
        m.mg[0] * p(7, 0) + m.mg[1] * p(6, 1),
        m.mg[1] * p(8, 1) + m.mg[2] * p(7, 2),
        m.mg[0] * p(8, 0) + m.mg[2] * p(6, 2),
        m.rg[0] * p(0, 0) + m.rg[1] * p(3, 1) + m.rg[2] * p(5, 2),
        m.rg[0] * p(3, 0) + m.rg[1] * p(1, 1) + m.rg[2] * p(4, 2),
        m.rg[0] * p(5, 0) + m.rg[1] * p(4, 1) + m.rg[2] * p(2, 2),
    ]


def normal_mix(r, m):
    u = m.lam * (r[0] + r[1] + r[2])
    return [u + m.mu2 * r[a] for a in range(3)] + list(r[3:])


def backward_mix(p, m):
    return [
        m.rg[0] * p(6, 0),
        m.rg[1] * p(7, 1),
        m.rg[2] * p(8, 2),
        m.rg[0] * p(7, 0) + m.rg[1] * p(6, 1),
        m.rg[1] * p(8, 1) + m.rg[2] * p(7, 2),
        m.rg[0] * p(8, 0) + m.rg[2] * p(6, 2),
        m.g[0] * p(0, 0) + m.mg[1] * p(3, 1) + m.mg[2] * p(5, 2),
        m.g[1] * p(1, 1) + m.mg[0] * p(3, 0) + m.mg[2] * p(4, 2),
        m.g[2] * p(2, 2) + m.mg[1] * p(4, 1) + m.mg[0] * p(5, 0),
    ]


def products(mat, values):
    size, width = values[0].shape
    pitch = mat.shape[2] // 3
    out = {}
    if width == FINE_DEV:
        groups = PAIRS
    else:
        groups = [((v,), s, c) for v, (s, c) in enumerate(NEED)]
    for names, start, count in groups:
        x = [values[v] for v in names]
        x = x[0] if len(x) == 1 else jnp.concatenate(x, axis=1)
        y = mm(mat[start, : count * size, :], right3(x, pitch))
        for n, v in enumerate(names):
            for i in range(count):
                out[v, (start + i) % 3] = y[
                    i * size : (i + 1) * size, n * width : (n + 1) * width
                ]
    return lambda v, axis: out[v, axis]


def apply_step(mat, values, m):
    return forward_mix(products(mat, values), m)


def apply_back(mat, values, m):
    return backward_mix(products(mat, normal_mix(values, m)), m)


def fold8(x):
    total = x[0:8]
    for n in range(8, x.shape[0], 8):
        total = total + x[n : n + 8]
    return total


def group_sums(r, x):
    mixed = (r[0] + r[1] + r[2]) * (x[0] + x[1] + x[2])
    groups = [add(*[r[v] * x[v] for v in range(g, g + 3)]) for g in (0, 3, 6)]
    return [fold8(g) for g in [mixed] + groups]


def plus(total, more):
    return more if total is None else [a + b for a, b in zip(total, more)]


def narrow(x, hot_c, rows):
    y = mm_t(stack2(x, rows), hot_c)
    return y[: x.shape[0]] + y[rows : rows + x.shape[0]]


def widen(x, hot_c2, rows):
    high, low = halves(padded(x, rows))
    return mm(jnp.concatenate([high, low], axis=1), hot_c2)[: x.shape[0]]


def trace_faces(tr, window, own, own_hl, fb, elems):
    size = window.shape[0] // VARS
    rows = own_hl.shape[0] // 2
    for v in range(VARS):
        t = mm(tr[...], right3(window[v * size : (v + 1) * size, :], tr.shape[1] // 3))
        for g in range(4):
            own[v * fb : (v + 1) * fb, g * elems : (g + 1) * elems] = t[g * fb : (g + 1) * fb]
    for g in range(4):
        cols = slice(g * elems, (g + 1) * elems)
        high, low = halves(padded(own[:, cols], rows))
        own_hl[:rows, cols] = high
        own_hl[rows:, cols] = low


def turn_blocks(mat, x, which):
    fb = x[0].shape[0]
    pick = [(w == 0, w == 1) for w in which]
    out = [None] * len(x)
    order = [f * VARS + v for f in range(len(which)) for v in range(VARS - 1)]
    order += [f * VARS + VARS - 1 for f in range(len(which))]
    for n in range(0, len(x), 2):
        names = order[n : n + 2]
        pair = [x[b] for b in names]
        y = mm(mat[...], right3(jnp.concatenate(pair, axis=0), 2 * fb))
        for i, b in enumerate(names):
            first, second = pick[b // VARS]
            part = [y[o * 2 * fb + i * fb : o * 2 * fb + (i + 1) * fb] for o in range(3)]
            out[b] = jnp.where(first, part[0], jnp.where(second, part[1], part[2]))
    return [out[n : n + VARS] for n in range(0, len(x), VARS)]


def split_rows(x, fb):
    return [x[v * fb : (v + 1) * fb] for v in range(VARS)]


def local_outer(own_hl, hot, turn, tn, out, fb, elems, faces):
    rows = own_hl.shape[0] // 2
    raw = []
    for f in faces:
        y = mm(own_hl[...], hot[:, f * elems : (f + 1) * elems])
        raw += split_rows(y[: VARS * fb] + y[rows : rows + VARS * fb], fb)
    turned = turn_blocks(tn, raw, [turn[f : f + 1, :] for f in faces])
    for f, x in zip(faces, turned):
        out[:, f * elems : (f + 1) * elems] = jnp.concatenate(x, axis=0)


def serve(hot_in, own_hl, tx):
    rows = own_hl.shape[0] // 2
    tx[:, :rows] = mm_t(hot_in[...], own_hl[:rows, :]) + mm_t(hot_in[...], own_hl[rows:, :])
    tx[:, rows:] = jnp.zeros((tx.shape[0], tx.shape[1] - rows), f32)


def flipped(rx):
    x = rx[...]
    return padded(x, up_to(x.shape[0], 128)).T[:, : x.shape[0]]


def face_rows(f, x, fc):
    if f == 3:
        return forward_mix(lambda v, axis: x[v], fc)
    axis = 2 - f
    kl, kp, _, km, kr = fc
    t = x[6 + axis]
    rows = [kl * t] * 3 + [None] * 6
    rows[axis] = kp * t
    for v, source in READS[axis].items():
        rows[v] = (km if v < 6 else kr) * x[source]
    return rows


def face_rows_back(f, r, fc):
    if f == 3:
        s = normal_mix(r, fc)
        return backward_mix(lambda v, axis: s[v], fc)
    axis = 2 - f
    kl, _, k2, km, kr = fc
    out = [None] * VARS
    out[6 + axis] = kl * (r[0] + r[1] + r[2]) + k2 * r[axis]
    for v, source in READS[axis].items():
        out[source] = (km if v < 6 else kr) * r[v]
    return out


def face_consts(f, fcon, con):
    if f == 3:
        m = Mat.__new__(Mat)
        m.lam, m.mu2 = row(fcon, 15), row(fcon, 16)
        m.mg = [row(fcon, 17 + a) for a in range(3)]
        m.rg = [row(fcon, 20 + a) for a in range(3)]
        m.g = [row(fcon, 23 + a) for a in range(3)]
        return m
    return [row(fcon, 5 * f + n) for n in range(5)]


def far_side(rx, slot_turn, tn, hot_slot, out_loc, fb):
    rows = up_to(VARS * fb, 16)
    turned = turn_blocks(tn, split_rows(flipped(rx), fb), [slot_turn[0:1, :]])[0]
    high_low = stack2(jnp.concatenate(turned, axis=0), rows)

    def far(f, elems):
        cols = slice(f * elems, (f + 1) * elems)
        y = mm(high_low, hot_slot[:, cols])
        return out_loc[:, cols] + (y[: VARS * fb] + y[rows : rows + VARS * fb])

    return far


def surface(lf, own, far, fcon, con, fb, elems, jump_ref, flux_ref):
    half_speed = row(fcon, 26)
    fluxes = [[] for _ in range(VARS)]
    for f in range(4):
        cols = slice(f * elems, (f + 1) * elems)
        a, b = split_rows(own[:, cols], fb), split_rows(far(f, elems), fb)
        rows = face_rows(f, [x + y for x, y in zip(a, b)], face_consts(f, fcon, con))
        for v in range(VARS):
            jump = a[v] - b[v]
            flux = add(half_speed * jump, rows[v])
            jump_ref[v * fb : (v + 1) * fb, cols] = jump
            flux_ref[v * fb : (v + 1) * fb, cols] = flux
            fluxes[v].append(flux)
    return [apply2(lf, jnp.concatenate(x, axis=0)) for x in fluxes]


def face_sums(lifted, jump_ref, flux_ref, half_speed, fb, elems):
    total, speed = None, None
    for f in range(4):
        cols = slice(f * elems, (f + 1) * elems)
        r, d, x = [split_rows(ref[:, cols], fb) for ref in (lifted, jump_ref, flux_ref)]
        of_jump, of_flux = group_sums(r, d), group_sums(r, x)
        total = plus(total, [a - half_speed * b for a, b in zip(of_flux, of_jump)])
        more = of_jump[1] + of_jump[2] + of_jump[3]
        speed = more if speed is None else speed + more
    return total, speed


def faces_cot(seed, lt, tnt, turn, extra, fcon, con, lifted, own_cot, x_hl, fb, elems):
    half_speed = row(fcon, 26)
    rows = x_hl.shape[0] // 2
    for v in range(VARS):
        y = mm(lt[...], right3(seed[v], lt.shape[1] // 3))
        for f in range(4):
            lifted[v * fb : (v + 1) * fb, f * elems : (f + 1) * elems] = y[f * fb : (f + 1) * fb]
    for faces in ((0, 1), (2, 3)):
        x = []
        for f in faces:
            cols = slice(f * elems, (f + 1) * elems)
            r = split_rows(lifted[:, cols], fb)
            back = face_rows_back(f, r, face_consts(f, fcon, con))
            for v in range(VARS):
                side = half_speed * r[v]
                own_cot[v * fb : (v + 1) * fb, cols] = add(side, back[v])
                x.append(-side if back[v] is None else back[v] - side)
        turned = turn_blocks(tnt, x, [turn[f : f + 1, :] for f in faces])
        for f, y in zip(faces, turned):
            cols = slice(f * elems, (f + 1) * elems)
            if extra is not None:
                y.append(extra[:, cols])
            high, low = halves(padded(jnp.concatenate(y, axis=0), rows))
            x_hl[:rows, cols] = high
            x_hl[rows:, cols] = low


def scatter_local(own_cot, x_hl, hot, fb, elems, g):
    rows = x_hl.shape[0] // 2
    cols = slice(g * elems, (g + 1) * elems)
    y = mm_t(x_hl[...], hot[cols, :])
    own_cot[:, cols] = own_cot[:, cols] + (y[: VARS * fb] + y[rows : rows + VARS * fb])


def faces_back(own_cot, rx, hot_in, trt, fb, elems):
    rows = up_to(VARS * fb, 16)
    arrived = stack2(flipped(rx)[: VARS * fb], rows)
    for g in range(4):
        cols = slice(g * elems, (g + 1) * elems)
        y = mm(arrived, hot_in[:, cols])
        own_cot[:, cols] = own_cot[:, cols] + (y[: VARS * fb] + y[rows : rows + VARS * fb])
    out = []
    for v in range(VARS):
        x = [own_cot[v * fb : (v + 1) * fb, g * elems : (g + 1) * elems] for g in range(4)]
        out.append(apply2(trt, jnp.concatenate(x, axis=0)))
    return out


def weave(steps, pieces):
    done = 0
    for n, step in enumerate(steps):
        step()
        until = (n + 1) * len(pieces) // len(steps)
        for piece in pieces[done:until]:
            piece()
        done = until


def peers_of(devices):
    me = lax.axis_index("dom")
    shifts = [n + 1 for n in range(REACH)] + [-(n + 1) for n in range(REACH)] + [devices // 2]
    return [
        [lax.rem(me + sign * s + 2 * devices, devices) for s in shifts] for sign in (1, -1)
    ]


def send_all(peers, src, dst, send_sems, recv_sems, base=0):
    copies = []
    for n in reversed(range(LANES)):
        rows = pl.ds(n * CAP, CAP)
        copy = pltpu.make_async_remote_copy(
            src_ref=src.at[rows],
            dst_ref=dst.at[rows],
            send_sem=send_sems.at[base + n],
            recv_sem=recv_sems.at[base + n],
            device_id=(peers[n],),
            device_id_type=pl.DeviceIdType.MESH,
        )
        copy.start()
        copies.append(copy)
    return copies


def one_hot(mask):
    return jnp.where(mask, 1.0, 0.0).astype(bf16)


def face_places(
    devices, neighbours, orientation, fine, hot, hot_slot, hot_c, turn, slot_turn, extra
):
    elems = neighbours.shape[1]
    me = lax.axis_index("dom")
    at = lax.broadcasted_iota(i32, (16, elems), 0)
    square = (elems, elems)
    at_n, at_e = lax.broadcasted_iota(i32, square, 0), lax.broadcasted_iota(i32, square, 1)
    at_s = lax.broadcasted_iota(i32, (SLOTS, elems), 0)
    at_8 = lax.broadcasted_iota(i32, (8, elems), 0)
    earlier = one_hot(at_n <= at_e)
    lanes, marks, keys = [], [], []
    for f in range(4):
        cols = slice(f * elems, (f + 1) * elems)
        name, code = neighbours[f : f + 1, :], orientation[f : f + 1, :]
        far_face = sum(jnp.where(code >= 3 * g, 1, 0) for g in (1, 2, 3))
        turn[f : f + 1, :] = code - 3 * far_face
        present = name >= 0
        safe = jnp.maximum(name, 0)
        owner = jnp.floor((safe.astype(f32) + 0.5) * (1.0 / elems)).astype(i32)
        index = safe - owner * elems
        away = owner - me
        away = jnp.where(away < 0, away + devices, away)
        keys.append((cols, present & (away == 0), far_face, index))
        lane = jnp.where(
            away <= REACH,
            away - 1,
            jnp.where(away >= devices - REACH, REACH + devices - away - 1, 2 * REACH),
        )
        lane = jnp.where(present & (away != 0), lane, LANES)
        lanes.append(lane)
        marks.append(jnp.where(at == lane, 1.0, 0.0))
        index_f, face_f = index.astype(f32), far_face.astype(f32)
        extra[:, cols] = jnp.where(
            at_8 == 0, index_f, jnp.where(at_8 == 1, face_f, jnp.where(at_8 == 2, 1.0, 0.0))
        )
    is_fine = fine[...] == 1
    marks.append(jnp.where((at == 0) & is_fine, 1.0, 0.0))
    run = mm(jnp.concatenate(marks, axis=0).astype(bf16), earlier)
    carry = jnp.zeros((16, 1), f32)
    for f in range(4):
        cols = slice(f * elems, (f + 1) * elems)
        mine = run[16 * f : 16 * f + 16]
        rank = jnp.sum((mine + carry - 1.0) * marks[f], axis=0, keepdims=True).astype(i32)
        carry = carry + mine[:, elems - 1 :]
        slot = jnp.where(lanes[f] < LANES, lanes[f] * CAP + rank, -1)
        hot_slot[:, cols] = one_hot(at_s == slot)
    rank = jnp.where(is_fine, run[64:65].astype(i32) - 1, -1)
    picked = one_hot(lax.broadcasted_iota(i32, (FINE_DEV, elems), 0) == rank)
    hot_c[:FINE_DEV, :] = picked
    hot_c[FINE_DEV:, :] = picked
    turns = jnp.concatenate([turn[f : f + 1, :].astype(f32) for f in range(4)], axis=1)
    turns = jnp.broadcast_to(turns, (16, 4 * elems)).astype(bf16)
    slot_turn[...] = mm_t(turns, hot_slot[...])

    def fill(cols, local, far_face, index):
        names = at_n.astype(f32).astype(bf16)
        for g in range(4):
            key = jnp.where(local & (far_face == g), index, -1).astype(f32).astype(bf16)
            hot[g * elems : (g + 1) * elems, cols] = jnp.where(
                names == key, jnp.ones(square, bf16), jnp.zeros(square, bf16)
            )

    return [functools.partial(fill, *key) for key in keys]


def constants(mat_ref, geo_ref, con, fcon):
    lam, mu, rinv = [row(mat_ref, n) for n in range(3)]
    geo = [row(geo_ref, n) for n in range(3)]
    rows = [lam, 2.0 * mu] + [mu * g for g in geo] + [rinv * g for g in geo]
    base = jnp.concatenate(rows, axis=0)
    for n, scale in enumerate([-1.0] + STEP_SCALE):
        con[8 * n : 8 * n + 8, :] = scale * base
    rows = []
    for f in range(3):
        h = 0.5 * geo[2 - f]
        rows += [lam * h, (lam + 2.0 * mu) * h, 2.0 * mu * h, mu * h, rinv * h]
    h = [(-0.5 * root_third) * g for g in geo]
    rows += [lam, 2.0 * mu] + [mu * x for x in h] + [rinv * x for x in h] + h
    rows += [0.5 * jnp.sqrt((lam + 2.0 * mu) * rinv)]
    for n, x in enumerate(rows):
        fcon[n : n + 1, :] = x


def pitched(pad, matrices):
    pad[...] = jnp.zeros(pad.shape, f32)
    for n, x in enumerate(matrices):
        pad[n, : x.shape[0], : x.shape[1]] = x
    return [pad[n] for n in range(len(matrices))]


def turn_matrix(pad, matrices):
    zero = jnp.zeros(pad.shape[1:], f32)
    out = []
    for x in pitched(pad, matrices):
        out += [jnp.concatenate([x, zero], axis=1), jnp.concatenate([zero, x], axis=1)]
    return left3(jnp.concatenate(out, axis=0))


def step_kernel(
    devices,
    state_in, cot_in, mat_in, geo_in, fine_in, neighbours_in, orientation_in, stiffness_in,
    trace_in, lift_in, turns_in,
    final, grad,
    state, cot, mat_ref, geo_ref, stiffness, face_trace, face_lift, face_turns,
    w1, wc, w2, coarse, seed1, middle, vol1, vol2, cur, direct2,
    q1, q2, hist,
    own, lifted1, lifted2, out_loc, own_cot1, own_cot2, jump, flux,
    tx0, tx1, tx2, tx3, rx0, rx1, rx2, rx3,
    con, fcon, con_f, geo_f, extra, slot_turn,
    k_pad, t_pad, l_pad, n_pad,
    ks, kt, tr, lt, trt, lf, tn, tnt, hot, hot_slot, hot_in, hot_c, own_hl, x_hl1, x_hl2,
    fine, neighbours, orientation, turn, load_sems, send_sems, recv_sems,
):
    loads = [
        pltpu.make_async_copy(src, dst, load_sems.at[n])
        for n, (src, dst) in enumerate([
            (neighbours_in, neighbours), (orientation_in, orientation), (mat_in, mat_ref),
            (geo_in, geo_ref), (fine_in, fine), (stiffness_in, stiffness),
            (trace_in, face_trace), (lift_in, face_lift), (turns_in, face_turns),
            (cot_in, cot), (state_in, state),
        ])
    ]
    for load in loads:
        load.start()
    up, down = peers_of(devices)
    barrier = pltpu.get_barrier_semaphore()
    for peer in up:
        pl.semaphore_signal(
            barrier, inc=1, device_id=(peer,), device_id_type=pl.DeviceIdType.MESH
        )
    elems = state.shape[1]
    count = state.shape[0]
    size = count // VARS
    fb = t_pad.shape[1]
    wide = up_to(count, 16)
    part = functools.partial

    for load in loads[:9]:
        load.wait()
    constants(mat_ref, geo_ref, con, fcon)
    trace = jnp.concatenate(pitched(t_pad, [face_trace[:, g, :] for g in range(4)]), axis=0)
    tr[...] = left3(trace)
    trt[...] = left2(trace.T[:size])
    lift = jnp.concatenate(pitched(l_pad, [-face_lift[:, f, :] for f in range(4)]), axis=0)
    lt[...] = left3(lift)
    lf[...] = left2(lift.T[:size])
    turns = [face_turns[o] for o in range(3)]
    tn[...] = turn_matrix(n_pad, turns)
    tnt[...] = turn_matrix(n_pad, [x.T for x in turns])
    hot_fills = face_places(
        devices, neighbours, orientation, fine, hot, hot_slot, hot_c, turn, slot_turn, extra
    )
    base, half_speed = Mat(con, 0, geo_ref), row(fcon, 26)

    loads[9].wait()
    seed2 = blocks(cot, size)
    faces_cot(seed2, lt, tnt, turn, extra, fcon, con, lifted2, own_cot2, x_hl2, fb, elems)
    serve(hot_slot, x_hl2, tx0)
    for piece in hot_fills:
        piece()

    def scatter(own_cot, x_hl):
        return [part(scatter_local, own_cot, x_hl, hot, fb, elems, g) for g in range(4)]

    pl.semaphore_wait(barrier, LANES)
    sent0 = send_all(up, tx0, rx0, send_sems, recv_sems, 0)

    stiff = pitched(k_pad, [stiffness[d] for d in range(3)])
    for mat, axes in ((ks, stiff), (kt, [x.T for x in stiff])):
        for n in range(3):
            order = [axes[(n + i) % 3][:size] for i in range(3)]
            mat[n] = left3(jnp.concatenate(order, axis=0))
    is_fine = fine[...] == 1
    loads[10].wait()

    def step1(k):
        old = blocks(state, size) if k == 0 else blocks(q1, size, (k - 1) * count)
        put(q1, apply_step(ks, old, Mat(con, 8 * (k + 1), geo_ref)), k * count)

    def gather():
        return [
            part(local_outer, own_hl, hot, turn, tn, out_loc, fb, elems, faces)
            for faces in ((0, 1), (2, 3))
        ]

    def volume(out, window):
        put(out, apply_step(kt, blocks(window, size), base))

    for piece in scatter(own_cot2, x_hl2):
        piece()
    for k in range(STEPS):
        step1(k)
    for v in range(VARS):
        rows = slice(v * size, (v + 1) * size)
        terms = [A0 * state[rows, :]]
        terms += [q1[k * count + v * size : k * count + (v + 1) * size, :] for k in range(STEPS)]
        w1[rows, :] = add(*terms)
        later = add(*[c * t if c != 1.0 else t for c, t in zip(C_OVER_A, terms)])
        wc[rows, :] = jnp.where(is_fine, 0.0, later)
    trace_faces(tr, w1, own, own_hl, fb, elems)
    for piece in gather():
        piece()
    for copy in sent0:
        copy.wait()

    key = rx0[:, VARS * fb : VARS * fb + 3]
    key = jnp.where(key[:, 2:3] > 0.5, key[:, 1:2] * float(elems) + key[:, 0:1], -1.0)
    at = lax.broadcasted_iota(i32, (SLOTS, 4 * elems), 1)
    hot_in[...] = one_hot(at == key.astype(i32))
    serve(hot_in, own_hl, tx1)
    sent1 = send_all(down, tx1, rx1, send_sems, recv_sems, LANES)

    put(direct2, apply_back(ks, seed2, base))
    back = faces_back(own_cot2, rx0, hot_in, trt, fb, elems)
    back = [a + b for a, b in zip(back, blocks(direct2, size))]
    put(coarse, [jnp.where(is_fine, 0.0, x) for x in back])
    seeds = split_rows(narrow(jnp.concatenate(back, axis=0), hot_c[:FINE_DEV, :], wide), size)
    put(hist, seeds, (STEPS - 1) * count)
    narrow_con = mm_t(
        jnp.concatenate(
            halves(con[0:16, :]) + halves(padded(geo_ref[...], 16)), axis=0
        ),
        hot_c[:FINE_DEV, :],
    )
    geo_f[...] = narrow_con[32:40] + narrow_con[48:56]
    for n, scale in enumerate(STEP_SCALE):
        con_f[8 * n : 8 * n + 8, :] = -scale * (narrow_con[0:8] + narrow_con[16:24])

    def back2(k):
        r = apply_back(kt, blocks(hist, size, k * count), Mat(con_f, 8 * k, geo_f))
        scale = A0 if k == 0 else 1.0
        direct = blocks(hist, size, (STEPS - 1) * count)
        r = [a + (b if k else scale * b) for a, b in zip(r, direct)]
        if k:
            put(hist, r, (k - 1) * count)
        else:
            seed1[...] = widen(jnp.concatenate(r, axis=0), hot_c[...], wide) + cot[...]

    for k in range(STEPS - 1, -1, -1):
        back2(k)
    faces_cot(
        blocks(seed1, size), lt, tnt, turn, None, fcon, con, lifted1, own_cot1, x_hl1, fb, elems
    )
    serve(hot_slot, x_hl1, tx3)
    sent3 = send_all(up, tx3, rx3, send_sems, recv_sems, 2 * LANES)
    for piece in scatter(own_cot1, x_hl1):
        piece()
    put(cur, apply_back(ks, blocks(seed1, size), base))
    volume(vol1, w1)
    for copy in sent1:
        copy.wait()

    far = far_side(rx1, slot_turn, tn, hot_slot, out_loc, fb)
    change = surface(lf, own, far, fcon, con, fb, elems, jump, flux)
    put(middle, [
        s + m + c for s, m, c in zip(blocks(state, size), blocks(vol1, size), change)
    ])
    start = split_rows(narrow(middle[...], hot_c[:FINE_DEV, :], wide), size)
    first = [A0 * x for x in start]

    def step2(k):
        old = start if k == 0 else blocks(q2, size, (k - 1) * count)
        put(q2, apply_step(ks, old, Mat(con_f, 8 * k, geo_f)), k * count)

    for k in range(STEPS):
        step2(k)
    window = [
        add(first[v], *[
            q2[k * count + v * size : k * count + (v + 1) * size, :] for k in range(STEPS)
        ])
        for v in range(VARS)
    ]
    w2[...] = widen(jnp.concatenate(window, axis=0), hot_c[...], wide) + wc[...]
    trace_faces(tr, w2, own, own_hl, fb, elems)
    serve(hot_in, own_hl, tx2)
    sent2 = send_all(down, tx2, rx2, send_sems, recv_sems, 3 * LANES)

    sums, speed = face_sums(lifted1, jump, flux, half_speed, fb, elems)
    sums = plus(sums, group_sums(blocks(seed1, size), blocks(vol1, size)))
    fine_sums = None
    for k in range(STEPS):
        fine_sums = plus(
            fine_sums, group_sums(blocks(hist, size, k * count), blocks(q2, size, k * count))
        )
    fine_sums = [jnp.sum(x, axis=0, keepdims=True) for x in fine_sums]
    fine_sums = widen(jnp.concatenate(fine_sums + fine_sums, axis=0), hot_c[...], 16)
    for copy in sent3:
        copy.wait()
    back = faces_back(own_cot1, rx3, hot_in, trt, fb, elems)
    put(seed1, [a + b for a, b in zip(back, blocks(cur, size))])
    chain = [sums]

    def back1(k):
        r = [a + C_OVER_A[k] * b for a, b in zip(blocks(seed1, size), blocks(coarse, size))]
        if k < STEPS:
            old = blocks(cur, size)
            r = [a + b for a, b in zip(r, apply_back(kt, old, Mat(con, 8 * (k + 1), geo_ref)))]
        put(cur, r)
        chain[0] = plus(
            chain[0], group_sums(blocks(cur, size), blocks(q1, size, (k - 1) * count))
        )

    weave([part(back1, k) for k in range(STEPS, 0, -1)], gather() + [part(volume, vol2, w2)])
    sums = plus(chain[0], group_sums(seed2, blocks(vol2, size)))
    for copy in sent2:
        copy.wait()

    far = far_side(rx2, slot_turn, tn, hot_slot, out_loc, fb)
    change = surface(lf, own, far, fcon, con, fb, elems, jump, flux)
    put(final, [
        s + m + c for s, m, c in zip(blocks(middle, size), blocks(vol2, size), change)
    ])
    more, more_speed = face_sums(lifted2, jump, flux, half_speed, fb, elems)
    sums = [jnp.sum(a + b, axis=0, keepdims=True) for a, b in zip(sums, more)]
    sums = [a + fine_sums[n : n + 1] for n, a in enumerate(sums)]
    g_speed = 0.5 * jnp.sum(speed + more_speed, axis=0, keepdims=True)
    lam, mu, rinv = [row(mat_ref, n) for n in range(3)]
    wave = jnp.sqrt((lam + 2.0 * mu) * rinv)
    g_lam = sums[0] / (3.0 * lam + 2.0 * mu)
    g_mu = (sums[1] - lam * g_lam + sums[2]) / mu
    g_speed = g_speed / wave
    grad[...] = jnp.concatenate(
        [
            g_lam + 0.5 * g_speed * rinv,
            g_mu + g_speed * rinv,
            sums[3] / rinv + 0.5 * g_speed * (lam + 2.0 * mu),
        ],
        axis=0,
    )


def finish_kernel(final, grad, final_out, grad_out, sems):
    copies = [
        pltpu.make_async_copy(final, final_out, sems.at[0]),
        pltpu.make_async_copy(grad, grad_out, sems.at[1]),
    ]
    for copy in copies:
        copy.start()
    for copy in copies:
        copy.wait()


def body(
    start_state, material, geometry, clusters, neighbours, orientation,
    stiffness, face_trace, face_lift, face_turns, cotangent,
):
    rows, elems = start_state.shape
    basis = rows // VARS
    devices = lax.axis_size("dom")
    fb = up_to(face_trace.shape[1], 8)
    pitch = up_to(basis, 16)
    frows = up_to(VARS * fb + 8, 16)
    full, faces, slots = (rows, elems), (VARS * fb, 4 * elems), (SLOTS, up_to(frows, 128))
    args = (
        start_state, cotangent, material, geometry, clusters.reshape(1, elems), neighbours,
        orientation, stiffness, face_trace.transpose(1, 0, 2), face_lift.transpose(2, 0, 1),
        face_turns,
    )
    scratch = [x.shape for x in args[:4]] + [x.shape for x in args[7:]]
    scratch += [full] * 10
    scratch += [(STEPS * rows, elems)] + [(STEPS * rows, FINE_DEV)] * 2
    scratch += [faces] * 8 + [slots] * 8
    scratch += [(8 * TERMS, elems), (32, elems), (8 * STEPS, FINE_DEV), (8, FINE_DEV)]
    scratch += [(8, 4 * elems), (16, SLOTS)]
    scratch += [(3, pitch, pitch), (4, fb, pitch), (4, fb, pitch), (3, fb, fb)]
    packed = [(3, 3 * basis, 3 * pitch)] * 2 + [(4 * fb, 3 * pitch)] * 2
    packed += [(2 * basis, 8 * fb)] * 2 + [(6 * fb, 6 * fb)] * 2
    packed += [(4 * elems, 4 * elems)] + [(SLOTS, 4 * elems)] * 2 + [(2 * FINE_DEV, elems)]
    packed += [(2 * frows, 4 * elems)] * 3
    args = [pltpu.with_memory_space_constraint(x, pltpu.HBM) for x in args]
    outs = pl.pallas_call(
        functools.partial(step_kernel, devices),
        out_shape=[
            jax.ShapeDtypeStruct((rows, elems), f32),
            jax.ShapeDtypeStruct((3, elems), f32),
        ],
        in_specs=[pl.BlockSpec(memory_space=pltpu.HBM)] * len(args),
        out_specs=[pl.BlockSpec(memory_space=pltpu.VMEM)] * 2,
        scratch_shapes=[pltpu.VMEM(s, f32) for s in scratch]
        + [pltpu.VMEM(s, bf16) for s in packed]
        + [pltpu.VMEM((1, elems), i32)]
        + [pltpu.VMEM((4, elems), i32)] * 3
        + [pltpu.SemaphoreType.DMA((len(args),))]
        + [pltpu.SemaphoreType.DMA((4 * LANES,))] * 2,
        compiler_params=pltpu.CompilerParams(
            vmem_limit_bytes=48 * 1024 * 1024, collective_id=0, has_side_effects=True
        ),
        name="ader_step",
    )(*args)
    return pl.pallas_call(
        finish_kernel,
        out_shape=[jax.ShapeDtypeStruct(x.shape, f32) for x in outs],
        in_specs=[pl.BlockSpec(memory_space=pltpu.VMEM)] * 2,
        out_specs=[pl.BlockSpec(memory_space=pl.ANY)] * 2,
        scratch_shapes=[pltpu.SemaphoreType.DMA((2,))],
        compiler_params=pltpu.CompilerParams(vmem_limit_bytes=2 * 1024 * 1024),
        name="finish",
    )(*outs)


def solution(mesh):
    return jax.shard_map(
        body,
        mesh=mesh,
        in_specs=(
            P(None, "dom"),
            P(None, "dom"),
            P(None, "dom"),
            P("dom"),
            P(None, "dom"),
            P(None, "dom"),
            P(),
            P(),
            P(),
            P(),
            P(None, "dom"),
        ),
        out_specs=(P(None, "dom"), P(None, "dom")),
        check_vma=False,
    )
```

```python
import functools

import jax
import jax.numpy as jnp
from jax import lax
from jax.experimental import pallas as pl
from jax.experimental.pallas import tpu as pltpu
from jax.sharding import PartitionSpec as P

VARS = 9
TERMS = 6
REACH = 4
CAP = 16
FINE_DEV = 128
LANES = 2 * REACH + 1
SLOTS = LANES * CAP
STEPS = TERMS - 1
f32, bf16, i32 = jnp.float32, jnp.bfloat16, jnp.int32

dt_step = 0.5
root_third = 0.5773502691896258
H = 0.5 * dt_step

A0 = H
STEP_SCALE = [H * H / 2.0] + [H / (k + 2.0) for k in range(1, STEPS)]
C_OVER_A = [2.0 ** (k + 1) - 1.0 for k in range(TERMS)]

NEED = [(0, 1), (1, 1), (2, 1), (0, 2), (1, 2), (2, 2), (0, 3), (0, 3), (0, 3)]
PAIRS = [((6, 7), 0, 3), ((8, 3), 0, 3), ((0, 1), 0, 2), ((4, 2), 1, 2), ((5,), 2, 2)]
READS = [
    {3: 7, 5: 8, 6: 0, 7: 3, 8: 5},
    {3: 6, 4: 8, 6: 3, 7: 1, 8: 4},
    {4: 7, 5: 6, 6: 5, 7: 4, 8: 2},
]


def up_to(n, m):
    return -(-n // m) * m


def halves(x):
    high = x.astype(bf16)
    return high, (x - high.astype(f32)).astype(bf16)


def padded(x, rows):
    if x.shape[0] == rows:
        return x
    return jnp.concatenate([x, jnp.zeros((rows - x.shape[0], x.shape[1]), f32)], axis=0)


def right3(x, rows):
    high, low = halves(padded(x, rows))
    return jnp.concatenate([high, high, low], axis=0)


def left3(a):
    high = a.astype(bf16).astype(f32)
    return jnp.concatenate([high, a - high, high], axis=1).astype(bf16)


def left2(a):
    high = a.astype(bf16).astype(f32)
    upper = jnp.concatenate([high, high], axis=1)
    lower = jnp.concatenate([a - high, jnp.zeros(a.shape, f32)], axis=1)
    return jnp.concatenate([upper, lower], axis=0).astype(bf16)


def apply2(mat, x):
    y = mm(mat[...], stack2(x, x.shape[0]))
    half = y.shape[0] // 2
    return y[:half] + y[half:]


def stack2(x, rows):
    return jnp.concatenate(halves(padded(x, rows)), axis=0)


def mm(a, b):
    return jnp.dot(a, b, preferred_element_type=f32)


def mm_t(a, b):
    return lax.dot_general(a, b, (((1,), (1,)), ((), ())), preferred_element_type=f32)


def add(*terms):
    total = None
    for t in terms:
        if t is not None:
            total = t if total is None else total + t
    return total


def blocks(ref, size, base=0):
    return [ref[base + v * size : base + (v + 1) * size, :] for v in range(VARS)]


def put(ref, values, base=0):
    size = values[0].shape[0]
    for v in range(VARS):
        ref[base + v * size : base + (v + 1) * size, :] = values[v]


def row(ref, n):
    return ref[n : n + 1, :]


class Mat:
    def __init__(self, con, base, geo):
        self.lam, self.mu2 = row(con, base), row(con, base + 1)
        self.mg = [row(con, base + 2 + a) for a in range(3)]
        self.rg = [row(con, base + 5 + a) for a in range(3)]
        self.g = [row(geo, a) for a in range(3)]


def forward_mix(p, m):
    t = [m.g[a] * p(6 + a, a) for a in range(3)]
    spread = m.lam * (t[0] + t[1] + t[2])
    return [
        spread + m.mu2 * t[0],
        spread + m.mu2 * t[1],
        spread + m.mu2 * t[2],
        m.mg[0] * p(7, 0) + m.mg[1] * p(6, 1),
        m.mg[1] * p(8, 1) + m.mg[2] * p(7, 2),
        m.mg[0] * p(8, 0) + m.mg[2] * p(6, 2),
        m.rg[0] * p(0, 0) + m.rg[1] * p(3, 1) + m.rg[2] * p(5, 2),
        m.rg[0] * p(3, 0) + m.rg[1] * p(1, 1) + m.rg[2] * p(4, 2),
        m.rg[0] * p(5, 0) + m.rg[1] * p(4, 1) + m.rg[2] * p(2, 2),
    ]


def normal_mix(r, m):
    u = m.lam * (r[0] + r[1] + r[2])
    return [u + m.mu2 * r[a] for a in range(3)] + list(r[3:])


def backward_mix(p, m):
    return [
        m.rg[0] * p(6, 0),
        m.rg[1] * p(7, 1),
        m.rg[2] * p(8, 2),
        m.rg[0] * p(7, 0) + m.rg[1] * p(6, 1),
        m.rg[1] * p(8, 1) + m.rg[2] * p(7, 2),
        m.rg[0] * p(8, 0) + m.rg[2] * p(6, 2),
        m.g[0] * p(0, 0) + m.mg[1] * p(3, 1) + m.mg[2] * p(5, 2),
        m.g[1] * p(1, 1) + m.mg[0] * p(3, 0) + m.mg[2] * p(4, 2),
        m.g[2] * p(2, 2) + m.mg[1] * p(4, 1) + m.mg[0] * p(5, 0),
    ]


def products(mat, values):
    size, width = values[0].shape
    pitch = mat.shape[2] // 3
    out = {}
    if width == FINE_DEV:
        groups = PAIRS
    else:
        groups = [((v,), s, c) for v, (s, c) in enumerate(NEED)]
    for names, start, count in groups:
        x = [values[v] for v in names]
        x = x[0] if len(x) == 1 else jnp.concatenate(x, axis=1)
        y = mm(mat[start, : count * size, :], right3(x, pitch))
        for n, v in enumerate(names):
            for i in range(count):
                out[v, (start + i) % 3] = y[
                    i * size : (i + 1) * size, n * width : (n + 1) * width
                ]
    return lambda v, axis: out[v, axis]


def apply_step(mat, values, m):
    return forward_mix(products(mat, values), m)


def apply_back(mat, values, m):
    return backward_mix(products(mat, normal_mix(values, m)), m)


def fold8(x):
    total = x[0:8]
    for n in range(8, x.shape[0], 8):
        total = total + x[n : n + 8]
    return total


def group_sums(r, x):
    mixed = (r[0] + r[1] + r[2]) * (x[0] + x[1] + x[2])
    groups = [add(*[r[v] * x[v] for v in range(g, g + 3)]) for g in (0, 3, 6)]
    return [fold8(g) for g in [mixed] + groups]


def plus(total, more):
    return more if total is None else [a + b for a, b in zip(total, more)]


def narrow(x, hot_c, rows):
    y = mm_t(stack2(x, rows), hot_c)
    return y[: x.shape[0]] + y[rows : rows + x.shape[0]]


def widen(x, hot_c2, rows):
    high, low = halves(padded(x, rows))
    return mm(jnp.concatenate([high, low], axis=1), hot_c2)[: x.shape[0]]


def trace_faces(tr, window, own, own_hl, fb, elems):
    size = window.shape[0] // VARS
    rows = own_hl.shape[0] // 2
    for v in range(VARS):
        t = mm(tr[...], right3(window[v * size : (v + 1) * size, :], tr.shape[1] // 3))
        for g in range(4):
            own[v * fb : (v + 1) * fb, g * elems : (g + 1) * elems] = t[g * fb : (g + 1) * fb]
    for g in range(4):
        cols = slice(g * elems, (g + 1) * elems)
        high, low = halves(padded(own[:, cols], rows))
        own_hl[:rows, cols] = high
        own_hl[rows:, cols] = low


def turn_blocks(mat, x, which):
    fb = x[0].shape[0]
    pick = [(w == 0, w == 1) for w in which]
    out = [None] * len(x)
    order = [f * VARS + v for f in range(len(which)) for v in range(VARS - 1)]
    order += [f * VARS + VARS - 1 for f in range(len(which))]
    for n in range(0, len(x), 2):
        names = order[n : n + 2]
        pair = [x[b] for b in names]
        y = mm(mat[...], right3(jnp.concatenate(pair, axis=0), 2 * fb))
        for i, b in enumerate(names):
            first, second = pick[b // VARS]
            part = [y[o * 2 * fb + i * fb : o * 2 * fb + (i + 1) * fb] for o in range(3)]
            out[b] = jnp.where(first, part[0], jnp.where(second, part[1], part[2]))
    return [out[n : n + VARS] for n in range(0, len(x), VARS)]


def split_rows(x, fb):
    return [x[v * fb : (v + 1) * fb] for v in range(VARS)]


def local_outer(own_hl, hot, turn, tn, out, fb, elems, faces):
    rows = own_hl.shape[0] // 2
    raw = []
    for f in faces:
        y = mm(own_hl[...], hot[:, f * elems : (f + 1) * elems])
        raw += split_rows(y[: VARS * fb] + y[rows : rows + VARS * fb], fb)
    turned = turn_blocks(tn, raw, [turn[f : f + 1, :] for f in faces])
    for f, x in zip(faces, turned):
        out[:, f * elems : (f + 1) * elems] = jnp.concatenate(x, axis=0)


def serve(hot_in, own_hl, tx):
    rows = own_hl.shape[0] // 2
    tx[:, :rows] = mm_t(hot_in[...], own_hl[:rows, :]) + mm_t(hot_in[...], own_hl[rows:, :])
    tx[:, rows:] = jnp.zeros((tx.shape[0], tx.shape[1] - rows), f32)


def flipped(rx):
    x = rx[...]
    return padded(x, up_to(x.shape[0], 128)).T[:, : x.shape[0]]


def face_rows(f, x, fc):
    if f == 3:
        return forward_mix(lambda v, axis: x[v], fc)
    axis = 2 - f
    kl, kp, _, km, kr = fc
    t = x[6 + axis]
    rows = [kl * t] * 3 + [None] * 6
    rows[axis] = kp * t
    for v, source in READS[axis].items():
        rows[v] = (km if v < 6 else kr) * x[source]
    return rows


def face_rows_back(f, r, fc):
    if f == 3:
        s = normal_mix(r, fc)
        return backward_mix(lambda v, axis: s[v], fc)
    axis = 2 - f
    kl, _, k2, km, kr = fc
    out = [None] * VARS
    out[6 + axis] = kl * (r[0] + r[1] + r[2]) + k2 * r[axis]
    for v, source in READS[axis].items():
        out[source] = (km if v < 6 else kr) * r[v]
    return out


def face_consts(f, fcon, con):
    if f == 3:
        m = Mat.__new__(Mat)
        m.lam, m.mu2 = row(fcon, 15), row(fcon, 16)
        m.mg = [row(fcon, 17 + a) for a in range(3)]
        m.rg = [row(fcon, 20 + a) for a in range(3)]
        m.g = [row(fcon, 23 + a) for a in range(3)]
        return m
    return [row(fcon, 5 * f + n) for n in range(5)]


def far_side(rx, slot_turn, tn, hot_slot, out_loc, fb):
    rows = up_to(VARS * fb, 16)
    turned = turn_blocks(tn, split_rows(flipped(rx), fb), [slot_turn[0:1, :]])[0]
    high_low = stack2(jnp.concatenate(turned, axis=0), rows)

    def far(f, elems):
        cols = slice(f * elems, (f + 1) * elems)
        y = mm(high_low, hot_slot[:, cols])
        return out_loc[:, cols] + (y[: VARS * fb] + y[rows : rows + VARS * fb])

    return far


def surface(lf, own, far, fcon, con, fb, elems, jump_ref, flux_ref):
    half_speed = row(fcon, 26)
    fluxes = [[] for _ in range(VARS)]
    for f in range(4):
        cols = slice(f * elems, (f + 1) * elems)
        a, b = split_rows(own[:, cols], fb), split_rows(far(f, elems), fb)
        rows = face_rows(f, [x + y for x, y in zip(a, b)], face_consts(f, fcon, con))
        for v in range(VARS):
            jump = a[v] - b[v]
            flux = add(half_speed * jump, rows[v])
            jump_ref[v * fb : (v + 1) * fb, cols] = jump
            flux_ref[v * fb : (v + 1) * fb, cols] = flux
            fluxes[v].append(flux)
    return [apply2(lf, jnp.concatenate(x, axis=0)) for x in fluxes]


def face_sums(lifted, jump_ref, flux_ref, half_speed, fb, elems):
    total, speed = None, None
    for f in range(4):
        cols = slice(f * elems, (f + 1) * elems)
        r, d, x = [split_rows(ref[:, cols], fb) for ref in (lifted, jump_ref, flux_ref)]
        of_jump, of_flux = group_sums(r, d), group_sums(r, x)
        total = plus(total, [a - half_speed * b for a, b in zip(of_flux, of_jump)])
        more = of_jump[1] + of_jump[2] + of_jump[3]
        speed = more if speed is None else speed + more
    return total, speed


def faces_cot(seed, lt, tnt, turn, extra, fcon, con, lifted, own_cot, x_hl, fb, elems):
    half_speed = row(fcon, 26)
    rows = x_hl.shape[0] // 2
    for v in range(VARS):
        y = mm(lt[...], right3(seed[v], lt.shape[1] // 3))
        for f in range(4):
            lifted[v * fb : (v + 1) * fb, f * elems : (f + 1) * elems] = y[f * fb : (f + 1) * fb]
    for faces in ((0, 1), (2, 3)):
        x = []
        for f in faces:
            cols = slice(f * elems, (f + 1) * elems)
            r = split_rows(lifted[:, cols], fb)
            back = face_rows_back(f, r, face_consts(f, fcon, con))
            for v in range(VARS):
                side = half_speed * r[v]
                own_cot[v * fb : (v + 1) * fb, cols] = add(side, back[v])
                x.append(-side if back[v] is None else back[v] - side)
        turned = turn_blocks(tnt, x, [turn[f : f + 1, :] for f in faces])
        for f, y in zip(faces, turned):
            cols = slice(f * elems, (f + 1) * elems)
            if extra is not None:
                y.append(extra[:, cols])
            high, low = halves(padded(jnp.concatenate(y, axis=0), rows))
            x_hl[:rows, cols] = high
            x_hl[rows:, cols] = low


def scatter_local(own_cot, x_hl, hot, fb, elems, g):
    rows = x_hl.shape[0] // 2
    cols = slice(g * elems, (g + 1) * elems)
    y = mm_t(x_hl[...], hot[cols, :])
    own_cot[:, cols] = own_cot[:, cols] + (y[: VARS * fb] + y[rows : rows + VARS * fb])


def faces_back(own_cot, rx, hot_in, trt, fb, elems):
    rows = up_to(VARS * fb, 16)
    arrived = stack2(flipped(rx)[: VARS * fb], rows)
    for g in range(4):
        cols = slice(g * elems, (g + 1) * elems)
        y = mm(arrived, hot_in[:, cols])
        own_cot[:, cols] = own_cot[:, cols] + (y[: VARS * fb] + y[rows : rows + VARS * fb])
    out = []
    for v in range(VARS):
        x = [own_cot[v * fb : (v + 1) * fb, g * elems : (g + 1) * elems] for g in range(4)]
        out.append(apply2(trt, jnp.concatenate(x, axis=0)))
    return out


def weave(steps, pieces):
    done = 0
    for n, step in enumerate(steps):
        step()
        until = (n + 1) * len(pieces) // len(steps)
        for piece in pieces[done:until]:
            piece()
        done = until


def peers_of(devices):
    me = lax.axis_index("dom")
    shifts = [n + 1 for n in range(REACH)] + [-(n + 1) for n in range(REACH)] + [devices // 2]
    return [
        [lax.rem(me + sign * s + 2 * devices, devices) for s in shifts] for sign in (1, -1)
    ]


def send_all(peers, src, dst, send_sems, recv_sems, base, near):
    last = [n for n in range(LANES - 1) if n not in near]
    copies = []
    for n in list(near) + [LANES - 1] + last:
        rows = pl.ds(n * CAP, CAP)
        copy = pltpu.make_async_remote_copy(
            src_ref=src.at[rows],
            dst_ref=dst.at[rows],
            send_sem=send_sems.at[base + n],
            recv_sem=recv_sems.at[base + n],
            device_id=(peers[n],),
            device_id_type=pl.DeviceIdType.MESH,
        )
        copy.start()
        copies.append(copy)
    return copies


def one_hot(mask):
    return jnp.where(mask, 1.0, 0.0).astype(bf16)


def face_places(
    devices, neighbours, orientation, fine, hot, hot_slot, hot_c, turn, slot_turn, extra
):
    elems = neighbours.shape[1]
    me = lax.axis_index("dom")
    at = lax.broadcasted_iota(i32, (16, elems), 0)
    square = (elems, elems)
    at_n, at_e = lax.broadcasted_iota(i32, square, 0), lax.broadcasted_iota(i32, square, 1)
    at_s = lax.broadcasted_iota(i32, (SLOTS, elems), 0)
    at_8 = lax.broadcasted_iota(i32, (8, elems), 0)
    earlier = one_hot(at_n <= at_e)
    lanes, marks, keys = [], [], []
    for f in range(4):
        cols = slice(f * elems, (f + 1) * elems)
        name, code = neighbours[f : f + 1, :], orientation[f : f + 1, :]
        far_face = sum(jnp.where(code >= 3 * g, 1, 0) for g in (1, 2, 3))
        turn[f : f + 1, :] = code - 3 * far_face
        present = name >= 0
        safe = jnp.maximum(name, 0)
        owner = jnp.floor((safe.astype(f32) + 0.5) * (1.0 / elems)).astype(i32)
        index = safe - owner * elems
        away = owner - me
        away = jnp.where(away < 0, away + devices, away)
        keys.append((cols, present & (away == 0), far_face, index))
        lane = jnp.where(
            away <= REACH,
            away - 1,
            jnp.where(away >= devices - REACH, REACH + devices - away - 1, 2 * REACH),
        )
        lane = jnp.where(present & (away != 0), lane, LANES)
        lanes.append(lane)
        marks.append(jnp.where(at == lane, 1.0, 0.0))
        index_f, face_f = index.astype(f32), far_face.astype(f32)
        extra[:, cols] = jnp.where(
            at_8 == 0, index_f, jnp.where(at_8 == 1, face_f, jnp.where(at_8 == 2, 1.0, 0.0))
        )
    is_fine = fine[...] == 1
    marks.append(jnp.where((at == 0) & is_fine, 1.0, 0.0))
    run = mm(jnp.concatenate(marks, axis=0).astype(bf16), earlier)
    carry = jnp.zeros((16, 1), f32)
    for f in range(4):
        cols = slice(f * elems, (f + 1) * elems)
        mine = run[16 * f : 16 * f + 16]
        rank = jnp.sum((mine + carry - 1.0) * marks[f], axis=0, keepdims=True).astype(i32)
        carry = carry + mine[:, elems - 1 :]
        slot = jnp.where(lanes[f] < LANES, lanes[f] * CAP + rank, -1)
        hot_slot[:, cols] = one_hot(at_s == slot)
    rank = jnp.where(is_fine, run[64:65].astype(i32) - 1, -1)
    picked = one_hot(lax.broadcasted_iota(i32, (FINE_DEV, elems), 0) == rank)
    hot_c[:FINE_DEV, :] = picked
    hot_c[FINE_DEV:, :] = picked
    turns = jnp.concatenate([turn[f : f + 1, :].astype(f32) for f in range(4)], axis=1)
    turns = jnp.broadcast_to(turns, (16, 4 * elems)).astype(bf16)
    slot_turn[...] = mm_t(turns, hot_slot[...])

    def fill(cols, local, far_face, index):
        names = at_n.astype(f32).astype(bf16)
        for g in range(4):
            key = jnp.where(local & (far_face == g), index, -1).astype(f32).astype(bf16)
            hot[g * elems : (g + 1) * elems, cols] = jnp.where(
                names == key, jnp.ones(square, bf16), jnp.zeros(square, bf16)
            )

    return [functools.partial(fill, *key) for key in keys]


def constants(mat_ref, geo_ref, con, fcon):
    lam, mu, rinv = [row(mat_ref, n) for n in range(3)]
    geo = [row(geo_ref, n) for n in range(3)]
    rows = [lam, 2.0 * mu] + [mu * g for g in geo] + [rinv * g for g in geo]
    base = jnp.concatenate(rows, axis=0)
    for n, scale in enumerate([-1.0] + STEP_SCALE):
        con[8 * n : 8 * n + 8, :] = scale * base
    rows = []
    for f in range(3):
        h = 0.5 * geo[2 - f]
        rows += [lam * h, (lam + 2.0 * mu) * h, 2.0 * mu * h, mu * h, rinv * h]
    h = [(-0.5 * root_third) * g for g in geo]
    rows += [lam, 2.0 * mu] + [mu * x for x in h] + [rinv * x for x in h] + h
    rows += [0.5 * jnp.sqrt((lam + 2.0 * mu) * rinv)]
    for n, x in enumerate(rows):
        fcon[n : n + 1, :] = x


def pitched(pad, matrices):
    pad[...] = jnp.zeros(pad.shape, f32)
    for n, x in enumerate(matrices):
        pad[n, : x.shape[0], : x.shape[1]] = x
    return [pad[n] for n in range(len(matrices))]


def turn_matrix(pad, matrices):
    zero = jnp.zeros(pad.shape[1:], f32)
    out = []
    for x in pitched(pad, matrices):
        out += [jnp.concatenate([x, zero], axis=1), jnp.concatenate([zero, x], axis=1)]
    return left3(jnp.concatenate(out, axis=0))


def step_kernel(
    devices,
    state_in, cot_in, mat_in, geo_in, fine_in, neighbours_in, orientation_in, stiffness_in,
    trace_in, lift_in, turns_in,
    final, grad,
    state, cot, mat_ref, geo_ref, stiffness, face_trace, face_lift, face_turns,
    w1, wc, w2, coarse, seed1, middle, vol1, vol2, cur, direct2,
    q1, q2, hist,
    own, lifted1, lifted2, out_loc, own_cot1, own_cot2, jump, flux,
    tx0, tx1, tx2, tx3, rx0, rx1, rx2, rx3,
    con, fcon, con_f, geo_f, extra, slot_turn,
    k_pad, t_pad, l_pad, n_pad,
    ks, kt, tr, lt, trt, lf, tn, tnt, hot, hot_slot, hot_in, hot_c, own_hl, x_hl1, x_hl2,
    fine, neighbours, orientation, turn, load_sems, send_sems, recv_sems,
):
    loads = [
        pltpu.make_async_copy(src, dst, load_sems.at[n])
        for n, (src, dst) in enumerate([
            (neighbours_in, neighbours), (orientation_in, orientation), (mat_in, mat_ref),
            (geo_in, geo_ref), (fine_in, fine), (stiffness_in, stiffness),
            (trace_in, face_trace), (lift_in, face_lift), (turns_in, face_turns),
            (cot_in, cot), (state_in, state),
        ])
    ]
    for load in loads:
        load.start()
    up, down = peers_of(devices)
    barrier = pltpu.get_barrier_semaphore()
    for peer in up:
        pl.semaphore_signal(
            barrier, inc=1, device_id=(peer,), device_id_type=pl.DeviceIdType.MESH
        )
    elems = state.shape[1]
    count = state.shape[0]
    size = count // VARS
    fb = t_pad.shape[1]
    wide = up_to(count, 16)
    part = functools.partial

    for load in loads[:9]:
        load.wait()
    constants(mat_ref, geo_ref, con, fcon)
    trace = jnp.concatenate(pitched(t_pad, [face_trace[:, g, :] for g in range(4)]), axis=0)
    tr[...] = left3(trace)
    trt[...] = left2(trace.T[:size])
    lift = jnp.concatenate(pitched(l_pad, [-face_lift[:, f, :] for f in range(4)]), axis=0)
    lt[...] = left3(lift)
    lf[...] = left2(lift.T[:size])
    turns = [face_turns[o] for o in range(3)]
    tn[...] = turn_matrix(n_pad, turns)
    tnt[...] = turn_matrix(n_pad, [x.T for x in turns])
    hot_fills = face_places(
        devices, neighbours, orientation, fine, hot, hot_slot, hot_c, turn, slot_turn, extra
    )
    base, half_speed = Mat(con, 0, geo_ref), row(fcon, 26)

    loads[9].wait()
    seed2 = blocks(cot, size)
    faces_cot(seed2, lt, tnt, turn, extra, fcon, con, lifted2, own_cot2, x_hl2, fb, elems)
    serve(hot_slot, x_hl2, tx0)
    for piece in hot_fills:
        piece()

    def scatter(own_cot, x_hl):
        return [part(scatter_local, own_cot, x_hl, hot, fb, elems, g) for g in range(4)]

    pl.semaphore_wait(barrier, LANES)
    sent0 = send_all(up, tx0, rx0, send_sems, recv_sems, 0, range(REACH))

    stiff = pitched(k_pad, [stiffness[d] for d in range(3)])
    for mat, axes in ((ks, stiff), (kt, [x.T for x in stiff])):
        for n in range(3):
            order = [axes[(n + i) % 3][:size] for i in range(3)]
            mat[n] = left3(jnp.concatenate(order, axis=0))
    is_fine = fine[...] == 1
    loads[10].wait()

    def step1(k):
        old = blocks(state, size) if k == 0 else blocks(q1, size, (k - 1) * count)
        put(q1, apply_step(ks, old, Mat(con, 8 * (k + 1), geo_ref)), k * count)

    def gather():
        return [
            part(local_outer, own_hl, hot, turn, tn, out_loc, fb, elems, faces)
            for faces in ((0, 1), (2, 3))
        ]

    def volume(out, window):
        put(out, apply_step(kt, blocks(window, size), base))

    for piece in scatter(own_cot2, x_hl2):
        piece()
    for k in range(STEPS):
        step1(k)
    for v in range(VARS):
        rows = slice(v * size, (v + 1) * size)
        terms = [A0 * state[rows, :]]
        terms += [q1[k * count + v * size : k * count + (v + 1) * size, :] for k in range(STEPS)]
        w1[rows, :] = add(*terms)
        later = add(*[c * t if c != 1.0 else t for c, t in zip(C_OVER_A, terms)])
        wc[rows, :] = jnp.where(is_fine, 0.0, later)
    trace_faces(tr, w1, own, own_hl, fb, elems)
    for piece in gather():
        piece()
    for copy in sent0:
        copy.wait()

    key = rx0[:, VARS * fb : VARS * fb + 3]
    key = jnp.where(key[:, 2:3] > 0.5, key[:, 1:2] * float(elems) + key[:, 0:1], -1.0)
    at = lax.broadcasted_iota(i32, (SLOTS, 4 * elems), 1)
    hot_in[...] = one_hot(at == key.astype(i32))
    serve(hot_in, own_hl, tx1)
    sent1 = send_all(down, tx1, rx1, send_sems, recv_sems, LANES, range(REACH, 2 * REACH))

    put(direct2, apply_back(ks, seed2, base))
    back = faces_back(own_cot2, rx0, hot_in, trt, fb, elems)
    back = [a + b for a, b in zip(back, blocks(direct2, size))]
    put(coarse, [jnp.where(is_fine, 0.0, x) for x in back])
    seeds = split_rows(narrow(jnp.concatenate(back, axis=0), hot_c[:FINE_DEV, :], wide), size)
    put(hist, seeds, (STEPS - 1) * count)
    narrow_con = mm_t(
        jnp.concatenate(
            halves(con[0:16, :]) + halves(padded(geo_ref[...], 16)), axis=0
        ),
        hot_c[:FINE_DEV, :],
    )
    geo_f[...] = narrow_con[32:40] + narrow_con[48:56]
    for n, scale in enumerate(STEP_SCALE):
        con_f[8 * n : 8 * n + 8, :] = -scale * (narrow_con[0:8] + narrow_con[16:24])

    def back2(k):
        r = apply_back(kt, blocks(hist, size, k * count), Mat(con_f, 8 * k, geo_f))
        scale = A0 if k == 0 else 1.0
        direct = blocks(hist, size, (STEPS - 1) * count)
        r = [a + (b if k else scale * b) for a, b in zip(r, direct)]
        if k:
            put(hist, r, (k - 1) * count)
        else:
            seed1[...] = widen(jnp.concatenate(r, axis=0), hot_c[...], wide) + cot[...]

    for k in range(STEPS - 1, -1, -1):
        back2(k)
    faces_cot(
        blocks(seed1, size), lt, tnt, turn, None, fcon, con, lifted1, own_cot1, x_hl1, fb, elems
    )
    serve(hot_slot, x_hl1, tx3)
    sent3 = send_all(up, tx3, rx3, send_sems, recv_sems, 2 * LANES, range(REACH))
    for piece in scatter(own_cot1, x_hl1):
        piece()
    put(cur, apply_back(ks, blocks(seed1, size), base))
    volume(vol1, w1)
    for copy in sent1:
        copy.wait()

    far = far_side(rx1, slot_turn, tn, hot_slot, out_loc, fb)
    change = surface(lf, own, far, fcon, con, fb, elems, jump, flux)
    put(middle, [
        s + m + c for s, m, c in zip(blocks(state, size), blocks(vol1, size), change)
    ])
    start = split_rows(narrow(middle[...], hot_c[:FINE_DEV, :], wide), size)
    first = [A0 * x for x in start]

    def step2(k):
        old = start if k == 0 else blocks(q2, size, (k - 1) * count)
        put(q2, apply_step(ks, old, Mat(con_f, 8 * k, geo_f)), k * count)

    for k in range(STEPS):
        step2(k)
    window = [
        add(first[v], *[
            q2[k * count + v * size : k * count + (v + 1) * size, :] for k in range(STEPS)
        ])
        for v in range(VARS)
    ]
    w2[...] = widen(jnp.concatenate(window, axis=0), hot_c[...], wide) + wc[...]
    trace_faces(tr, w2, own, own_hl, fb, elems)
    serve(hot_in, own_hl, tx2)
    sent2 = send_all(down, tx2, rx2, send_sems, recv_sems, 3 * LANES, range(REACH, 2 * REACH))

    sums, speed = face_sums(lifted1, jump, flux, half_speed, fb, elems)
    sums = plus(sums, group_sums(blocks(seed1, size), blocks(vol1, size)))
    fine_sums = None
    for k in range(STEPS):
        fine_sums = plus(
            fine_sums, group_sums(blocks(hist, size, k * count), blocks(q2, size, k * count))
        )
    fine_sums = [jnp.sum(x, axis=0, keepdims=True) for x in fine_sums]
    fine_sums = widen(jnp.concatenate(fine_sums + fine_sums, axis=0), hot_c[...], 16)
    for copy in sent3:
        copy.wait()
    back = faces_back(own_cot1, rx3, hot_in, trt, fb, elems)
    put(seed1, [a + b for a, b in zip(back, blocks(cur, size))])
    chain = [sums]

    def back1(k):
        r = [a + C_OVER_A[k] * b for a, b in zip(blocks(seed1, size), blocks(coarse, size))]
        if k < STEPS:
            old = blocks(cur, size)
            r = [a + b for a, b in zip(r, apply_back(kt, old, Mat(con, 8 * (k + 1), geo_ref)))]
        put(cur, r)
        chain[0] = plus(
            chain[0], group_sums(blocks(cur, size), blocks(q1, size, (k - 1) * count))
        )

    weave([part(back1, k) for k in range(STEPS, 0, -1)], gather() + [part(volume, vol2, w2)])
    sums = plus(chain[0], group_sums(seed2, blocks(vol2, size)))
    for copy in sent2:
        copy.wait()

    far = far_side(rx2, slot_turn, tn, hot_slot, out_loc, fb)
    change = surface(lf, own, far, fcon, con, fb, elems, jump, flux)
    put(final, [
        s + m + c for s, m, c in zip(blocks(middle, size), blocks(vol2, size), change)
    ])
    more, more_speed = face_sums(lifted2, jump, flux, half_speed, fb, elems)
    sums = [jnp.sum(a + b, axis=0, keepdims=True) for a, b in zip(sums, more)]
    sums = [a + fine_sums[n : n + 1] for n, a in enumerate(sums)]
    g_speed = 0.5 * jnp.sum(speed + more_speed, axis=0, keepdims=True)
    lam, mu, rinv = [row(mat_ref, n) for n in range(3)]
    wave = jnp.sqrt((lam + 2.0 * mu) * rinv)
    g_lam = sums[0] / (3.0 * lam + 2.0 * mu)
    g_mu = (sums[1] - lam * g_lam + sums[2]) / mu
    g_speed = g_speed / wave
    grad[...] = jnp.concatenate(
        [
            g_lam + 0.5 * g_speed * rinv,
            g_mu + g_speed * rinv,
            sums[3] / rinv + 0.5 * g_speed * (lam + 2.0 * mu),
        ],
        axis=0,
    )


def finish_kernel(final, grad, final_out, grad_out, sems):
    copies = [
        pltpu.make_async_copy(final, final_out, sems.at[0]),
        pltpu.make_async_copy(grad, grad_out, sems.at[1]),
    ]
    for copy in copies:
        copy.start()
    for copy in copies:
        copy.wait()


def body(
    start_state, material, geometry, clusters, neighbours, orientation,
    stiffness, face_trace, face_lift, face_turns, cotangent,
):
    rows, elems = start_state.shape
    basis = rows // VARS
    devices = lax.axis_size("dom")
    fb = up_to(face_trace.shape[1], 8)
    pitch = up_to(basis, 16)
    frows = up_to(VARS * fb + 8, 16)
    full, faces, slots = (rows, elems), (VARS * fb, 4 * elems), (SLOTS, up_to(frows, 128))
    args = (
        start_state, cotangent, material, geometry, clusters.reshape(1, elems), neighbours,
        orientation, stiffness, face_trace.transpose(1, 0, 2), face_lift.transpose(2, 0, 1),
        face_turns,
    )
    scratch = [x.shape for x in args[:4]] + [x.shape for x in args[7:]]
    scratch += [full] * 10
    scratch += [(STEPS * rows, elems)] + [(STEPS * rows, FINE_DEV)] * 2
    scratch += [faces] * 8 + [slots] * 8
    scratch += [(8 * TERMS, elems), (32, elems), (8 * STEPS, FINE_DEV), (8, FINE_DEV)]
    scratch += [(8, 4 * elems), (16, SLOTS)]
    scratch += [(3, pitch, pitch), (4, fb, pitch), (4, fb, pitch), (3, fb, fb)]
    packed = [(3, 3 * basis, 3 * pitch)] * 2 + [(4 * fb, 3 * pitch)] * 2
    packed += [(2 * basis, 8 * fb)] * 2 + [(6 * fb, 6 * fb)] * 2
    packed += [(4 * elems, 4 * elems)] + [(SLOTS, 4 * elems)] * 2 + [(2 * FINE_DEV, elems)]
    packed += [(2 * frows, 4 * elems)] * 3
    args = [pltpu.with_memory_space_constraint(x, pltpu.HBM) for x in args]
    outs = pl.pallas_call(
        functools.partial(step_kernel, devices),
        out_shape=[
            jax.ShapeDtypeStruct((rows, elems), f32),
            jax.ShapeDtypeStruct((3, elems), f32),
        ],
        in_specs=[pl.BlockSpec(memory_space=pltpu.HBM)] * len(args),
        out_specs=[pl.BlockSpec(memory_space=pltpu.VMEM)] * 2,
        scratch_shapes=[pltpu.VMEM(s, f32) for s in scratch]
        + [pltpu.VMEM(s, bf16) for s in packed]
        + [pltpu.VMEM((1, elems), i32)]
        + [pltpu.VMEM((4, elems), i32)] * 3
        + [pltpu.SemaphoreType.DMA((len(args),))]
        + [pltpu.SemaphoreType.DMA((4 * LANES,))] * 2,
        compiler_params=pltpu.CompilerParams(
            vmem_limit_bytes=48 * 1024 * 1024, collective_id=0, has_side_effects=True
        ),
        name="ader_step",
    )(*args)
    return pl.pallas_call(
        finish_kernel,
        out_shape=[jax.ShapeDtypeStruct(x.shape, f32) for x in outs],
        in_specs=[pl.BlockSpec(memory_space=pltpu.VMEM)] * 2,
        out_specs=[pl.BlockSpec(memory_space=pl.ANY)] * 2,
        scratch_shapes=[pltpu.SemaphoreType.DMA((2,))],
        compiler_params=pltpu.CompilerParams(vmem_limit_bytes=2 * 1024 * 1024),
        name="finish",
    )(*outs)


def solution(mesh):
    return jax.shard_map(
        body,
        mesh=mesh,
        in_specs=(
            P(None, "dom"),
            P(None, "dom"),
            P(None, "dom"),
            P("dom"),
            P(None, "dom"),
            P(None, "dom"),
            P(),
            P(),
            P(),
            P(),
            P(None, "dom"),
        ),
        out_specs=(P(None, "dom"), P(None, "dom")),
        check_vma=False,
    )
```

```python
import functools

import jax
import jax.numpy as jnp
from jax import lax
from jax.experimental import pallas as pl
from jax.experimental.pallas import tpu as pltpu
from jax.sharding import PartitionSpec as P

VARS = 9
TERMS = 6
REACH = 4
CAP = 16
FINE_DEV = 128
LANES = 2 * REACH + 1
SLOTS = LANES * CAP
STEPS = TERMS - 1
f32, bf16, i32 = jnp.float32, jnp.bfloat16, jnp.int32

dt_step = 0.5
root_third = 0.5773502691896258
H = 0.5 * dt_step

A0 = H
STEP_SCALE = [H * H / 2.0] + [H / (k + 2.0) for k in range(1, STEPS)]
C_OVER_A = [2.0 ** (k + 1) - 1.0 for k in range(TERMS)]

NEED = [(0, 1), (1, 1), (2, 1), (0, 2), (1, 2), (2, 2), (0, 3), (0, 3), (0, 3)]
PAIRS = [((6, 7), 0, 3), ((8, 3), 0, 3), ((0, 1), 0, 2), ((4, 2), 1, 2), ((5,), 2, 2)]
READS = [
    {3: 7, 5: 8, 6: 0, 7: 3, 8: 5},
    {3: 6, 4: 8, 6: 3, 7: 1, 8: 4},
    {4: 7, 5: 6, 6: 5, 7: 4, 8: 2},
]


def up_to(n, m):
    return -(-n // m) * m


def halves(x):
    high = x.astype(bf16)
    return high, (x - high.astype(f32)).astype(bf16)


def padded(x, rows):
    if x.shape[0] == rows:
        return x
    return jnp.concatenate([x, jnp.zeros((rows - x.shape[0], x.shape[1]), f32)], axis=0)


def right3(x, rows):
    high, low = halves(padded(x, rows))
    return jnp.concatenate([high, high, low], axis=0)


def left3(a):
    high = a.astype(bf16).astype(f32)
    return jnp.concatenate([high, a - high, high], axis=1).astype(bf16)


def left2(a):
    high = a.astype(bf16).astype(f32)
    upper = jnp.concatenate([high, high], axis=1)
    lower = jnp.concatenate([a - high, jnp.zeros(a.shape, f32)], axis=1)
    return jnp.concatenate([upper, lower], axis=0).astype(bf16)


def apply2(mat, x):
    y = mm(mat[...], stack2(x, x.shape[0]))
    half = y.shape[0] // 2
    return y[:half] + y[half:]


def stack2(x, rows):
    return jnp.concatenate(halves(padded(x, rows)), axis=0)


def mm(a, b):
    return jnp.dot(a, b, preferred_element_type=f32)


def mm_t(a, b):
    return lax.dot_general(a, b, (((1,), (1,)), ((), ())), preferred_element_type=f32)


def add(*terms):
    total = None
    for t in terms:
        if t is not None:
            total = t if total is None else total + t
    return total


def blocks(ref, size, base=0):
    return [ref[base + v * size : base + (v + 1) * size, :] for v in range(VARS)]


def put(ref, values, base=0):
    size = values[0].shape[0]
    for v in range(VARS):
        ref[base + v * size : base + (v + 1) * size, :] = values[v]


def row(ref, n):
    return ref[n : n + 1, :]


class Mat:
    def __init__(self, con, base, geo):
        self.lam, self.mu2 = row(con, base), row(con, base + 1)
        self.mg = [row(con, base + 2 + a) for a in range(3)]
        self.rg = [row(con, base + 5 + a) for a in range(3)]
        self.g = [row(geo, a) for a in range(3)]


def forward_mix(p, m):
    t = [m.g[a] * p(6 + a, a) for a in range(3)]
    spread = m.lam * (t[0] + t[1] + t[2])
    return [
        spread + m.mu2 * t[0],
        spread + m.mu2 * t[1],
        spread + m.mu2 * t[2],
        m.mg[0] * p(7, 0) + m.mg[1] * p(6, 1),
        m.mg[1] * p(8, 1) + m.mg[2] * p(7, 2),
        m.mg[0] * p(8, 0) + m.mg[2] * p(6, 2),
        m.rg[0] * p(0, 0) + m.rg[1] * p(3, 1) + m.rg[2] * p(5, 2),
        m.rg[0] * p(3, 0) + m.rg[1] * p(1, 1) + m.rg[2] * p(4, 2),
        m.rg[0] * p(5, 0) + m.rg[1] * p(4, 1) + m.rg[2] * p(2, 2),
    ]


def normal_mix(r, m):
    u = m.lam * (r[0] + r[1] + r[2])
    return [u + m.mu2 * r[a] for a in range(3)] + list(r[3:])


def backward_mix(p, m):
    return [
        m.rg[0] * p(6, 0),
        m.rg[1] * p(7, 1),
        m.rg[2] * p(8, 2),
        m.rg[0] * p(7, 0) + m.rg[1] * p(6, 1),
        m.rg[1] * p(8, 1) + m.rg[2] * p(7, 2),
        m.rg[0] * p(8, 0) + m.rg[2] * p(6, 2),
        m.g[0] * p(0, 0) + m.mg[1] * p(3, 1) + m.mg[2] * p(5, 2),
        m.g[1] * p(1, 1) + m.mg[0] * p(3, 0) + m.mg[2] * p(4, 2),
        m.g[2] * p(2, 2) + m.mg[1] * p(4, 1) + m.mg[0] * p(5, 0),
    ]


def products(mat, values):
    size, width = values[0].shape
    pitch = mat.shape[2] // 3
    out = {}
    if width == FINE_DEV:
        groups = PAIRS
    else:
        groups = [((v,), s, c) for v, (s, c) in enumerate(NEED)]
    for names, start, count in groups:
        x = [values[v] for v in names]
        x = x[0] if len(x) == 1 else jnp.concatenate(x, axis=1)
        y = mm(mat[start, : count * size, :], right3(x, pitch))
        for n, v in enumerate(names):
            for i in range(count):
                out[v, (start + i) % 3] = y[
                    i * size : (i + 1) * size, n * width : (n + 1) * width
                ]
    return lambda v, axis: out[v, axis]


def apply_step(mat, values, m):
    return forward_mix(products(mat, values), m)


def apply_back(mat, values, m):
    return backward_mix(products(mat, normal_mix(values, m)), m)


def fold8(x):
    total = x[0:8]
    for n in range(8, x.shape[0], 8):
        total = total + x[n : n + 8]
    return total


def group_sums(r, x):
    mixed = (r[0] + r[1] + r[2]) * (x[0] + x[1] + x[2])
    groups = [add(*[r[v] * x[v] for v in range(g, g + 3)]) for g in (0, 3, 6)]
    return [fold8(g) for g in [mixed] + groups]


def plus(total, more):
    return more if total is None else [a + b for a, b in zip(total, more)]


def narrow(x, hot_c, rows):
    y = mm_t(stack2(x, rows), hot_c)
    return y[: x.shape[0]] + y[rows : rows + x.shape[0]]


def widen(x, hot_c2, rows):
    high, low = halves(padded(x, rows))
    return mm(jnp.concatenate([high, low], axis=1), hot_c2)[: x.shape[0]]


def trace_faces(tr, window, own, own_hl, fb, elems):
    size = window.shape[0] // VARS
    rows = own_hl.shape[0] // 2
    for v in range(VARS):
        t = mm(tr[...], right3(window[v * size : (v + 1) * size, :], tr.shape[1] // 3))
        for g in range(4):
            own[v * fb : (v + 1) * fb, g * elems : (g + 1) * elems] = t[g * fb : (g + 1) * fb]
    for g in range(4):
        cols = slice(g * elems, (g + 1) * elems)
        high, low = halves(padded(own[:, cols], rows))
        own_hl[:rows, cols] = high
        own_hl[rows:, cols] = low


def turn_blocks(mat, x, which):
    fb = x[0].shape[0]
    pick = [(w == 0, w == 1) for w in which]
    out = [None] * len(x)
    order = [f * VARS + v for f in range(len(which)) for v in range(VARS - 1)]
    order += [f * VARS + VARS - 1 for f in range(len(which))]
    for n in range(0, len(x), 2):
        names = order[n : n + 2]
        pair = [x[b] for b in names]
        y = mm(mat[...], right3(jnp.concatenate(pair, axis=0), 2 * fb))
        for i, b in enumerate(names):
            first, second = pick[b // VARS]
            part = [y[o * 2 * fb + i * fb : o * 2 * fb + (i + 1) * fb] for o in range(3)]
            out[b] = jnp.where(first, part[0], jnp.where(second, part[1], part[2]))
    return [out[n : n + VARS] for n in range(0, len(x), VARS)]


def split_rows(x, fb):
    return [x[v * fb : (v + 1) * fb] for v in range(VARS)]


def local_outer(own_hl, hot, turn, tn, out, fb, elems, faces):
    rows = own_hl.shape[0] // 2
    raw = []
    for f in faces:
        y = mm(own_hl[...], hot[:, f * elems : (f + 1) * elems])
        raw += split_rows(y[: VARS * fb] + y[rows : rows + VARS * fb], fb)
    turned = turn_blocks(tn, raw, [turn[f : f + 1, :] for f in faces])
    for f, x in zip(faces, turned):
        out[:, f * elems : (f + 1) * elems] = jnp.concatenate(x, axis=0)


def serve(hot_in, own_hl, tx):
    rows = own_hl.shape[0] // 2
    tx[:, :rows] = mm_t(hot_in[...], own_hl[:rows, :]) + mm_t(hot_in[...], own_hl[rows:, :])
    tx[:, rows:] = jnp.zeros((tx.shape[0], tx.shape[1] - rows), f32)


def flipped(rx):
    x = rx[...]
    return padded(x, up_to(x.shape[0], 128)).T[:, : x.shape[0]]


def face_rows(f, x, fc):
    if f == 3:
        return forward_mix(lambda v, axis: x[v], fc)
    axis = 2 - f
    kl, kp, _, km, kr = fc
    t = x[6 + axis]
    rows = [kl * t] * 3 + [None] * 6
    rows[axis] = kp * t
    for v, source in READS[axis].items():
        rows[v] = (km if v < 6 else kr) * x[source]
    return rows


def face_rows_back(f, r, fc):
    if f == 3:
        s = normal_mix(r, fc)
        return backward_mix(lambda v, axis: s[v], fc)
    axis = 2 - f
    kl, _, k2, km, kr = fc
    out = [None] * VARS
    out[6 + axis] = kl * (r[0] + r[1] + r[2]) + k2 * r[axis]
    for v, source in READS[axis].items():
        out[source] = (km if v < 6 else kr) * r[v]
    return out


def face_consts(f, fcon, con):
    if f == 3:
        m = Mat.__new__(Mat)
        m.lam, m.mu2 = row(fcon, 15), row(fcon, 16)
        m.mg = [row(fcon, 17 + a) for a in range(3)]
        m.rg = [row(fcon, 20 + a) for a in range(3)]
        m.g = [row(fcon, 23 + a) for a in range(3)]
        return m
    return [row(fcon, 5 * f + n) for n in range(5)]


def far_side(rx, slot_turn, tn, hot_slot, out_loc, fb):
    rows = up_to(VARS * fb, 16)
    turned = turn_blocks(tn, split_rows(flipped(rx), fb), [slot_turn[0:1, :]])[0]
    high_low = stack2(jnp.concatenate(turned, axis=0), rows)

    def far(f, elems):
        cols = slice(f * elems, (f + 1) * elems)
        y = mm(high_low, hot_slot[:, cols])
        return out_loc[:, cols] + (y[: VARS * fb] + y[rows : rows + VARS * fb])

    return far


def surface(lf, own, far, fcon, con, fb, elems, jump_ref, flux_ref):
    half_speed = row(fcon, 26)
    fluxes = [[] for _ in range(VARS)]
    for f in range(4):
        cols = slice(f * elems, (f + 1) * elems)
        a, b = split_rows(own[:, cols], fb), split_rows(far(f, elems), fb)
        rows = face_rows(f, [x + y for x, y in zip(a, b)], face_consts(f, fcon, con))
        for v in range(VARS):
            jump = a[v] - b[v]
            flux = add(half_speed * jump, rows[v])
            jump_ref[v * fb : (v + 1) * fb, cols] = jump
            flux_ref[v * fb : (v + 1) * fb, cols] = flux
            fluxes[v].append(flux)
    return [apply2(lf, jnp.concatenate(x, axis=0)) for x in fluxes]


def face_sums(lifted, jump_ref, flux_ref, half_speed, fb, elems):
    total, speed = None, None
    for f in range(4):
        cols = slice(f * elems, (f + 1) * elems)
        r, d, x = [split_rows(ref[:, cols], fb) for ref in (lifted, jump_ref, flux_ref)]
        of_jump, of_flux = group_sums(r, d), group_sums(r, x)
        total = plus(total, [a - half_speed * b for a, b in zip(of_flux, of_jump)])
        more = of_jump[1] + of_jump[2] + of_jump[3]
        speed = more if speed is None else speed + more
    return total, speed


def faces_cot(seed, lt, tnt, turn, extra, fcon, con, lifted, own_cot, x_hl, fb, elems):
    half_speed = row(fcon, 26)
    rows = x_hl.shape[0] // 2
    for v in range(VARS):
        y = mm(lt[...], right3(seed[v], lt.shape[1] // 3))
        for f in range(4):
            lifted[v * fb : (v + 1) * fb, f * elems : (f + 1) * elems] = y[f * fb : (f + 1) * fb]
    for faces in ((0, 1), (2, 3)):
        x = []
        for f in faces:
            cols = slice(f * elems, (f + 1) * elems)
            r = split_rows(lifted[:, cols], fb)
            back = face_rows_back(f, r, face_consts(f, fcon, con))
            for v in range(VARS):
                side = half_speed * r[v]
                own_cot[v * fb : (v + 1) * fb, cols] = add(side, back[v])
                x.append(-side if back[v] is None else back[v] - side)
        turned = turn_blocks(tnt, x, [turn[f : f + 1, :] for f in faces])
        for f, y in zip(faces, turned):
            cols = slice(f * elems, (f + 1) * elems)
            if extra is not None:
                y.append(extra[:, cols])
            high, low = halves(padded(jnp.concatenate(y, axis=0), rows))
            x_hl[:rows, cols] = high
            x_hl[rows:, cols] = low


def scatter_local(own_cot, x_hl, hot, fb, elems, g):
    rows = x_hl.shape[0] // 2
    cols = slice(g * elems, (g + 1) * elems)
    y = mm_t(x_hl[...], hot[cols, :])
    own_cot[:, cols] = own_cot[:, cols] + (y[: VARS * fb] + y[rows : rows + VARS * fb])


def faces_back(own_cot, rx, hot_in, trt, fb, elems):
    rows = up_to(VARS * fb, 16)
    arrived = stack2(flipped(rx)[: VARS * fb], rows)
    for g in range(4):
        cols = slice(g * elems, (g + 1) * elems)
        y = mm(arrived, hot_in[:, cols])
        own_cot[:, cols] = own_cot[:, cols] + (y[: VARS * fb] + y[rows : rows + VARS * fb])
    out = []
    for v in range(VARS):
        x = [own_cot[v * fb : (v + 1) * fb, g * elems : (g + 1) * elems] for g in range(4)]
        out.append(apply2(trt, jnp.concatenate(x, axis=0)))
    return out


def weave(steps, pieces):
    done = 0
    for n, step in enumerate(steps):
        step()
        until = (n + 1) * len(pieces) // len(steps)
        for piece in pieces[done:until]:
            piece()
        done = until


def peers_of(devices):
    me = lax.axis_index("dom")
    shifts = [n + 1 for n in range(REACH)] + [-(n + 1) for n in range(REACH)] + [devices // 2]
    return [
        [lax.rem(me + sign * s + 2 * devices, devices) for s in shifts] for sign in (1, -1)
    ]


def send_all(peers, src, dst, send_sems, recv_sems, base, near):
    last = [n for n in range(LANES - 1) if n not in near]
    copies = []
    for n in list(reversed(near)) + [LANES - 1] + last:
        rows = pl.ds(n * CAP, CAP)
        copy = pltpu.make_async_remote_copy(
            src_ref=src.at[rows],
            dst_ref=dst.at[rows],
            send_sem=send_sems.at[base + n],
            recv_sem=recv_sems.at[base + n],
            device_id=(peers[n],),
            device_id_type=pl.DeviceIdType.MESH,
        )
        copy.start()
        copies.append(copy)
    return copies


def one_hot(mask):
    return jnp.where(mask, 1.0, 0.0).astype(bf16)


def face_places(
    devices, neighbours, orientation, fine, hot, hot_slot, hot_c, turn, slot_turn, extra
):
    elems = neighbours.shape[1]
    me = lax.axis_index("dom")
    at = lax.broadcasted_iota(i32, (16, elems), 0)
    square = (elems, elems)
    at_n, at_e = lax.broadcasted_iota(i32, square, 0), lax.broadcasted_iota(i32, square, 1)
    at_s = lax.broadcasted_iota(i32, (SLOTS, elems), 0)
    at_8 = lax.broadcasted_iota(i32, (8, elems), 0)
    earlier = one_hot(at_n <= at_e)
    lanes, marks, keys = [], [], []
    for f in range(4):
        cols = slice(f * elems, (f + 1) * elems)
        name, code = neighbours[f : f + 1, :], orientation[f : f + 1, :]
        far_face = sum(jnp.where(code >= 3 * g, 1, 0) for g in (1, 2, 3))
        turn[f : f + 1, :] = code - 3 * far_face
        present = name >= 0
        safe = jnp.maximum(name, 0)
        owner = jnp.floor((safe.astype(f32) + 0.5) * (1.0 / elems)).astype(i32)
        index = safe - owner * elems
        away = owner - me
        away = jnp.where(away < 0, away + devices, away)
        keys.append((cols, present & (away == 0), far_face, index))
        lane = jnp.where(
            away <= REACH,
            away - 1,
            jnp.where(away >= devices - REACH, REACH + devices - away - 1, 2 * REACH),
        )
        lane = jnp.where(present & (away != 0), lane, LANES)
        lanes.append(lane)
        marks.append(jnp.where(at == lane, 1.0, 0.0))
        index_f, face_f = index.astype(f32), far_face.astype(f32)
        extra[:, cols] = jnp.where(
            at_8 == 0, index_f, jnp.where(at_8 == 1, face_f, jnp.where(at_8 == 2, 1.0, 0.0))
        )
    is_fine = fine[...] == 1
    marks.append(jnp.where((at == 0) & is_fine, 1.0, 0.0))
    run = mm(jnp.concatenate(marks, axis=0).astype(bf16), earlier)
    carry = jnp.zeros((16, 1), f32)
    for f in range(4):
        cols = slice(f * elems, (f + 1) * elems)
        mine = run[16 * f : 16 * f + 16]
        rank = jnp.sum((mine + carry - 1.0) * marks[f], axis=0, keepdims=True).astype(i32)
        carry = carry + mine[:, elems - 1 :]
        slot = jnp.where(lanes[f] < LANES, lanes[f] * CAP + rank, -1)
        hot_slot[:, cols] = one_hot(at_s == slot)
    rank = jnp.where(is_fine, run[64:65].astype(i32) - 1, -1)
    picked = one_hot(lax.broadcasted_iota(i32, (FINE_DEV, elems), 0) == rank)
    hot_c[:FINE_DEV, :] = picked
    hot_c[FINE_DEV:, :] = picked
    turns = jnp.concatenate([turn[f : f + 1, :].astype(f32) for f in range(4)], axis=1)
    turns = jnp.broadcast_to(turns, (16, 4 * elems)).astype(bf16)
    slot_turn[...] = mm_t(turns, hot_slot[...])

    def fill(cols, local, far_face, index):
        names = at_n.astype(f32).astype(bf16)
        for g in range(4):
            key = jnp.where(local & (far_face == g), index, -1).astype(f32).astype(bf16)
            hot[g * elems : (g + 1) * elems, cols] = jnp.where(
                names == key, jnp.ones(square, bf16), jnp.zeros(square, bf16)
            )

    return [functools.partial(fill, *key) for key in keys]


def constants(mat_ref, geo_ref, con, fcon):
    lam, mu, rinv = [row(mat_ref, n) for n in range(3)]
    geo = [row(geo_ref, n) for n in range(3)]
    rows = [lam, 2.0 * mu] + [mu * g for g in geo] + [rinv * g for g in geo]
    base = jnp.concatenate(rows, axis=0)
    for n, scale in enumerate([-1.0] + STEP_SCALE):
        con[8 * n : 8 * n + 8, :] = scale * base
    rows = []
    for f in range(3):
        h = 0.5 * geo[2 - f]
        rows += [lam * h, (lam + 2.0 * mu) * h, 2.0 * mu * h, mu * h, rinv * h]
    h = [(-0.5 * root_third) * g for g in geo]
    rows += [lam, 2.0 * mu] + [mu * x for x in h] + [rinv * x for x in h] + h
    rows += [0.5 * jnp.sqrt((lam + 2.0 * mu) * rinv)]
    for n, x in enumerate(rows):
        fcon[n : n + 1, :] = x


def pitched(pad, matrices):
    pad[...] = jnp.zeros(pad.shape, f32)
    for n, x in enumerate(matrices):
        pad[n, : x.shape[0], : x.shape[1]] = x
    return [pad[n] for n in range(len(matrices))]


def turn_matrix(pad, matrices):
    zero = jnp.zeros(pad.shape[1:], f32)
    out = []
    for x in pitched(pad, matrices):
        out += [jnp.concatenate([x, zero], axis=1), jnp.concatenate([zero, x], axis=1)]
    return left3(jnp.concatenate(out, axis=0))


def step_kernel(
    devices,
    state_in, cot_in, mat_in, geo_in, fine_in, neighbours_in, orientation_in, stiffness_in,
    trace_in, lift_in, turns_in,
    final, grad,
    state, cot, mat_ref, geo_ref, stiffness, face_trace, face_lift, face_turns,
    w1, wc, w2, coarse, seed1, middle, vol1, vol2, cur, direct2,
    q1, q2, hist,
    own, lifted1, lifted2, out_loc, own_cot1, own_cot2, jump, flux,
    tx0, tx1, tx2, tx3, rx0, rx1, rx2, rx3,
    con, fcon, con_f, geo_f, extra, slot_turn,
    k_pad, t_pad, l_pad, n_pad,
    ks, kt, tr, lt, trt, lf, tn, tnt, hot, hot_slot, hot_in, hot_c, own_hl, x_hl1, x_hl2,
    fine, neighbours, orientation, turn, load_sems, send_sems, recv_sems,
):
    loads = [
        pltpu.make_async_copy(src, dst, load_sems.at[n])
        for n, (src, dst) in enumerate([
            (neighbours_in, neighbours), (orientation_in, orientation), (mat_in, mat_ref),
            (geo_in, geo_ref), (fine_in, fine), (stiffness_in, stiffness),
            (trace_in, face_trace), (lift_in, face_lift), (turns_in, face_turns),
            (cot_in, cot), (state_in, state),
        ])
    ]
    for load in loads:
        load.start()
    up, down = peers_of(devices)
    barrier = pltpu.get_barrier_semaphore()
    for peer in up:
        pl.semaphore_signal(
            barrier, inc=1, device_id=(peer,), device_id_type=pl.DeviceIdType.MESH
        )
    elems = state.shape[1]
    count = state.shape[0]
    size = count // VARS
    fb = t_pad.shape[1]
    wide = up_to(count, 16)
    part = functools.partial

    for load in loads[:9]:
        load.wait()
    constants(mat_ref, geo_ref, con, fcon)
    trace = jnp.concatenate(pitched(t_pad, [face_trace[:, g, :] for g in range(4)]), axis=0)
    tr[...] = left3(trace)
    trt[...] = left2(trace.T[:size])
    lift = jnp.concatenate(pitched(l_pad, [-face_lift[:, f, :] for f in range(4)]), axis=0)
    lt[...] = left3(lift)
    lf[...] = left2(lift.T[:size])
    turns = [face_turns[o] for o in range(3)]
    tn[...] = turn_matrix(n_pad, turns)
    tnt[...] = turn_matrix(n_pad, [x.T for x in turns])
    hot_fills = face_places(
        devices, neighbours, orientation, fine, hot, hot_slot, hot_c, turn, slot_turn, extra
    )
    base, half_speed = Mat(con, 0, geo_ref), row(fcon, 26)

    loads[9].wait()
    seed2 = blocks(cot, size)
    faces_cot(seed2, lt, tnt, turn, extra, fcon, con, lifted2, own_cot2, x_hl2, fb, elems)
    serve(hot_slot, x_hl2, tx0)
    for piece in hot_fills:
        piece()

    def scatter(own_cot, x_hl):
        return [part(scatter_local, own_cot, x_hl, hot, fb, elems, g) for g in range(4)]

    pl.semaphore_wait(barrier, LANES)
    sent0 = send_all(up, tx0, rx0, send_sems, recv_sems, 0, range(REACH))

    stiff = pitched(k_pad, [stiffness[d] for d in range(3)])
    for mat, axes in ((ks, stiff), (kt, [x.T for x in stiff])):
        for n in range(3):
            order = [axes[(n + i) % 3][:size] for i in range(3)]
            mat[n] = left3(jnp.concatenate(order, axis=0))
    is_fine = fine[...] == 1
    loads[10].wait()

    def step1(k):
        old = blocks(state, size) if k == 0 else blocks(q1, size, (k - 1) * count)
        put(q1, apply_step(ks, old, Mat(con, 8 * (k + 1), geo_ref)), k * count)

    def gather():
        return [
            part(local_outer, own_hl, hot, turn, tn, out_loc, fb, elems, faces)
            for faces in ((0, 1), (2, 3))
        ]

    def volume(out, window):
        put(out, apply_step(kt, blocks(window, size), base))

    for piece in scatter(own_cot2, x_hl2):
        piece()
    for k in range(STEPS):
        step1(k)
    for v in range(VARS):
        rows = slice(v * size, (v + 1) * size)
        terms = [A0 * state[rows, :]]
        terms += [q1[k * count + v * size : k * count + (v + 1) * size, :] for k in range(STEPS)]
        w1[rows, :] = add(*terms)
        later = add(*[c * t if c != 1.0 else t for c, t in zip(C_OVER_A, terms)])
        wc[rows, :] = jnp.where(is_fine, 0.0, later)
    trace_faces(tr, w1, own, own_hl, fb, elems)
    for piece in gather():
        piece()
    for copy in sent0:
        copy.wait()

    key = rx0[:, VARS * fb : VARS * fb + 3]
    key = jnp.where(key[:, 2:3] > 0.5, key[:, 1:2] * float(elems) + key[:, 0:1], -1.0)
    at = lax.broadcasted_iota(i32, (SLOTS, 4 * elems), 1)
    hot_in[...] = one_hot(at == key.astype(i32))
    serve(hot_in, own_hl, tx1)
    sent1 = send_all(down, tx1, rx1, send_sems, recv_sems, LANES, range(REACH, 2 * REACH))

    put(direct2, apply_back(ks, seed2, base))
    back = faces_back(own_cot2, rx0, hot_in, trt, fb, elems)
    back = [a + b for a, b in zip(back, blocks(direct2, size))]
    put(coarse, [jnp.where(is_fine, 0.0, x) for x in back])
    seeds = split_rows(narrow(jnp.concatenate(back, axis=0), hot_c[:FINE_DEV, :], wide), size)
    put(hist, seeds, (STEPS - 1) * count)
    narrow_con = mm_t(
        jnp.concatenate(
            halves(con[0:16, :]) + halves(padded(geo_ref[...], 16)), axis=0
        ),
        hot_c[:FINE_DEV, :],
    )
    geo_f[...] = narrow_con[32:40] + narrow_con[48:56]
    for n, scale in enumerate(STEP_SCALE):
        con_f[8 * n : 8 * n + 8, :] = -scale * (narrow_con[0:8] + narrow_con[16:24])

    def back2(k):
        r = apply_back(kt, blocks(hist, size, k * count), Mat(con_f, 8 * k, geo_f))
        scale = A0 if k == 0 else 1.0
        direct = blocks(hist, size, (STEPS - 1) * count)
        r = [a + (b if k else scale * b) for a, b in zip(r, direct)]
        if k:
            put(hist, r, (k - 1) * count)
        else:
            seed1[...] = widen(jnp.concatenate(r, axis=0), hot_c[...], wide) + cot[...]

    for k in range(STEPS - 1, -1, -1):
        back2(k)
    faces_cot(
        blocks(seed1, size), lt, tnt, turn, None, fcon, con, lifted1, own_cot1, x_hl1, fb, elems
    )
    serve(hot_slot, x_hl1, tx3)
    sent3 = send_all(up, tx3, rx3, send_sems, recv_sems, 2 * LANES, range(REACH))
    for piece in scatter(own_cot1, x_hl1):
        piece()
    put(cur, apply_back(ks, blocks(seed1, size), base))
    volume(vol1, w1)
    for copy in sent1:
        copy.wait()

    far = far_side(rx1, slot_turn, tn, hot_slot, out_loc, fb)
    change = surface(lf, own, far, fcon, con, fb, elems, jump, flux)
    put(middle, [
        s + m + c for s, m, c in zip(blocks(state, size), blocks(vol1, size), change)
    ])
    start = split_rows(narrow(middle[...], hot_c[:FINE_DEV, :], wide), size)
    first = [A0 * x for x in start]

    def step2(k):
        old = start if k == 0 else blocks(q2, size, (k - 1) * count)
        put(q2, apply_step(ks, old, Mat(con_f, 8 * k, geo_f)), k * count)

    for k in range(STEPS):
        step2(k)
    window = [
        add(first[v], *[
            q2[k * count + v * size : k * count + (v + 1) * size, :] for k in range(STEPS)
        ])
        for v in range(VARS)
    ]
    w2[...] = widen(jnp.concatenate(window, axis=0), hot_c[...], wide) + wc[...]
    trace_faces(tr, w2, own, own_hl, fb, elems)
    serve(hot_in, own_hl, tx2)
    sent2 = send_all(down, tx2, rx2, send_sems, recv_sems, 3 * LANES, range(REACH, 2 * REACH))

    sums, speed = face_sums(lifted1, jump, flux, half_speed, fb, elems)
    sums = plus(sums, group_sums(blocks(seed1, size), blocks(vol1, size)))
    fine_sums = None
    for k in range(STEPS):
        fine_sums = plus(
            fine_sums, group_sums(blocks(hist, size, k * count), blocks(q2, size, k * count))
        )
    fine_sums = [jnp.sum(x, axis=0, keepdims=True) for x in fine_sums]
    fine_sums = widen(jnp.concatenate(fine_sums + fine_sums, axis=0), hot_c[...], 16)
    for copy in sent3:
        copy.wait()
    back = faces_back(own_cot1, rx3, hot_in, trt, fb, elems)
    put(seed1, [a + b for a, b in zip(back, blocks(cur, size))])
    chain = [sums]

    def back1(k):
        r = [a + C_OVER_A[k] * b for a, b in zip(blocks(seed1, size), blocks(coarse, size))]
        if k < STEPS:
            old = blocks(cur, size)
            r = [a + b for a, b in zip(r, apply_back(kt, old, Mat(con, 8 * (k + 1), geo_ref)))]
        put(cur, r)
        chain[0] = plus(
            chain[0], group_sums(blocks(cur, size), blocks(q1, size, (k - 1) * count))
        )

    weave([part(back1, k) for k in range(STEPS, 0, -1)], gather() + [part(volume, vol2, w2)])
    sums = plus(chain[0], group_sums(seed2, blocks(vol2, size)))
    for copy in sent2:
        copy.wait()

    far = far_side(rx2, slot_turn, tn, hot_slot, out_loc, fb)
    change = surface(lf, own, far, fcon, con, fb, elems, jump, flux)
    put(final, [
        s + m + c for s, m, c in zip(blocks(middle, size), blocks(vol2, size), change)
    ])
    more, more_speed = face_sums(lifted2, jump, flux, half_speed, fb, elems)
    sums = [jnp.sum(a + b, axis=0, keepdims=True) for a, b in zip(sums, more)]
    sums = [a + fine_sums[n : n + 1] for n, a in enumerate(sums)]
    g_speed = 0.5 * jnp.sum(speed + more_speed, axis=0, keepdims=True)
    lam, mu, rinv = [row(mat_ref, n) for n in range(3)]
    wave = jnp.sqrt((lam + 2.0 * mu) * rinv)
    g_lam = sums[0] / (3.0 * lam + 2.0 * mu)
    g_mu = (sums[1] - lam * g_lam + sums[2]) / mu
    g_speed = g_speed / wave
    grad[...] = jnp.concatenate(
        [
            g_lam + 0.5 * g_speed * rinv,
            g_mu + g_speed * rinv,
            sums[3] / rinv + 0.5 * g_speed * (lam + 2.0 * mu),
        ],
        axis=0,
    )


def finish_kernel(final, grad, final_out, grad_out, sems):
    copies = [
        pltpu.make_async_copy(final, final_out, sems.at[0]),
        pltpu.make_async_copy(grad, grad_out, sems.at[1]),
    ]
    for copy in copies:
        copy.start()
    for copy in copies:
        copy.wait()


def body(
    start_state, material, geometry, clusters, neighbours, orientation,
    stiffness, face_trace, face_lift, face_turns, cotangent,
):
    rows, elems = start_state.shape
    basis = rows // VARS
    devices = lax.axis_size("dom")
    fb = up_to(face_trace.shape[1], 8)
    pitch = up_to(basis, 16)
    frows = up_to(VARS * fb + 8, 16)
    full, faces, slots = (rows, elems), (VARS * fb, 4 * elems), (SLOTS, up_to(frows, 128))
    args = (
        start_state, cotangent, material, geometry, clusters.reshape(1, elems), neighbours,
        orientation, stiffness, face_trace.transpose(1, 0, 2), face_lift.transpose(2, 0, 1),
        face_turns,
    )
    scratch = [x.shape for x in args[:4]] + [x.shape for x in args[7:]]
    scratch += [full] * 10
    scratch += [(STEPS * rows, elems)] + [(STEPS * rows, FINE_DEV)] * 2
    scratch += [faces] * 8 + [slots] * 8
    scratch += [(8 * TERMS, elems), (32, elems), (8 * STEPS, FINE_DEV), (8, FINE_DEV)]
    scratch += [(8, 4 * elems), (16, SLOTS)]
    scratch += [(3, pitch, pitch), (4, fb, pitch), (4, fb, pitch), (3, fb, fb)]
    packed = [(3, 3 * basis, 3 * pitch)] * 2 + [(4 * fb, 3 * pitch)] * 2
    packed += [(2 * basis, 8 * fb)] * 2 + [(6 * fb, 6 * fb)] * 2
    packed += [(4 * elems, 4 * elems)] + [(SLOTS, 4 * elems)] * 2 + [(2 * FINE_DEV, elems)]
    packed += [(2 * frows, 4 * elems)] * 3
    args = [pltpu.with_memory_space_constraint(x, pltpu.HBM) for x in args]
    outs = pl.pallas_call(
        functools.partial(step_kernel, devices),
        out_shape=[
            jax.ShapeDtypeStruct((rows, elems), f32),
            jax.ShapeDtypeStruct((3, elems), f32),
        ],
        in_specs=[pl.BlockSpec(memory_space=pltpu.HBM)] * len(args),
        out_specs=[pl.BlockSpec(memory_space=pltpu.VMEM)] * 2,
        scratch_shapes=[pltpu.VMEM(s, f32) for s in scratch]
        + [pltpu.VMEM(s, bf16) for s in packed]
        + [pltpu.VMEM((1, elems), i32)]
        + [pltpu.VMEM((4, elems), i32)] * 3
        + [pltpu.SemaphoreType.DMA((len(args),))]
        + [pltpu.SemaphoreType.DMA((4 * LANES,))] * 2,
        compiler_params=pltpu.CompilerParams(
            vmem_limit_bytes=48 * 1024 * 1024, collective_id=0, has_side_effects=True
        ),
        name="ader_step",
    )(*args)
    return pl.pallas_call(
        finish_kernel,
        out_shape=[jax.ShapeDtypeStruct(x.shape, f32) for x in outs],
        in_specs=[pl.BlockSpec(memory_space=pltpu.VMEM)] * 2,
        out_specs=[pl.BlockSpec(memory_space=pl.ANY)] * 2,
        scratch_shapes=[pltpu.SemaphoreType.DMA((2,))],
        compiler_params=pltpu.CompilerParams(vmem_limit_bytes=2 * 1024 * 1024),
        name="finish",
    )(*outs)


def solution(mesh):
    return jax.shard_map(
        body,
        mesh=mesh,
        in_specs=(
            P(None, "dom"),
            P(None, "dom"),
            P(None, "dom"),
            P("dom"),
            P(None, "dom"),
            P(None, "dom"),
            P(),
            P(),
            P(),
            P(),
            P(None, "dom"),
        ),
        out_specs=(P(None, "dom"), P(None, "dom")),
        check_vma=False,
    )
```
